32 devices in a mesh: dp: 4 (over y, x), seq: 4 (over z), tensor: 2 (over core).
Axes of the slice: x: 2, y: 2, z: 4, core: 2. Of those that a mesh axis runs over, the one named last changes fastest.
Arguments:
- hidden: bfloat16 [8, 1024, 768], P('dp', 'seq'), may hold values from -6 to 6
- cotangent: bfloat16 [8, 1024, 768], P('dp', 'seq'), may hold values from -6 to 6
- gating: float32 [768, 1536], P(('dp', 'seq'), 'tensor'), may hold values from -0.21875 to 0.21875
- values: float32 [768, 1536], P(('dp', 'seq'), 'tensor'), may hold values from -0.21875 to 0.21875
- selector: float32 [768, 256], P(('dp', 'seq'), 'tensor'), may hold values from -0.21875 to 0.21875
- timestep: float32 [768, 24], P(('dp', 'seq'), 'tensor'), may hold values from -0.4375 to 0.4375
- output: float32 [1536, 768], P('tensor', ('dp', 'seq')), may hold values from -0.15625 to 0.15625
- prenorm: float32 [768], P(('dp', 'seq')), may hold values from 0.5 to 1.5
- postnorm: float32 [1536], P('tensor'), may hold values from 0.5 to 1.5
- filters: float32 [5, 1536], P(None, 'tensor'), may hold values from -3 to 3
- kernels: float32 [5, 256], P(None, 'tensor'), may hold values from -3 to 3
- scalars: float32 [3, 24], P(None, 'tensor'), may hold values from -14 to 2
- gating_adam: float32 [2, 768, 1536], P(None, ('dp', 'seq'), 'tensor'), may hold values from -2 to 2, as said below
- values_adam: float32 [2, 768, 1536], P(None, ('dp', 'seq'), 'tensor'), may hold values from -2 to 2, as said below
- selector_adam: float32 [2, 768, 256], P(None, ('dp', 'seq'), 'tensor'), may hold values from -2 to 2, as said below
- timestep_adam: float32 [2, 768, 24], P(None, ('dp', 'seq'), 'tensor'), may hold values from -2 to 2, as said below
- output_adam: float32 [2, 1536, 768], P(None, 'tensor', ('dp', 'seq')), may hold values from -2 to 2, as said below
- prenorm_adam: float32 [2, 768], P(None, ('dp', 'seq')), may hold values from -97 to 97, as said below
- postnorm_adam: float32 [2, 1536], P(None, 'tensor'), may hold values from -2 to 2, as said below
- filters_adam: float32 [2, 5, 1536], P(None, None, 'tensor'), may hold values from -2 to 2, as said below
- kernels_adam: float32 [2, 5, 256], P(None, None, 'tensor'), may hold values from -2 to 2, as said below
- scalars_adam: float32 [2, 3, 24], P(None, None, 'tensor'), may hold values from -2 to 2, as said below
Outputs:
- result: float32 [8, 1024, 768], P('dp', 'seq')
- hidden_grad: float32 [8, 1024, 768], P('dp', 'seq')
- gating_grad: float32 [768, 1536], P(('dp', 'seq'), 'tensor')
- values_grad: float32 [768, 1536], P(('dp', 'seq'), 'tensor')
- selector_grad: float32 [768, 256], P(('dp', 'seq'), 'tensor')
- timestep_grad: float32 [768, 24], P(('dp', 'seq'), 'tensor')
- output_grad: float32 [1536, 768], P('tensor', ('dp', 'seq'))
- prenorm_grad: float32 [768], P(('dp', 'seq'))
- postnorm_grad: float32 [1536], P('tensor')
- filters_grad: float32 [5, 1536], P(None, 'tensor')
- kernels_grad: float32 [5, 256], P(None, 'tensor')
- scalars_grad: float32 [3, 24], P(None, 'tensor')
- gating_next: float32 [768, 1536], P(('dp', 'seq'), 'tensor')
- values_next: float32 [768, 1536], P(('dp', 'seq'), 'tensor')
- selector_next: float32 [768, 256], P(('dp', 'seq'), 'tensor')
- timestep_next: float32 [768, 24], P(('dp', 'seq'), 'tensor')
- output_next: float32 [1536, 768], P('tensor', ('dp', 'seq'))
- prenorm_next: float32 [768], P(('dp', 'seq'))
- postnorm_next: float32 [1536], P('tensor')
- filters_next: float32 [5, 1536], P(None, 'tensor')
- kernels_next: float32 [5, 256], P(None, 'tensor')
- scalars_next: float32 [3, 24], P(None, 'tensor')
- gating_state: float32 [2, 768, 1536], P(None, ('dp', 'seq'), 'tensor')
- values_state: float32 [2, 768, 1536], P(None, ('dp', 'seq'), 'tensor')
- selector_state: float32 [2, 768, 256], P(None, ('dp', 'seq'), 'tensor')
- timestep_state: float32 [2, 768, 24], P(None, ('dp', 'seq'), 'tensor')
- output_state: float32 [2, 1536, 768], P(None, 'tensor', ('dp', 'seq'))
- prenorm_state: float32 [2, 768], P(None, ('dp', 'seq'))
- postnorm_state: float32 [2, 1536], P(None, 'tensor')
- filters_state: float32 [2, 5, 1536], P(None, None, 'tensor')
- kernels_state: float32 [2, 5, 256], P(None, None, 'tensor')
- scalars_state: float32 [2, 3, 24], P(None, None, 'tensor')
The draws below stay inside these ranges and needn't reach their ends.
Inputs may be any that keep to these rules, and one draw needn't show every extreme that they name: `gating_adam`: index 1 is positive. `values_adam`: index 1 is positive. `selector_adam`: index 1 is positive. `timestep_adam`: index 1 is positive. `output_adam`: index 1 is positive. `prenorm_adam`: index 1 is positive. `postnorm_adam`: index 1 is positive. `filters_adam`: index 1 is positive. `kernels_adam`: index 1 is positive. `scalars_adam`: index 1 is positive.
All inputs are finite; a program needn't handle non-finite values.
Results may differ from the reference program's by a relative error of at most 0.015.
The reference program's roundings to bfloat16 on the way count: a program that leaves them out, or rounds other values in their place, can miss the bound.
Values may be sent and summed in bfloat16 or wider, within the bound.
A program may use at most 128 MiB of HBM per device.

```python
import math
import jax
import jax.numpy as jnp
from jax import lax

D = 768
INNER = 1536
STATE = 128
HEADDIM = 64
KCONV = 4
GROUP = 256
STEP = 2
HEADS = 24
SEQS = 8
LENGTH = 1024
N_SEQ = 4


def moment_pair(key, shape):
    first_key, second_key = jax.random.split(key)
    first = 0.4 * jnp.clip(jax.random.normal(first_key, shape, jnp.float32), -4.0, 4.0)
    second = 0.016 * jnp.exp(jax.random.uniform(second_key, shape, jnp.float32, -1.2, 1.2))
    return jnp.stack([first, second])


def draw_scalars(key, part):
    keys = jax.random.split(jax.random.fold_in(key, 7), 5)
    log_rate = jax.random.uniform(keys[0], (HEADS,), jnp.float32, 0.0, math.log(4.0))
    rate = jnp.exp(log_rate)
    slow_share = 0.5
    skip_top = 1.5
    slow = jax.random.uniform(keys[1], (HEADS,), jnp.float32) < slow_share
    reach = jnp.exp(jax.random.uniform(keys[2], (HEADS,), jnp.float32, math.log(0.3), math.log(0.6 * N_SEQ))) / (rate * LENGTH)
    quick = jnp.exp(jax.random.uniform(keys[3], (HEADS,), jnp.float32, math.log(0.02), math.log(0.07))) / rate
    delta = jnp.where(slow, reach, quick) * math.exp(-2.0)
    bias = jnp.log(jnp.expm1(delta))
    skip = jax.random.uniform(keys[4], (HEADS,), jnp.float32, 0.5, skip_top)
    return jnp.stack([bias, log_rate, skip])


def draw_gating_adam(key, part):
    return moment_pair(jax.random.fold_in(key, 101), (D, INNER))


def draw_values_adam(key, part):
    return moment_pair(jax.random.fold_in(key, 102), (D, INNER))


def draw_selector_adam(key, part):
    return moment_pair(jax.random.fold_in(key, 103), (D, 2 * STATE))


def draw_timestep_adam(key, part):
    return moment_pair(jax.random.fold_in(key, 104), (D, HEADS))


def draw_output_adam(key, part):
    return moment_pair(jax.random.fold_in(key, 105), (INNER, D))


def draw_prenorm_adam(key, part):
    magnitude = math.sqrt(SEQS * LENGTH)
    first_key, second_key = jax.random.split(jax.random.fold_in(key, 106))
    first = 0.15 * magnitude * jnp.clip(jax.random.normal(first_key, (D,), jnp.float32), -4.0, 4.0)
    second = 0.0017 * magnitude * magnitude * jnp.exp(jax.random.uniform(second_key, (D,), jnp.float32, -1.2, 1.2))
    return jnp.stack([first, second])


def draw_postnorm_adam(key, part):
    return moment_pair(jax.random.fold_in(key, 107), (INNER,))


def draw_filters_adam(key, part):
    return moment_pair(jax.random.fold_in(key, 108), (KCONV + 1, INNER))


def draw_kernels_adam(key, part):
    return moment_pair(jax.random.fold_in(key, 109), (KCONV + 1, 2 * STATE))


def draw_scalars_adam(key, part):
    return moment_pair(jax.random.fold_in(key, 110), (3, HEADS))


def level_of(rng, extent, cuts, smallest, high):
    loudness = 1.0
    for position, parts in cuts:
        heights = jax.random.uniform(jax.random.fold_in(jax.random.fold_in(rng, 6), position), (parts,), jnp.float32, smallest / len(cuts), high / len(cuts))
        loudness = loudness * jnp.repeat(jnp.exp(heights), extent[position] // parts).reshape((-1,) + (1,) * (len(extent) - 1 - position))
    return loudness


def bell_draw(rng, extent, width, limit, cuts=(), held_as=jnp.bfloat16):
    loudness = level_of(rng, extent, cuts, -0.22, 0.18) if cuts else 1.0
    values = jax.random.normal(rng, extent, jnp.float32) * width * loudness
    return jnp.minimum(jnp.maximum(values, -limit), limit).astype(held_as)


def setup_inputs(seed: int = 0) -> dict:
    key_of = jax.random.split(jax.random.key(seed), 23)
    return {
        "hidden": bell_draw(key_of[0], (SEQS, LENGTH, D), 1.0, 6.0, ((0, 4), (1, 4))),
        "cotangent": bell_draw(key_of[1], (SEQS, LENGTH, D), 1.0, 6.0, ((0, 4), (1, 4))),
        "gating": bell_draw(key_of[2], (D, INNER), D ** -0.5, 0.21875, ((0, 16), (1, 2)), jnp.float32),
        "values": bell_draw(key_of[3], (D, INNER), D ** -0.5, 0.21875, ((0, 16), (1, 2)), jnp.float32),
        "selector": bell_draw(key_of[4], (D, 2 * STATE), D ** -0.5, 0.21875, ((0, 16), (1, 2)), jnp.float32),
        "timestep": bell_draw(key_of[5], (D, HEADS), (D // 4) ** -0.5, 0.4375, ((0, 16), (1, 2)), jnp.float32),
        "output": bell_draw(key_of[6], (INNER, D), INNER ** -0.5, 0.15625, ((0, 2), (1, 16)), jnp.float32),
        "prenorm": jnp.clip(1.0 + 0.1 * jax.random.normal(key_of[7], (D,), jnp.float32), 0.5, 1.5),
        "postnorm": jnp.clip(1.0 + 0.1 * jax.random.normal(key_of[8], (INNER,), jnp.float32), 0.5, 1.5),
        "filters": bell_draw(key_of[9], (KCONV + 1, INNER), KCONV ** -0.5, 3.0, ((1, 2),), jnp.float32),
        "kernels": bell_draw(key_of[10], (KCONV + 1, 2 * STATE), KCONV ** -0.5, 3.0, ((1, 2),), jnp.float32),
        "scalars": draw_scalars(jax.random.fold_in(key_of[22], 71), 0),
        "gating_adam": draw_gating_adam(jax.random.fold_in(key_of[22], 71), 0),
        "values_adam": draw_values_adam(jax.random.fold_in(key_of[22], 71), 0),
        "selector_adam": draw_selector_adam(jax.random.fold_in(key_of[22], 71), 0),
        "timestep_adam": draw_timestep_adam(jax.random.fold_in(key_of[22], 71), 0),
        "output_adam": draw_output_adam(jax.random.fold_in(key_of[22], 71), 0),
        "prenorm_adam": draw_prenorm_adam(jax.random.fold_in(key_of[22], 71), 0),
        "postnorm_adam": draw_postnorm_adam(jax.random.fold_in(key_of[22], 71), 0),
        "filters_adam": draw_filters_adam(jax.random.fold_in(key_of[22], 71), 0),
        "kernels_adam": draw_kernels_adam(jax.random.fold_in(key_of[22], 71), 0),
        "scalars_adam": draw_scalars_adam(jax.random.fold_in(key_of[22], 71), 0),
    }


epsilon = 1e-05
highest = lax.Precision.HIGHEST
learn_rate = 0.01
first_decay = 0.9
second_decay = 0.999
adam_epsilon = 1e-08
weight_decay = 0.1

def swish_parts(value):
    sigmoid = jax.nn.sigmoid(value)
    return (value * sigmoid, sigmoid * (1.0 + value * (1.0 - sigmoid)))

def product(form, left, right):
    return jnp.einsum(form, left.astype(jnp.float32), right.astype(jnp.float32), precision=highest)

def conv_apply(padded, taps):
    tap_count = taps.shape[0] - 1
    length = padded.shape[1] - tap_count + 1
    wide = padded.astype(jnp.float32)
    total = taps[tap_count] + taps[0] * wide[:, 0:length]
    for index in range(1, tap_count):
        total = total + taps[index] * wide[:, index:index + length]
    return total

def conv_back(padded, taps, grad_pre):
    tap_count = taps.shape[0] - 1
    length = grad_pre.shape[1]
    wide = padded.astype(jnp.float32)
    tap_rows = [lax.optimization_barrier(jnp.sum(grad_pre * wide[:, index:index + length], axis=(0, 1))) for index in range(tap_count)]
    tap_rows.append(lax.optimization_barrier(jnp.sum(grad_pre, axis=(0, 1))))
    grad_pad = jnp.zeros(padded.shape, jnp.float32)
    for index in range(tap_count):
        grad_pad = grad_pad + jnp.pad(taps[index] * grad_pre, ((0, 0), (index, tap_count - 1 - index), (0, 0)))
    return (jnp.stack(tap_rows), grad_pad)

def group_terms(inner, write_vec, read_vec, delta, running):
    length = inner.shape[1]
    scores = product('btn,bun->btu', read_vec, write_vec)
    causal = jnp.arange(length)[:, None] >= jnp.arange(length)[None, :]
    by_head = jnp.transpose(running, (0, 2, 1))
    gap = by_head[:, :, :, None] - by_head[:, :, None, :]
    decays = jnp.exp(jnp.where(causal, gap, -jnp.inf))
    step_head = jnp.transpose(delta, (0, 2, 1))
    mixing = scores[:, None] * decays * step_head[:, :, None, :]
    mixing_b = mixing.astype(jnp.bfloat16)
    within = product('bhtu,buhp->bthp', mixing_b, inner)
    inner_f = inner.astype(jnp.float32)
    weight_end = jnp.exp(running[:, -1:, :] - running) * delta
    local_state = product('bthp,btn->bhpn', inner_f * weight_end[..., None], write_vec)
    carry_decay = jnp.exp(running[:, -1, :])
    return (scores, decays, mixing_b, within, weight_end, local_state, carry_decay)

def group_back_first(inner, write_vec, read_vec, delta, running, skip, entering, grad_mixer, scores, decays, mixing_b):
    grad_half = grad_mixer.astype(jnp.bfloat16)
    inner_f = inner.astype(jnp.float32)
    skip_grad = lax.optimization_barrier(jnp.sum(grad_mixer * inner_f, axis=(0, 1, 3)))
    grad_inner = skip[None, None, :, None] * grad_mixer + product('bhtu,bthp->buhp', mixing_b, grad_half)
    grad_mix = product('bthp,buhp->bhtu', grad_half, inner)
    step_head = jnp.transpose(delta, (0, 2, 1))
    kernel = grad_mix * decays * scores[:, None]
    grad_delta = jnp.transpose(lax.optimization_barrier(jnp.sum(kernel, axis=2)), (0, 2, 1))
    weighted = kernel * step_head[:, :, None, :]
    grad_running = jnp.transpose(lax.optimization_barrier(jnp.sum(weighted, axis=3)) - lax.optimization_barrier(jnp.sum(weighted, axis=2)), (0, 2, 1))
    grad_scores = lax.optimization_barrier(jnp.sum(grad_mix * decays * step_head[:, :, None, :], axis=1))
    grad_read = product('btu,bun->btn', grad_scores, write_vec)
    grad_write = product('btu,btn->bun', grad_scores, read_vec)
    growth = jnp.exp(running)
    across = product('btn,bhpn->bthp', read_vec, entering)
    grad_running = grad_running + lax.optimization_barrier(jnp.sum(grad_mixer * across, axis=3)) * growth
    scaled = grad_mixer * growth[..., None]
    grad_read = grad_read + product('bthp,bhpn->btn', scaled, entering)
    pushed = product('bthp,btn->bhpn', scaled, read_vec)
    return (grad_inner, grad_delta, grad_running, grad_write, grad_read, skip_grad, pushed)

def group_back_second(inner, write_vec, delta, running, weight_end, entering, carry_decay, end_grad, grad_inner, grad_delta, grad_running, grad_write):
    inner_f = inner.astype(jnp.float32)
    decay_grad = lax.optimization_barrier(jnp.sum(end_grad * entering, axis=(2, 3)))
    end_extra = decay_grad * carry_decay
    grad_xw = product('bhpn,btn->bthp', end_grad, write_vec)
    grad_write = grad_write + product('bhpn,bthp->btn', end_grad, inner_f * weight_end[..., None])
    grad_inner = grad_inner + grad_xw * weight_end[..., None]
    grad_weight = lax.optimization_barrier(jnp.sum(grad_xw * inner_f, axis=3))
    grad_delta = grad_delta + grad_weight * jnp.exp(running[:, -1:, :] - running)
    spread = grad_weight * weight_end
    end_extra = end_extra + lax.optimization_barrier(jnp.sum(spread, axis=1))
    grad_running = grad_running - spread
    grad_running = jnp.concatenate([grad_running[:, :-1], grad_running[:, -1:] + end_extra[:, None]], axis=1)
    grad_log = jnp.flip(jnp.cumsum(jnp.flip(grad_running, 1), axis=1), 1)
    return (grad_inner, grad_delta, grad_write, grad_log)

def adamw(param, moments, grad):
    first = first_decay * moments[0] + (1.0 - first_decay) * grad
    second = second_decay * moments[1] + (1.0 - second_decay) * grad * grad
    first_hat = first / (1.0 - first_decay ** STEP)
    second_hat = second / (1.0 - second_decay ** STEP)
    fresh = param - learn_rate * (first_hat / (jnp.sqrt(second_hat) + adam_epsilon) + weight_decay * param)
    return (fresh, jnp.stack([first, second]))

def advance(state, item):
    return (item[0][:, None, None] * state + item[1], state)

def reference(hidden, cotangent, gating, values, selector, timestep, output, prenorm, postnorm, filters, kernels, scalars, gating_adam, values_adam, selector_adam, timestep_adam, output_adam, prenorm_adam, postnorm_adam, filters_adam, kernels_adam, scalars_adam):
    half = jnp.bfloat16
    single = jnp.float32
    gate_weight = gating.astype(half)
    value_weight = values.astype(half)
    select_weight = selector.astype(half)
    delta_weight = timestep.astype(half)
    out_weight = output.astype(half)
    entry_gain = prenorm.astype(half).astype(single)
    groups = LENGTH // GROUP
    lead = KCONV - 1
    bias = scalars[0]
    rate = -jnp.exp(scalars[1])
    skip = scalars[2]

    def one_sequence(carry, pair):
        tokens, upstream = pair
        residual = tokens.astype(single)
        entry_scale = lax.rsqrt(lax.optimization_barrier(jnp.mean(residual * residual, axis=-1, keepdims=True)) + epsilon)
        normed = (residual * entry_scale * entry_gain).astype(half)
        gate_raw = jnp.dot(normed, gate_weight, preferred_element_type=single).astype(half)
        inner_raw = jnp.dot(normed, value_weight, preferred_element_type=single).astype(half)
        select_raw = jnp.dot(normed, select_weight, preferred_element_type=single).astype(half)
        delta_raw = jnp.dot(normed, delta_weight, preferred_element_type=single)
        inner_pad = jnp.concatenate([jnp.zeros((lead, INNER), half), inner_raw], axis=0)[None]
        select_pad = jnp.concatenate([jnp.zeros((lead, 2 * STATE), half), select_raw], axis=0)[None]
        inner_value, inner_slope = swish_parts(conv_apply(inner_pad, filters)[0])
        select_value, select_slope = swish_parts(conv_apply(select_pad, kernels)[0])
        inner_act = inner_value.astype(half)
        select_act = select_value.astype(half)
        delta = jax.nn.softplus(delta_raw + bias)
        inner_h = inner_act.reshape(groups, GROUP, HEADS, HEADDIM)
        write_vec = select_act[:, :STATE].reshape(groups, GROUP, STATE)
        read_vec = select_act[:, STATE:].reshape(groups, GROUP, STATE)
        delta_c = delta.reshape(groups, GROUP, HEADS)
        running = jnp.cumsum(delta_c * rate, axis=1)
        scores, decays, mixing_b, within, weight_end, local_state, carry_decay = group_terms(inner_h, write_vec, read_vec, delta_c, running)
        zeros = jnp.zeros((HEADS, HEADDIM, STATE), single)
        entering = lax.scan(advance, zeros, (carry_decay, local_state))[1]
        growth = jnp.exp(running)
        across = product('btn,bhpn->bthp', read_vec, entering)
        inner_f = inner_h.astype(single)
        mixer_out = (within + growth[..., None] * across + skip[None, None, :, None] * inner_f).reshape(LENGTH, INNER)
        gate_act, gate_slope = swish_parts(gate_raw.astype(single))
        gated = mixer_out * gate_act
        gate_scale = lax.rsqrt(lax.optimization_barrier(jnp.mean(gated * gated, axis=-1, keepdims=True)) + epsilon)
        mixed = (gated * gate_scale * postnorm).astype(half)
        result = residual + jnp.dot(mixed, out_weight, preferred_element_type=single)
        grad_mixed = jnp.dot(upstream, out_weight.T, preferred_element_type=single)
        output_grad = jnp.dot(mixed.T, upstream, preferred_element_type=single)
        postnorm_grad = lax.optimization_barrier(jnp.sum(grad_mixed * gated * gate_scale, axis=0))
        hat_gated = grad_mixed * postnorm
        cube = gate_scale * gate_scale * gate_scale
        grad_gated = gate_scale * hat_gated - gated * cube * lax.optimization_barrier(jnp.mean(hat_gated * gated, axis=-1, keepdims=True))
        grad_mixer = (grad_gated * gate_act).reshape(groups, GROUP, HEADS, HEADDIM)
        grad_gate = (grad_gated * mixer_out * gate_slope).astype(half)
        grad_inner, grad_delta, grad_running, grad_write, grad_read, skip_grad, pushed = group_back_first(inner_h, write_vec, read_vec, delta_c, running, skip, entering, grad_mixer, scores, decays, mixing_b)
        end_grad = lax.scan(advance, zeros, (carry_decay, pushed), reverse=True)[1]
        grad_inner, grad_delta, grad_write, grad_log = group_back_second(inner_h, write_vec, delta_c, running, weight_end, entering, carry_decay, end_grad, grad_inner, grad_delta, grad_running, grad_write)
        grad_delta = grad_delta + grad_log * rate
        alog_grad = lax.optimization_barrier(jnp.sum(grad_log * delta_c, axis=(0, 1))) * rate
        grad_delta_pre = grad_delta.reshape(LENGTH, HEADS) * jax.nn.sigmoid(delta_raw + bias)
        bias_grad = lax.optimization_barrier(jnp.sum(grad_delta_pre, axis=0))
        grad_select = jnp.concatenate([grad_write, grad_read], axis=2).reshape(LENGTH, 2 * STATE)
        filters_grad, inner_pad_grad = conv_back(inner_pad, filters, (grad_inner.reshape(LENGTH, INNER) * inner_slope)[None])
        kernels_grad, select_pad_grad = conv_back(select_pad, kernels, (grad_select * select_slope)[None])
        inner_raw_grad = inner_pad_grad[0, lead:].astype(half)
        select_raw_grad = select_pad_grad[0, lead:].astype(half)
        delta_half = grad_delta_pre.astype(half)
        grad_normed = jnp.dot(grad_gate, gate_weight.T, preferred_element_type=single)
        grad_normed = grad_normed + jnp.dot(inner_raw_grad, value_weight.T, preferred_element_type=single)
        grad_normed = grad_normed + jnp.dot(select_raw_grad, select_weight.T, preferred_element_type=single)
        grad_normed = grad_normed + jnp.dot(delta_half, delta_weight.T, preferred_element_type=single)
        prenorm_grad = lax.optimization_barrier(jnp.sum(grad_normed * residual * entry_scale, axis=0))
        hat = grad_normed * entry_gain
        hidden_grad = upstream.astype(single) + entry_scale * hat - residual * entry_scale * entry_scale * entry_scale * lax.optimization_barrier(jnp.mean(hat * residual, axis=-1, keepdims=True))
        terms = (jnp.dot(normed.T, grad_gate, preferred_element_type=single), jnp.dot(normed.T, inner_raw_grad, preferred_element_type=single), jnp.dot(normed.T, select_raw_grad, preferred_element_type=single), jnp.dot(normed.T, delta_half, preferred_element_type=single), output_grad, prenorm_grad, postnorm_grad, filters_grad, kernels_grad, jnp.stack([bias_grad, alog_grad, skip_grad]))
        carry = tuple((total + term for total, term in zip(carry, terms)))
        return (carry, (result, hidden_grad))
    params = (gating, values, selector, timestep, output, prenorm, postnorm, filters, kernels, scalars)
    moments = (gating_adam, values_adam, selector_adam, timestep_adam, output_adam, prenorm_adam, postnorm_adam, filters_adam, kernels_adam, scalars_adam)
    start = tuple((jnp.zeros(param.shape, single) for param in params))
    grads, stacked = lax.scan(one_sequence, start, (hidden, cotangent))
    updated = [adamw(param, moment, grad) for param, moment, grad in zip(params, moments, grads)]
    return (stacked[0], stacked[1], grads[0], grads[1], grads[2], grads[3], grads[4], grads[5], grads[6], grads[7], grads[8], grads[9], updated[0][0], updated[1][0], updated[2][0], updated[3][0], updated[4][0], updated[5][0], updated[6][0], updated[7][0], updated[8][0], updated[9][0], updated[0][1], updated[1][1], updated[2][1], updated[3][1], updated[4][1], updated[5][1], updated[6][1], updated[7][1], updated[8][1], updated[9][1])
```

```python
import functools
from typing import NamedTuple
import jax
import jax.numpy as jnp
from jax import lax
from jax.experimental import pallas as pl
from jax.experimental.pallas import tpu as pltpu
from jax.sharding import PartitionSpec as P

INNER = 1536
STATE = 128
HEADDIM = 64
STEP = 2


epsilon = 1e-05
highest = lax.Precision.HIGHEST
learn_rate = 0.01
first_decay = 0.9
second_decay = 0.999
adam_epsilon = 1e-08
weight_decay = 0.1


def from_behind(block, axis, distance):
    devices = range(lax.axis_size(axis))
    route = [(i - distance, i) for i in devices if i - distance in devices]
    return lax.ppermute(block, axis, route)


MESH = pl.DeviceIdType.MESH
VMEM = pl.BlockSpec(memory_space=pltpu.VMEM)
ANY = pl.BlockSpec(memory_space=pl.ANY)
LANES = 128
PARTS = 12
VMEM_BYTES = 60 * 2**20


def send(src, dst, send_sem, recv_sem, device):
    return pltpu.make_async_remote_copy(
        src_ref=src,
        dst_ref=dst,
        send_sem=send_sem,
        recv_sem=recv_sem,
        device_id=device,
        device_id_type=MESH,
    )


def greet(devices):
    barrier = pltpu.get_barrier_semaphore()
    for device in devices:
        pl.semaphore_signal(barrier, inc=1, device_id=device, device_id_type=MESH)
    pl.semaphore_wait(barrier, len(devices))


def params_of(collective_id):
    return pltpu.CompilerParams(collective_id=collective_id, has_side_effects=True)


def swap_kernel(x_ref, o_ref, send_sem, recv_sem):
    other = {"tensor": 1 - lax.axis_index("tensor")}
    greet([other])
    copy = send(x_ref, o_ref, send_sem, recv_sem, other)
    copy.start()
    copy.wait()


def swap(value, collective_id):
    return pl.pallas_call(
        swap_kernel,
        out_shape=jax.ShapeDtypeStruct(value.shape, value.dtype),
        in_specs=[VMEM],
        out_specs=VMEM,
        scratch_shapes=[pltpu.SemaphoreType.DMA, pltpu.SemaphoreType.DMA],
        compiler_params=params_of(collective_id),
    )(value)


def carry_kernel(count, step, parts, decay_ref, local_ref, o_ref, out_buf, in_buf, send_sem, recv_sem):
    me = lax.axis_index("seq")
    target = lax.rem(me + count + step, count)
    source = lax.rem(me + count - step, count)
    first, last = (0, count - 1) if step > 0 else (count - 1, 0)
    greet([{"seq": target}, {"seq": source}])
    size = local_ref.shape[0] // parts

    def copy_of(part):
        return send(
            out_buf.at[part],
            in_buf.at[part],
            send_sem.at[part],
            recv_sem.at[part],
            {"seq": target},
        )

    for part in range(parts):
        rows = pl.ds(part * size, size)

        @pl.when(me == first)
        def _():
            o_ref[rows] = jnp.zeros((size,) + o_ref.shape[1:], o_ref.dtype)
            out_buf[part] = local_ref[rows].astype(jnp.bfloat16)

        @pl.when(me != first)
        def _():
            copy_of(part).wait_recv()
            entering = in_buf[part]
            o_ref[rows] = entering
            out_buf[part] = (
                decay_ref[rows] * entering.astype(jnp.float32) + local_ref[rows]
            ).astype(jnp.bfloat16)

        @pl.when(me != last)
        def _():
            copy_of(part).start()

    @pl.when(me != last)
    def _():
        for part in range(parts):
            copy_of(part).wait_send()


def carry(decay, local, count, step, collective_id):
    seqs, heads, wide, deep = local.shape
    total = seqs * heads
    parts = 6 if total % 6 == 0 else 1
    size = total // parts
    spread = jnp.broadcast_to(decay.reshape(total, 1, 1), (total, 1, deep))
    result = pl.pallas_call(
        functools.partial(carry_kernel, count, step, parts),
        out_shape=jax.ShapeDtypeStruct((total, wide, deep), jnp.bfloat16),
        in_specs=[VMEM, VMEM],
        out_specs=VMEM,
        scratch_shapes=[
            pltpu.VMEM((parts, size, wide, deep), jnp.bfloat16),
            pltpu.VMEM((parts, size, wide, deep), jnp.bfloat16),
            pltpu.SemaphoreType.DMA((parts,)),
            pltpu.SemaphoreType.DMA((parts,)),
        ],
        compiler_params=params_of(collective_id),
    )(spread, local.reshape(total, wide, deep))
    return result.reshape(local.shape)


def swish_parts(value):
    sigmoid = jax.nn.sigmoid(value)
    return (value * sigmoid, sigmoid * (1.0 + value * (1.0 - sigmoid)))


def conv_apply(padded, taps):
    tap_count = taps.shape[0] - 1
    length = padded.shape[1] - tap_count + 1
    wide = padded.astype(jnp.float32)
    total = taps[tap_count] + taps[0] * wide[:, 0:length]
    for index in range(1, tap_count):
        total = total + taps[index] * wide[:, index : index + length]
    return total


def conv_back(padded, taps, grad_pre):
    tap_count = taps.shape[0] - 1
    length = grad_pre.shape[1]
    wide = padded.astype(jnp.float32)
    tap_rows = [
        jnp.sum(grad_pre * wide[:, index : index + length], axis=(0, 1))
        for index in range(tap_count)
    ]
    tap_rows.append(jnp.sum(grad_pre, axis=(0, 1)))
    grad_pad = jnp.zeros(padded.shape, jnp.float32)
    for index in range(tap_count):
        grad_pad = grad_pad + jnp.pad(
            taps[index] * grad_pre, ((0, 0), (index, tap_count - 1 - index), (0, 0))
        )
    return (jnp.stack(tap_rows), grad_pad)


def adamw(param, moments, grad):
    first = first_decay * moments[0] + (1.0 - first_decay) * grad
    second = second_decay * moments[1] + (1.0 - second_decay) * grad * grad
    first_hat = first / (1.0 - first_decay**STEP)
    second_hat = second / (1.0 - second_decay**STEP)
    fresh = param - learn_rate * (
        first_hat / (jnp.sqrt(second_hat) + adam_epsilon) + weight_decay * param
    )
    return (fresh, jnp.stack([first, second]))


def general(
    hidden,
    cotangent,
    gating,
    values,
    selector,
    timestep,
    output,
    prenorm,
    postnorm,
    filters,
    kernels,
    scalars,
    gating_adam,
    values_adam,
    selector_adam,
    timestep_adam,
    output_adam,
    prenorm_adam,
    postnorm_adam,
    filters_adam,
    kernels_adam,
    scalars_adam,
):
    half = jnp.bfloat16
    single = jnp.float32
    n_seq = lax.axis_size("seq")
    core = lax.axis_index("tensor")
    seqs_dev, length, width = hidden.shape
    rows = seqs_dev * length
    own_rows = gating.shape[0]
    lead = filters.shape[0] - 2
    heads_here = timestep.shape[1]
    inner_here = gating.shape[1]
    select_here = selector.shape[1]
    conv_end = 2 * inner_here + select_here
    step_wide = 128
    in_wide = conv_end + step_wide
    packed = jnp.concatenate(
        [
            gating.astype(half),
            values.astype(half),
            selector.astype(half),
            timestep.astype(half),
            prenorm.astype(half)[:, None],
            jnp.zeros((own_rows, step_wide - heads_here - 1), half),
            output.T.astype(half),
        ],
        axis=1,
    )
    weights = lax.all_gather(packed, ("dp", "seq"), axis=0, tiled=True)
    in_weight = weights[:, :in_wide]
    out_weight = weights[:, in_wide:]
    bias = scalars[0]
    rate = -jnp.exp(scalars[1])
    skip = scalars[2]
    entry_gain = weights[:, conv_end + heads_here].astype(single)
    residual = hidden.astype(single)
    entry_scale = lax.rsqrt(jnp.mean(residual * residual, axis=-1, keepdims=True) + epsilon)
    normed = (residual * entry_scale * entry_gain).astype(half)
    flat = normed.reshape(rows, width)
    raw = jnp.dot(flat, in_weight, preferred_element_type=single)
    gate_raw = raw[:, :inner_here].astype(half).reshape(seqs_dev, length, inner_here)
    conv_raw = raw[:, inner_here:conv_end].astype(half).reshape(seqs_dev, length, -1)
    delta_raw = raw[:, conv_end : conv_end + heads_here].reshape(seqs_dev, length, heads_here)
    tails = from_behind(conv_raw[:, length - lead :], "seq", 1)
    conv_pad = jnp.concatenate([tails, conv_raw], axis=1)
    taps = jnp.concatenate([filters, kernels], axis=1)
    conv_value, conv_slope = swish_parts(conv_apply(conv_pad, taps))
    conv_act = conv_value.astype(half)
    inner_act = conv_act[:, :, :inner_here]
    mine = conv_act[:, :, inner_here:]
    theirs = swap(mine.reshape(rows, select_here), 1).reshape(mine.shape)
    write_vec = jnp.where(core == 0, mine, theirs)
    read_vec = jnp.where(core == 0, theirs, mine)
    delta = jax.nn.softplus(delta_raw + bias)
    lower = jnp.tril(jnp.ones((length, length), single))
    running = jnp.einsum("tu,buh->bth", lower, delta * rate, precision=highest)
    inner_h = inner_act.reshape(seqs_dev, length, heads_here, HEADDIM)
    inner_f = inner_h.astype(single)
    weight_end = jnp.exp(running[:, -1:, :] - running) * delta
    carry_decay = jnp.exp(running[:, -1, :])
    growth = jnp.exp(running)
    inner_w = (inner_f * weight_end[..., None]).astype(half)
    local_state = jnp.einsum("bthp,btn->bhpn", inner_w, write_vec, preferred_element_type=single)
    entering = carry(carry_decay, local_state, n_seq, 1, 7)
    scores = jnp.einsum("btn,bun->btu", read_vec, write_vec, preferred_element_type=single)
    causal = jnp.arange(length)[:, None] >= jnp.arange(length)[None, :]
    by_head = jnp.transpose(running, (0, 2, 1))
    gap = by_head[:, :, :, None] - by_head[:, :, None, :]
    decays = jnp.exp(jnp.where(causal, gap, -jnp.inf))
    step_head = jnp.transpose(delta, (0, 2, 1))
    mixing_b = (scores[:, None] * decays * step_head[:, :, None, :]).astype(half)
    within = jnp.einsum("bhtu,buhp->bthp", mixing_b, inner_h, preferred_element_type=single)
    across = jnp.einsum("btn,bhpn->bthp", read_vec, entering, preferred_element_type=single)
    mixer_out = (within + growth[..., None] * across + skip[None, None, :, None] * inner_f).reshape(
        seqs_dev, length, inner_here
    )
    gate_act, gate_slope = swish_parts(gate_raw.astype(single))
    gated = mixer_out * gate_act
    upstream = cotangent.reshape(rows, width)
    grad_mixed = jnp.dot(upstream, out_weight, preferred_element_type=single).reshape(
        seqs_dev, length, inner_here
    )
    hat_gated = grad_mixed * postnorm
    sums = jnp.stack([jnp.sum(gated * gated, axis=-1), jnp.sum(hat_gated * gated, axis=-1)])
    lanes = sums.reshape(-1, 128)
    sums = (lanes + swap(lanes, 2)).reshape(sums.shape)
    squares, dots = sums[0], sums[1]
    gate_scale = lax.rsqrt(squares / INNER + epsilon)[..., None]
    mixed_flat = (gated * gate_scale * postnorm).astype(half).reshape(rows, inner_here)
    branch = lax.dot_general(
        mixed_flat, out_weight, (((1,), (1,)), ((), ())), preferred_element_type=single
    ).astype(half)
    output_grad = lax.dot_general(
        upstream, mixed_flat, (((0,), (0,)), ((), ())), preferred_element_type=single
    )
    postnorm_grad = jnp.sum(grad_mixed * gated * gate_scale, axis=(0, 1))
    cube = gate_scale * gate_scale * gate_scale
    grad_gated = gate_scale * hat_gated - gated * cube * (dots / INNER)[..., None]
    grad_mixer = (grad_gated * gate_act).reshape(seqs_dev, length, heads_here, HEADDIM)
    grad_gate = (grad_gated * mixer_out * gate_slope).astype(half).reshape(rows, inner_here)

    scaled = (grad_mixer * growth[..., None]).astype(half)
    pushed = jnp.einsum("bthp,btn->bhpn", scaled, read_vec, preferred_element_type=single)
    end_grad = carry(carry_decay, pushed, n_seq, -1, 8)

    grad_half = grad_mixer.astype(half)
    skip_grad = jnp.sum(grad_mixer * inner_f, axis=(0, 1, 3))
    grad_inner = skip[None, None, :, None] * grad_mixer + jnp.einsum(
        "bhtu,bthp->buhp", mixing_b, grad_half, preferred_element_type=single
    )
    grad_mix = jnp.einsum("bthp,buhp->bhtu", grad_half, inner_h, preferred_element_type=single)
    spread_mix = grad_mix * decays
    kernel = spread_mix * scores[:, None]
    grad_delta = jnp.transpose(jnp.sum(kernel, axis=2), (0, 2, 1))
    weighted = kernel * step_head[:, :, None, :]
    grad_running = jnp.transpose(jnp.sum(weighted, axis=3) - jnp.sum(weighted, axis=2), (0, 2, 1))
    grad_scores = jnp.sum(spread_mix * step_head[:, :, None, :], axis=1).astype(half)
    grad_read = jnp.einsum("btu,bun->btn", grad_scores, write_vec, preferred_element_type=single)
    grad_write = jnp.einsum("btu,btn->bun", grad_scores, read_vec, preferred_element_type=single)
    grad_running = grad_running + jnp.sum(grad_mixer * across, axis=3) * growth
    grad_read = grad_read + jnp.einsum(
        "bthp,bhpn->btn", scaled, entering, preferred_element_type=single
    )

    decay_grad = jnp.sum(end_grad.astype(single) * entering.astype(single), axis=(2, 3))
    end_extra = decay_grad * carry_decay
    grad_xw = jnp.einsum("bhpn,btn->bthp", end_grad, write_vec, preferred_element_type=single)
    grad_write = grad_write + jnp.einsum(
        "bhpn,bthp->btn", end_grad, inner_w, preferred_element_type=single
    )
    grad_inner = grad_inner + grad_xw * weight_end[..., None]
    grad_weight = jnp.sum(grad_xw * inner_f, axis=3)
    grad_delta = grad_delta + grad_weight * jnp.exp(running[:, -1:, :] - running)
    spread = grad_weight * weight_end
    end_extra = end_extra + jnp.sum(spread, axis=1)
    grad_running = grad_running - spread
    grad_running = jnp.concatenate(
        [grad_running[:, :-1], grad_running[:, -1:] + end_extra[:, None]], axis=1
    )
    grad_log = jnp.einsum("tu,bth->buh", lower, grad_running, precision=highest)

    grad_delta = grad_delta + grad_log * rate
    alog_grad = jnp.sum(grad_log * delta, axis=(0, 1)) * rate
    grad_delta_pre = grad_delta * jax.nn.sigmoid(delta_raw + bias)
    bias_grad = jnp.sum(grad_delta_pre, axis=(0, 1))
    kept = jnp.where(core == 0, grad_write, grad_read)
    given = jnp.where(core == 0, grad_read, grad_write)
    grad_select = kept + swap(given.reshape(rows, select_here), 4).reshape(kept.shape)
    grad_conv = jnp.concatenate(
        [grad_inner.reshape(seqs_dev, length, inner_here), grad_select], axis=2
    )
    taps_grad, conv_pad_grad = conv_back(conv_pad, taps, grad_conv * conv_slope)
    back = from_behind(conv_pad_grad[:, :lead], "seq", -1)
    conv_raw_grad = (
        jnp.concatenate(
            [conv_pad_grad[:, lead:length], conv_pad_grad[:, length:] + back], axis=1
        )
        .astype(half)
        .reshape(rows, -1)
    )
    grad_all = jnp.concatenate(
        [
            grad_gate,
            conv_raw_grad,
            grad_delta_pre.astype(half).reshape(rows, heads_here),
            jnp.zeros((rows, step_wide - heads_here), half),
        ],
        axis=1,
    )
    grad_part = lax.dot_general(
        grad_all, in_weight, (((1,), (1,)), ((), ())), preferred_element_type=single
    ).astype(half)
    in_grad = lax.dot_general(
        flat, grad_all, (((0,), (0,)), ((), ())), preferred_element_type=single
    )
    prenorm_part = jnp.sum(
        grad_part.astype(single).reshape(seqs_dev, length, width) * residual * entry_scale,
        axis=(0, 1),
    )
    gain_column = conv_end + heads_here
    packed_grad = jnp.concatenate(
        [
            in_grad.astype(half),
            output_grad.astype(half),
        ],
        axis=1,
    )
    tap_rows = filters.shape[0]
    scalars_local = jnp.stack([bias_grad, alog_grad, skip_grad])
    loose = jnp.concatenate([taps_grad[:, inner_here:].reshape(-1), scalars_local.reshape(-1)])
    small = jnp.concatenate(
        [
            taps_grad[:, :inner_here],
            postnorm_grad[None],
            jnp.pad(loose, (0, inner_here - loose.shape[0]))[None],
            prenorm_part[None],
        ],
        axis=0,
    )
    summed = lax.psum_scatter(
        packed_grad.astype(single), ("dp", "seq"), scatter_dimension=0, tiled=True
    )
    small = lax.psum(small, ("dp", "seq"))
    prenorm_grad = lax.psum(small[-1], "tensor")
    branch_far, part_far = swap(branch, 3), swap(grad_part, 5)
    own = lax.axis_index("dp") * n_seq + lax.axis_index("seq")
    prenorm_grad = lax.dynamic_slice_in_dim(prenorm_grad, own * own_rows, own_rows)
    branch = branch.astype(single) + branch_far.astype(single)
    result = residual + branch.reshape(seqs_dev, length, width)
    grad_part = grad_part.astype(single) + part_far.astype(single)
    grad_normed = grad_part.reshape(seqs_dev, length, width)
    hat = grad_normed * entry_gain
    hidden_grad = (
        cotangent.astype(single)
        + entry_scale * hat
        - residual
        * entry_scale
        * entry_scale
        * entry_scale
        * jnp.mean(hat * residual, axis=-1, keepdims=True)
    )
    loose_end = tap_rows * select_here
    grads = (
        summed[:, :inner_here],
        summed[:, inner_here : 2 * inner_here],
        summed[:, 2 * inner_here : conv_end],
        summed[:, conv_end:gain_column],
        summed[:, in_wide:].T,
        prenorm_grad,
        small[tap_rows],
        small[:tap_rows],
        small[tap_rows + 1, :loose_end].reshape(tap_rows, select_here),
        small[tap_rows + 1, loose_end : loose_end + 3 * heads_here].reshape(3, heads_here),
    )
    params = (
        gating,
        values,
        selector,
        timestep,
        output,
        prenorm,
        postnorm,
        filters,
        kernels,
        scalars,
    )
    moments = (
        gating_adam,
        values_adam,
        selector_adam,
        timestep_adam,
        output_adam,
        prenorm_adam,
        postnorm_adam,
        filters_adam,
        kernels_adam,
        scalars_adam,
    )
    updated = [adamw(param, moment, grad) for param, moment, grad in zip(params, moments, grads)]
    return (
        result,
        hidden_grad,
        grads[0],
        grads[1],
        grads[2],
        grads[3],
        grads[4],
        grads[5],
        grads[6],
        grads[7],
        grads[8],
        grads[9],
        updated[0][0],
        updated[1][0],
        updated[2][0],
        updated[3][0],
        updated[4][0],
        updated[5][0],
        updated[6][0],
        updated[7][0],
        updated[8][0],
        updated[9][0],
        updated[0][1],
        updated[1][1],
        updated[2][1],
        updated[3][1],
        updated[4][1],
        updated[5][1],
        updated[6][1],
        updated[7][1],
        updated[8][1],
        updated[9][1],
    )


def split(value, parts):
    pieces = []
    for _ in range(parts):
        piece = value.astype(jnp.bfloat16)
        pieces.append(piece)
        value = value - piece.astype(jnp.float32)
    return pieces


def mul(left, right):
    return jnp.dot(left, right, preferred_element_type=jnp.float32)


def mul_nt(left, right):
    return lax.dot_general(
        left, right, (((1,), (1,)), ((), ())), preferred_element_type=jnp.float32
    )


def mul_tn(left, right):
    return lax.dot_general(
        left, right, (((0,), (0,)), ((), ())), preferred_element_type=jnp.float32
    )


def wide_mul(value, table, parts):
    total = None
    for piece in split(value, parts):
        term = mul(piece, table)
        total = term if total is None else total + term
    return total


def table_mul(table, value, parts):
    total = None
    for piece in split(value, parts):
        term = mul(table, piece)
        total = term if total is None else total + term
    return total


def iota(shape, axis):
    return lax.broadcasted_iota(jnp.int32, shape, axis)


def each(count, step, body, start=None):
    def one(index, state):
        return body(pl.multiple_of(index * step, step), state)

    return lax.fori_loop(0, count, one, 0 if start is None else start)


def fold(value):
    rows, columns = value.shape
    return jnp.sum(value.reshape(rows // 8, 8, columns), axis=0)


class Table(NamedTuple):
    gat: object
    val: object
    sel: object
    hid: object
    cot: object
    wa: object
    wb: object
    scale: object
    normed: object
    raw: object
    draw: object
    delta: object
    run: object
    run3: object
    wend: object
    runt: object
    deltat: object
    gdt: object
    growth: object
    ending: object
    x: object
    xw: object
    slope: object
    mine: object
    theirs: object
    bvec: object
    cvec: object
    scores: object
    local: object
    decay: object
    enter: object
    leave: object
    gend: object
    gout: object
    mix: object
    mixer: object
    across: object
    z: object
    gmix: object
    sums: object
    sums_far: object
    mixed: object
    gz: object
    gmh: object
    scaled: object
    gin: object
    gsc: object
    grun: object
    seg: object
    gread: object
    kept: object
    given: object
    given_far: object
    gpre: object
    ga: object
    da: object
    db: object
    branch: object
    part: object
    small: object
    zsmall: object
    dsmall: object
    tsmall: object
    rxa_a: object
    rya_a: object
    ryb_a: object
    rxb_a: object
    ta_a: object
    tb_a: object
    zb_a: object
    zin_a: object
    rxa_b: object
    rya_b: object
    ryb_b: object
    rxb_b: object
    ta_b: object
    tb_b: object
    zb_b: object
    zin_b: object
    sem_load: object
    sem_own: object
    sem_tail: object
    sem_swap: object
    sem_last: object
    sem_carry: object
    sem_zsmall: object
    sem_dsmall: object
    sem_gza: object
    sem_gathera: object
    sem_gzb: object
    sem_gatherb: object
    sem_reducea: object
    sem_rza: object
    sem_reduceb: object
    sem_rzb: object


def half(*shape):
    return pltpu.VMEM(shape, jnp.bfloat16)


def single(*shape):
    return pltpu.VMEM(shape, jnp.float32)


def dma(*shape):
    return pltpu.SemaphoreType.DMA(shape)


def plan(n, seqs, length, width, inner, pick, own, deep):
    rows = seqs * length
    total = seqs * inner
    first, second = inner + pick + LANES, 2 * inner
    return Table(
        gat=single(own, inner),
        val=single(own, inner),
        sel=single(own, pick),
        hid=half(rows, width),
        cot=half(rows, width),
        wa=half(4, n, own, first),
        wb=half(4, n, own, second),
        scale=single(rows, LANES),
        normed=half(rows, width),
        raw=single(seqs, length + 8, inner + pick),
        draw=single(rows, LANES),
        delta=single(rows, LANES),
        run=single(rows, LANES),
        run3=half(rows, 3 * LANES),
        wend=single(rows, LANES),
        runt=single(seqs * 16, length),
        deltat=single(seqs * 16, length),
        gdt=single(LANES, length),
        growth=single(rows, inner),
        ending=single(rows, inner),
        x=half(rows, inner),
        xw=half(rows, inner),
        slope=single(rows, inner + pick),
        mine=half(rows, pick),
        theirs=half(rows, pick),
        bvec=half(rows, pick),
        cvec=half(rows, pick),
        scores=single(rows, length),
        local=single(total, deep),
        decay=single(total, deep),
        enter=half(total, deep),
        leave=half(total, deep),
        gend=half(total, deep),
        gout=half(total, deep),
        mix=half(seqs * (inner // HEADDIM), length, length),
        mixer=single(rows, inner),
        across=single(rows, inner),
        z=half(rows, inner),
        gmix=single(rows, inner),
        sums=single(rows, LANES),
        sums_far=single(rows, LANES),
        mixed=half(rows, inner),
        gz=half(rows, inner),
        gmh=half(rows, inner),
        scaled=half(rows, inner),
        gin=single(rows, inner),
        gsc=single(rows, length),
        grun=single(rows, LANES),
        seg=single(rows, LANES),
        gread=single(rows, pick),
        kept=single(rows, pick),
        given=single(rows, pick),
        given_far=single(rows, pick),
        gpre=single(seqs, length + 8, inner + pick),
        ga=half(rows, first),
        da=half(2, 2, n, own, first),
        db=half(2, 2, n, own, second),
        branch=half(rows, width),
        part=half(rows, width),
        small=single(16, inner + pick),
        zsmall=single(n, 16, inner + pick),
        dsmall=single(5, 16, inner + pick),
        tsmall=single(16, inner + pick),
        rxa_a=half(n, 2, own, first // 2),
        rya_a=half(n, own, first // 2),
        ryb_a=half(n, 2, own, first // 2),
        rxb_a=half(n, own, first // 2),
        ta_a=half(n, own, first // 2),
        tb_a=half(n, own, first // 2),
        zb_a=half(n - 1, own, first),
        zin_a=half(n - 1, own, first),
        rxa_b=half(n, 2, own, second // 2),
        rya_b=half(n, own, second // 2),
        ryb_b=half(n, 2, own, second // 2),
        rxb_b=half(n, own, second // 2),
        ta_b=half(n, own, second // 2),
        tb_b=half(n, own, second // 2),
        zb_b=half(n - 1, own, second),
        zin_b=half(n - 1, own, second),
        sem_load=dma(5),
        sem_own=dma(2),
        sem_tail=dma(4),
        sem_swap=dma(12),
        sem_last=dma(2),
        sem_carry=dma(4, PARTS),
        sem_zsmall=dma(2, n - 1),
        sem_dsmall=dma(2, 3),
        sem_gza=dma(2, n - 1),
        sem_gathera=dma(8, n),
        sem_gzb=dma(2, n - 1),
        sem_gatherb=dma(8, n),
        sem_reducea=dma(8, n),
        sem_rza=dma(2, n - 1),
        sem_reduceb=dma(8, n),
        sem_rzb=dma(2, n - 1),
    )


class Gather:
    def __init__(self, n, block, near, far, place):
        self.n, (d, s, x, y) = n, place
        self.xn, self.yn = y * 2 + (1 - x), (1 - y) * 2 + x
        self.block, self.near, self.far = block, near, far
        self.d = d
        self.zf = [lax.rem(s + n - k, n) for k in range(n)]
        self.h = block.shape[3] // 2
        own = block.at[d, s]
        self.zc = [
            send(own, own, near.at[0, k - 1], near.at[1, k - 1], {"seq": lax.rem(s + k, n)})
            for k in range(1, n)
        ]
        self.xc, self.yc, self.fx, self.fy = [], [], [], []

    def begin(self):
        for copy in self.zc:
            copy.start()
        self.spread(0)

    def spread(self, j):
        if j:
            self.zc[j - 1].wait_recv()
        piece = self.block.at[self.d, self.zf[j]]
        copy = send(piece, piece, self.far.at[0, j], self.far.at[1, j], {"dp": self.xn})
        copy.start()
        self.xc.append(copy)
        copy = send(piece, piece, self.far.at[2, j], self.far.at[3, j], {"dp": self.yn})
        copy.start()
        self.yc.append(copy)

    def forward(self, j):
        z, h = self.zf[j], self.h
        self.xc[j].wait_recv()
        piece = self.block.at[self.xn, z, :, pl.ds(0, h)]
        copy = send(piece, piece, self.far.at[4, j], self.far.at[5, j], {"dp": self.yn})
        copy.start()
        self.fy.append(copy)
        self.yc[j].wait_recv()
        piece = self.block.at[self.yn, z, :, pl.ds(h, h)]
        copy = send(piece, piece, self.far.at[6, j], self.far.at[7, j], {"dp": self.xn})
        copy.start()
        self.fx.append(copy)

    def finish(self):
        for copy in self.fx + self.fy:
            copy.wait_recv()

    def close(self):
        for copy in self.zc + self.xc + self.yc + self.fx + self.fy:
            copy.wait_send()


class Reduce:
    def __init__(self, n, grad, bufs, sems, near, place):
        self.n, (d, s, self.x, self.y) = n, place
        x, y = self.x, self.y
        self.grad, self.sems, self.near = grad, sems, near
        self.rxa, self.rya, self.ryb, self.rxb, self.ta, self.tb, self.zb, self.zin = bufs
        self.xn, self.yn = {"dp": y * 2 + (1 - x)}, {"dp": (1 - y) * 2 + x}
        self.zt = [lax.rem(s + k, n) for k in range(n)]
        h = grad.shape[4] // 2
        self.left, self.right = pl.ds(0, h), pl.ds(h, h)
        self.order = list(range(1, n)) + [0]
        self.a1, self.b1, self.a2, self.b2, self.z1 = {}, {}, {}, {}, {}

    def begin(self):
        sems, x, y = self.sems, self.x, self.y
        for j in self.order:
            z = self.zt[j]
            self.a1[j] = send(
                self.grad.at[:, 1 - x, z, :, self.left],
                self.rxa.at[j], sems.at[0, j], sems.at[1, j], self.xn,
            )
            self.a1[j].start()
            self.b1[j] = send(
                self.grad.at[1 - y, :, z, :, self.right],
                self.ryb.at[j], sems.at[2, j], sems.at[3, j], self.yn,
            )
            self.b1[j].start()

    def middle(self, j):
        sems, x, y, z = self.sems, self.x, self.y, self.zt[j]
        single, half = jnp.float32, jnp.bfloat16
        self.a1[j].wait_recv()
        self.ta[j] = (
            self.grad[1 - y, x, z, :, self.left].astype(single)
            + self.rxa[j, 1 - y].astype(single)
        ).astype(half)
        self.a2[j] = send(
            self.ta.at[j], self.rya.at[j], sems.at[4, j], sems.at[5, j], self.yn
        )
        self.a2[j].start()
        self.b1[j].wait_recv()
        self.tb[j] = (
            self.grad[y, 1 - x, z, :, self.right].astype(single)
            + self.ryb[j, 1 - x].astype(single)
        ).astype(half)
        self.b2[j] = send(
            self.tb.at[j], self.rxb.at[j], sems.at[6, j], sems.at[7, j], self.xn
        )
        self.b2[j].start()

    def join(self, j, out):
        x, y, z = self.x, self.y, self.zt[j]
        single, half = jnp.float32, jnp.bfloat16
        self.a2[j].wait_recv()
        low = (
            self.grad[y, x, z, :, self.left].astype(single)
            + self.rxa[j, y].astype(single)
            + self.rya[j].astype(single)
        )
        self.b2[j].wait_recv()
        high = (
            self.grad[y, x, z, :, self.right].astype(single)
            + self.ryb[j, x].astype(single)
            + self.rxb[j].astype(single)
        )
        if j == 0:
            out[:, self.left] = low
            out[:, self.right] = high
        else:
            self.zb[j - 1, :, self.left] = low.astype(half)
            self.zb[j - 1, :, self.right] = high.astype(half)
            self.z1[j] = send(
                self.zb.at[j - 1], self.zin.at[j - 1],
                self.near.at[0, j - 1], self.near.at[1, j - 1], {"seq": self.zt[j]},
            )
            self.z1[j].start()

    def finish(self, out):
        for j in range(1, self.n):
            self.z1[j].wait_recv()
            out[...] = out[...] + self.zin[j - 1].astype(jnp.float32)

    def close(self):
        for group in (self.a1, self.b1, self.a2, self.b2, self.z1):
            for copy in group.values():
                copy.wait_send()


def main_kernel(n, seqs, length, heads, *refs):
    inputs, refs = refs[:8], refs[8:]
    hid_h, cot_h, gat_h, val_h, sel_h, step_ref, outt_ref, vec_ref = inputs
    outputs, refs = refs[:8], refs[8:]
    suma_o, sumb_o, small_o, gain_o, branch_o, branch_far, part_o, part_far = outputs
    r = Table(*refs)
    half, single = jnp.bfloat16, jnp.float32
    d, s = lax.axis_index("dp"), lax.axis_index("seq")
    core = lax.axis_index("tensor")
    y, x = d // 2, lax.rem(d, 2)
    place = (d, s, x, y)
    rows, width = r.hid.shape
    inner, pick = r.x.shape[1], r.mine.shape[1]
    conv = inner + pick
    pairs = inner // LANES
    deep = r.enter.shape[1]
    other = {"tensor": 1 - core}
    zt = [lax.rem(s + k, n) for k in range(n)]
    others = [{"dp": lax.rem(d + k, 4)} for k in range(1, 4)]
    after, before = {"seq": lax.rem(s + 1, n)}, {"seq": lax.rem(s + n - 1, n)}

    loads = [
        pltpu.make_async_copy(src, dst, r.sem_load.at[i])
        for i, (src, dst) in enumerate(
            [(val_h, r.val), (sel_h, r.sel), (gat_h, r.gat), (hid_h, r.hid), (cot_h, r.cot)]
        )
    ]
    for copy in loads:
        copy.start()
    greet([{"seq": zt[k]} for k in range(1, n)] + others + [other])

    wa, wb = r.wa, r.wb
    loads[0].wait()
    wa[d, s, :, :inner] = r.val[...].astype(half)
    loads[1].wait()
    wa[d, s, :, inner:conv] = r.sel[...].astype(half)
    wa[d, s, :, conv:] = step_ref[...].astype(half)
    ga = Gather(n, wa, r.sem_gza, r.sem_gathera, place)
    gb = Gather(n, wb, r.sem_gzb, r.sem_gatherb, place)
    ga.begin()
    loads[2].wait()
    wb[d, s, :, :inner] = r.gat[...].astype(half)
    wb[d, s, :, inner:] = outt_ref[...]

    loads[3].wait()
    loads[4].wait()
    tile = 32

    def scale_of(at, state):
        wide = r.hid[pl.ds(at, tile), :].astype(single)
        mean = jnp.sum(wide * wide, axis=1, keepdims=True) * (1.0 / width)
        r.scale[pl.ds(at, tile), :] = jnp.broadcast_to(
            lax.rsqrt(mean + epsilon), (tile, LANES)
        )
        return state

    each(rows // tile, tile, scale_of)

    heads_table = (iota((LANES, inner), 1) // HEADDIM == iota((LANES, inner), 0)).astype(half)
    table_heads = (iota((inner, LANES), 0) // HEADDIM == iota((inner, LANES), 1)).astype(half)
    lane = iota((1, LANES), 1)
    real = lane < heads
    bias = vec_ref[8:9, :LANES]
    rate = jnp.where(real, -jnp.exp(vec_ref[9:10, :LANES]), 0.0)
    skip = wide_mul(jnp.broadcast_to(vec_ref[10:11, :LANES], (8, LANES)), heads_table, 3)[0:1]
    post = vec_ref[5:6, :inner]

    for j in range(1, n):
        ga.spread(j)
        ga.forward(j - 1)
    ga.forward(n - 1)
    gb.begin()
    ga.finish()

    step_t = wa[:, :, :, conv:].astype(single).reshape(width, LANES).T
    gain = step_t[heads : heads + 1, :]
    gain_o[...] = jnp.broadcast_to(gain, (8, width))

    def norm_of(at, state):
        wide = r.hid[pl.ds(at, tile), :].astype(single)
        scale = r.scale[pl.ds(at, tile), 0:1]
        r.normed[pl.ds(at, tile), :] = (wide * scale * gain).astype(half)
        return state

    each(rows // tile, tile, norm_of)

    def weight_of(block, at, wide):
        return block[:, :, :, pl.ds(at, wide)].reshape(width, wide)

    tail = mul(r.normed[...], weight_of(wa, inner, 2 * LANES))
    r.draw[...] = jnp.where(real, tail[:, pick:], 0.0)
    for q in range(seqs):
        r.raw[q, 8:, inner:] = (
            tail[q * length : (q + 1) * length, :pick].astype(half).astype(single)
        )

    def raw_of(at, state):
        value = mul(r.normed[...], weight_of(wa, at, 256)).astype(half).astype(single)
        for q in range(seqs):
            r.raw[q, 8:, pl.ds(at, 256)] = value[q * length : (q + 1) * length]
        return state

    each(inner // 256, 256, raw_of)

    tails = send(
        r.raw.at[:, pl.ds(length, 8)], r.raw.at[:, pl.ds(0, 8)],
        r.sem_tail.at[0], r.sem_tail.at[1], after,
    )

    @pl.when(s == 0)
    def _():
        r.raw[:, 0:8] = jnp.zeros((seqs, 8, conv), single)

    @pl.when(s != n - 1)
    def _():
        tails.start()

    gb.spread(1)
    gb.forward(0)

    low = (iota((length, length), 0) >= iota((length, length), 1)).astype(half)
    high = (iota((length, length), 0) <= iota((length, length), 1)).astype(half)
    cdecays = []
    for q in range(seqs):
        span = pl.ds(q * length, length)
        value = r.draw[span, :] + bias
        delta = jnp.maximum(value, 0.0) + jnp.log1p(jnp.exp(-jnp.abs(value)))
        delta = jnp.where(real, delta, 0.0)
        run = table_mul(low, delta * rate, 3)
        last = run[length - 1 : length, :]
        r.delta[span, :] = delta
        r.run[span, :] = run
        for i, piece in enumerate(split(run, 3)):
            r.run3[span, i * LANES : (i + 1) * LANES] = piece
        wend = jnp.exp(last - run) * delta
        r.wend[span, :] = wend
        r.runt[q * 16 : (q + 1) * 16, :] = run.T[:16]
        r.deltat[q * 16 : (q + 1) * 16, :] = delta.T[:16]
        cdecay = jnp.exp(last)
        cdecays.append(cdecay)
        pickrow = iota((inner, LANES), 0) // HEADDIM == iota((inner, LANES), 1)
        column = jnp.sum(jnp.where(pickrow, cdecay, 0.0), axis=1, keepdims=True)
        r.decay[q * inner : (q + 1) * inner, :] = jnp.broadcast_to(column, (inner, deep))
        r.growth[span, :] = wide_mul(jnp.exp(run), heads_table, 2)
        r.ending[span, :] = wide_mul(wend, heads_table, 2)

    @pl.when(s != 0)
    def _():
        tails.wait_recv()

    gb.spread(2)
    gb.forward(1)

    def conv_of(first, wide):
        taps = [vec_ref[k : k + 1, first : first + wide] for k in range(5)]
        for q in range(seqs):

            def one(at, state):
                padded = r.raw[q, pl.ds(at, tile + 8), first : first + wide]
                total = taps[4] + taps[3] * padded[8:]
                for k in range(3):
                    total = total + taps[k] * pltpu.roll(padded, 3 - k, 0)[8:]
                sigmoid = jax.nn.sigmoid(total)
                span = pl.ds(pl.multiple_of(q * length + at, tile), tile)
                act = (total * sigmoid).astype(half)
                if first:
                    r.mine[span, :] = act
                else:
                    r.x[span, :] = act
                    r.xw[span, :] = (act.astype(single) * r.ending[span, :]).astype(half)
                r.slope[span, first : first + wide] = sigmoid * (
                    1.0 + total * (1.0 - sigmoid)
                )
                return state

            each(length // tile, tile, one)

    conv_of(inner, pick)
    swaps = r.sem_swap
    trade = send(r.mine, r.theirs, swaps.at[0], swaps.at[1], other)
    trade.start()
    conv_of(0, inner)
    gb.spread(3)
    gb.forward(2)
    trade.wait_recv()
    mine, theirs = r.mine[...], r.theirs[...]
    r.bvec[...] = jnp.where(core == 0, mine, theirs)
    r.cvec[...] = jnp.where(core == 0, theirs, mine)
    total = seqs * inner
    size = total // PARTS
    for q in range(seqs):
        span = pl.ds(q * length, length)
        r.local[q * inner : (q + 1) * inner, :] = mul_tn(r.xw[span, :], r.bvec[span, :])
        r.scores[span, :] = mul_nt(r.cvec[span, :], r.bvec[span, :])

    def carry_step(part, first, last, came, went, sem, target):
        span = pl.ds(pl.multiple_of(part * size, size), size)
        copy = send(
            went.at[span], came.at[span],
            r.sem_carry.at[sem, part], r.sem_carry.at[sem + 1, part], target,
        )

        @pl.when(s == first)
        def _():
            came[span, :] = jnp.zeros((size, deep), half)
            went[span, :] = r.local[span, :].astype(half)

        @pl.when(s != first)
        def _():
            copy.wait_recv()
            went[span, :] = (
                r.decay[span, :] * came[span, :].astype(single) + r.local[span, :]
            ).astype(half)

        @pl.when(s != last)
        def _():
            copy.start()

    def carry_close(last, came, went, sem, target):
        @pl.when(s != last)
        def _():
            for part in range(PARTS):
                span = pl.ds(part * size, size)
                send(
                    went.at[span], came.at[span],
                    r.sem_carry.at[sem, part], r.sem_carry.at[sem + 1, part], target,
                ).wait_send()

    causal = iota((length, length), 0) >= iota((length, length), 1)
    side = iota((1, LANES), 1) // HEADDIM

    def decays_of(q, h):
        span = pl.ds(pl.multiple_of(q * length, length), length)
        choose = (lax.rem(iota((3 * LANES, LANES), 0), LANES) == h).astype(half)
        column = mul(r.run3[span, :], choose)
        row = r.runt[pl.ds(q * 16 + h, 1), :]
        gap = jnp.concatenate([column] * (length // LANES), axis=1) - row
        return jnp.exp(jnp.where(causal, gap, -1e30))

    def within_of(index, state):
        q, p = index // pairs, lax.rem(index, pairs)
        span = pl.ds(pl.multiple_of(q * length, length), length)
        lanes = pl.ds(pl.multiple_of(p * LANES, LANES), LANES)
        value = r.x[span, lanes]
        scores = r.scores[span, :]
        out = None
        for a in range(2):
            h = 2 * p + a
            step = r.deltat[pl.ds(q * 16 + h, 1), :]
            mixing = (scores * decays_of(q, h) * step).astype(half)
            r.mix[2 * index + a] = mixing
            term = mul(mixing, jnp.where(side == a, value, jnp.zeros_like(value)))
            out = term if out is None else out + term
        r.mixer[span, lanes] = out
        carry_step(index, 0, n - 1, r.enter, r.leave, 0, after)
        return state

    lax.fori_loop(0, seqs * pairs, within_of, 0)
    gb.forward(n - 1)
    gb.finish()

    def gate_of(at, state):
        r.z[:, pl.ds(at, 256)] = mul(r.normed[...], weight_of(wb, at, 256)).astype(half)
        r.gmix[:, pl.ds(at, 256)] = mul(
            r.cot[...], weight_of(wb, pl.multiple_of(inner + at, 256), 256)
        )
        return state

    each(inner // 256, 256, gate_of)

    trades = []
    for q in range(seqs):
        span = pl.ds(q * length, length)
        r.across[span, :] = mul_nt(
            r.cvec[span, :], r.enter[q * inner : (q + 1) * inner, :]
        )

        def mixer_of(at, state):
            span = pl.ds(pl.multiple_of(q * length + at, tile), tile)
            mixer = (
                r.mixer[span, :]
                + r.growth[span, :] * r.across[span, :]
                + skip * r.x[span, :].astype(single)
            )
            r.mixer[span, :] = mixer
            z = r.z[span, :].astype(single)
            gated = mixer * (z * jax.nn.sigmoid(z))
            squares = jnp.sum(gated * gated, axis=1, keepdims=True)
            dots = jnp.sum(r.gmix[span, :] * post * gated, axis=1, keepdims=True)
            r.sums[span, :] = jnp.where(lane == 0, squares, jnp.where(lane == 1, dots, 0.0))
            return state

        each(length // tile, tile, mixer_of)
        copy = send(
            r.sums.at[span], r.sums_far.at[span],
            swaps.at[2 + 2 * q], swaps.at[3 + 2 * q], other,
        )
        copy.start()
        trades.append(copy)

    full = 2 * inner

    def back_of(q):
        def one(at, state):
            span = pl.ds(pl.multiple_of(q * length + at, tile), tile)
            both = r.sums[span, :] + r.sums_far[span, :]
            scale = lax.rsqrt(both[:, 0:1] * (1.0 / full) + epsilon)
            dots = both[:, 1:2] * (1.0 / full)
            mixer, z = r.mixer[span, :], r.z[span, :].astype(single)
            sigmoid = jax.nn.sigmoid(z)
            act, slope = z * sigmoid, sigmoid * (1.0 + z * (1.0 - sigmoid))
            gated = mixer * act
            gmixed = r.gmix[span, :]
            r.mixed[span, :] = (gated * scale * post).astype(half)
            ggated = scale * (gmixed * post) - gated * (scale * scale * scale * dots)
            gmixer = ggated * act
            r.gz[span, :] = (ggated * mixer * slope).astype(half)
            r.gmh[span, :] = gmixer.astype(half)
            scaled = gmixer * r.growth[span, :]
            r.scaled[span, :] = scaled.astype(half)
            r.gmix[span, :] = gmixer
            r.across[span, :] = scaled * r.across[span, :]
            return (
                state[0] + fold(gmixed * gated * scale),
                state[1] + fold(gmixer * r.x[span, :].astype(single)),
            )

        return one

    state = (jnp.zeros((8, inner), single), jnp.zeros((8, inner), single))
    push = []
    for q in range(seqs):
        trades[q].wait_recv()
        state = each(length // tile, tile, back_of(q), state)
        span = pl.ds(q * length, length)
        r.local[q * inner : (q + 1) * inner, :] = mul_tn(r.scaled[span, :], r.cvec[span, :])
    r.small[...] = jnp.zeros(r.small.shape, single)
    r.small[5:6, :inner] = jnp.sum(state[0], axis=0, keepdims=True)
    r.small[10:11, :LANES] = jnp.sum(wide_mul(state[1], table_heads, 3), axis=0, keepdims=True)

    ra = Reduce(
        n, r.da, (r.rxa_a, r.rya_a, r.ryb_a, r.rxb_a, r.ta_a, r.tb_a, r.zb_a, r.zin_a),
        r.sem_reducea, r.sem_rza, place,
    )
    rb = Reduce(
        n, r.db, (r.rxa_b, r.rya_b, r.ryb_b, r.rxb_b, r.ta_b, r.tb_b, r.zb_b, r.zin_b),
        r.sem_reduceb, r.sem_rzb, place,
    )

    span_y = width // 2

    def grad_b(index, state):
        lanes = pl.ds(pl.multiple_of(index * span_y, span_y), span_y)
        own = r.db.shape[3]
        r.db[index, :, :, :, pl.ds(0, inner)] = (
            mul_tn(r.normed[:, lanes], r.gz[...]).astype(half).reshape(2, n, own, inner)
        )
        r.db[index, :, :, :, pl.ds(inner, inner)] = (
            mul_tn(r.cot[:, lanes], r.mixed[...]).astype(half).reshape(2, n, own, inner)
        )
        return state

    lax.fori_loop(0, 2, grad_b, 0)
    rb.begin()

    def branch_of(index, state):
        lanes = pl.ds(pl.multiple_of(index * span_y, span_y), span_y)
        weight = wb[pl.ds(2 * index, 2), :, :, pl.ds(inner, inner)].reshape(span_y, inner)
        r.branch[:, lanes] = mul_nt(r.mixed[...], weight).astype(half)
        return state

    lax.fori_loop(0, 2, branch_of, 0)
    keep = [pltpu.make_async_copy(r.branch, branch_o, r.sem_own.at[0])]
    keep[0].start()
    far = [send(r.branch, branch_far, swaps.at[6], swaps.at[7], other)]
    far[0].start()

    r.gsc[...] = jnp.zeros(r.gsc.shape, single)
    r.grun[...] = jnp.zeros(r.grun.shape, single)
    r.gdt[...] = jnp.zeros(r.gdt.shape, single)

    def intra_of(index, state):
        q, p = index // pairs, lax.rem(index, pairs)
        span = pl.ds(pl.multiple_of(q * length, length), length)
        lanes = pl.ds(pl.multiple_of(p * LANES, LANES), LANES)
        value, upper = r.x[span, lanes], r.gmh[span, lanes]
        scores = r.scores[span, :]
        out = None
        for a in range(2):
            h = 2 * p + a
            step = r.deltat[pl.ds(q * 16 + h, 1), :]
            masked = jnp.where(side == a, upper, jnp.zeros_like(upper))
            spread = mul_nt(masked, value) * decays_of(q, h)
            kernel = spread * scores
            r.gdt[pl.ds(q * 16 + h, 1), :] = jnp.sum(kernel, axis=0, keepdims=True)
            r.gsc[span, :] += spread * step
            weighted = jnp.sum(kernel * step, axis=1, keepdims=True)
            r.grun[span, :] += jnp.where(lane == h, weighted, 0.0)
            term = mul_tn(r.mix[2 * index + a], masked)
            out = term if out is None else out + term
        r.gin[span, lanes] = out
        carry_step(index, n - 1, 0, r.gend, r.gout, 2, before)
        return state

    lax.fori_loop(0, seqs * pairs, intra_of, 0)
    for j in rb.order:
        rb.middle(j)

    gdt = r.gdt[...].T
    bias_row, log_row = jnp.zeros((1, LANES), single), jnp.zeros((1, LANES), single)
    seg = [wide_mul(r.across[pl.ds(q * length, length), :], table_heads, 2) for q in range(seqs)]
    for q in range(seqs):
        span = pl.ds(q * length, length)
        states = pl.ds(q * inner, inner)
        r.across[span, :] = mul_nt(r.bvec[span, :], r.gend[states, :])
        r.gread[span, :] = mul(r.scaled[span, :], r.enter[states, :])
        gsc = r.gsc[span, :].astype(half)
        gread = r.gread[span, :] + mul(gsc, r.bvec[span, :])
        gwrite = mul_tn(gsc, r.cvec[span, :]) + mul(r.xw[span, :], r.gend[states, :])
        r.kept[span, :] = jnp.where(core == 0, gwrite, gread)
        r.given[span, :] = jnp.where(core == 0, gread, gwrite)
    trade2 = send(r.given, r.given_far, swaps.at[8], swaps.at[9], other)
    trade2.start()

    def inner_of(at, state):
        span = pl.ds(at, tile)
        back = r.across[span, :]
        total = (
            r.gin[span, :] + skip * r.gmix[span, :] + back * r.ending[span, :]
        )
        r.gin[span, :] = total
        r.across[span, :] = back * r.x[span, :].astype(single)
        return state

    each(rows // tile, tile, inner_of)

    for q in range(seqs):
        span = pl.ds(q * length, length)
        states = pl.ds(q * inner, inner)
        weight = wide_mul(r.across[span, :], table_heads, 2)
        product = r.gend[states, :].astype(single) * r.enter[states, :].astype(single)
        ones = jnp.ones((8, deep), half)
        across = sum(mul_nt(ones, piece) for piece in split(product, 2))
        end_row = wide_mul(across, table_heads, 3)[0:1] * cdecays[q]
        delta, run, wend = r.delta[span, :], r.run[span, :], r.wend[span, :]
        gdelta = jnp.where(
            lane < heads, pltpu.roll(gdt, LANES - 16 * q, 1) if q else gdt, 0.0
        )
        grun = r.grun[span, :] - delta * gdelta + seg[q]
        last = run[length - 1 : length, :]
        gdelta = gdelta + weight * jnp.exp(last - run)
        spread = weight * wend
        end_row = end_row + jnp.sum(spread, axis=0, keepdims=True)
        grun = grun - spread + jnp.where(iota((length, 1), 0) == length - 1, end_row, 0.0)
        glog = table_mul(high, grun, 3)
        gdelta = gdelta + glog * rate
        log_row = log_row + jnp.sum(glog * delta, axis=0, keepdims=True) * rate
        gdraw = jnp.where(real, gdelta * jax.nn.sigmoid(r.draw[span, :] + bias), 0.0)
        bias_row = bias_row + jnp.sum(gdraw, axis=0, keepdims=True)
        r.ga[span, conv:] = gdraw.astype(half)
    r.small[8:9, :LANES] = bias_row
    r.small[9:10, :LANES] = log_row

    for j in rb.order:
        rb.join(j, sumb_o)

    trade2.wait_recv()
    for q in range(seqs):

        def pre_of(at, state):
            span = pl.ds(pl.multiple_of(q * length + at, tile), tile)
            r.gpre[q, pl.ds(at, tile), :inner] = r.gin[span, :] * r.slope[span, :inner]
            r.gpre[q, pl.ds(at, tile), inner:] = (
                r.kept[span, :] + r.given_far[span, :]
            ) * r.slope[span, inner:]
            return state

        each(length // tile, tile, pre_of)

    tails2 = send(
        r.gpre.at[:, pl.ds(0, 8)], r.gpre.at[:, pl.ds(length, 8)],
        r.sem_tail.at[2], r.sem_tail.at[3], before,
    )

    @pl.when(s == n - 1)
    def _():
        r.gpre[:, length:] = jnp.zeros((seqs, 8, conv), single)

    @pl.when(s != 0)
    def _():
        tails2.start()

    taps_sum = tuple(jnp.zeros((8, conv), single) for _ in range(5))
    for q in range(seqs):

        def taps_of(at, state):
            pre = r.gpre[q, pl.ds(at, tile), :]
            padded = r.raw[q, pl.ds(at, tile + 8), :]
            terms = [pre * pltpu.roll(padded, 3 - k, 0)[8:] for k in range(3)]
            terms += [pre * padded[8:], pre]
            return tuple(total + fold(term) for total, term in zip(state, terms))

        taps_sum = each(length // tile, tile, taps_of, taps_sum)
    for k in range(5):
        r.small[k : k + 1, :] = jnp.sum(taps_sum[k], axis=0, keepdims=True)

    @pl.when(s != n - 1)
    def _():
        tails2.wait_recv()

    taps = [vec_ref[k : k + 1, :] for k in range(4)]
    for q in range(seqs):

        def raw_grad(at, state):
            padded = r.gpre[q, pl.ds(at, tile + 8), :]
            total = taps[3] * padded[:tile]
            for k in range(3):
                total = total + taps[k] * pltpu.roll(padded, tile + 8 - (3 - k), 0)[:tile]
            span = pl.ds(pl.multiple_of(q * length + at, tile), tile)
            r.ga[span, :conv] = total.astype(half)
            return state

        each(length // tile, tile, raw_grad)

    def grad_a(index, state):
        lanes = pl.ds(pl.multiple_of(index * span_y, span_y), span_y)
        own, wide = r.da.shape[3:]
        r.da[index] = (
            mul_tn(r.normed[:, lanes], r.ga[...]).astype(half).reshape(2, n, own, wide)
        )
        return state

    lax.fori_loop(0, 2, grad_a, 0)
    ra.begin()

    def part_of(index, state):
        lanes = pl.ds(pl.multiple_of(index * span_y, span_y), span_y)
        block = pl.ds(2 * index, 2)
        gate = wb[block, :, :, pl.ds(0, inner)].reshape(span_y, inner)
        value = wa[block].reshape(span_y, wa.shape[3])
        r.part[:, lanes] = (mul_nt(r.gz[...], gate) + mul_nt(r.ga[...], value)).astype(half)
        return state

    lax.fori_loop(0, 2, part_of, 0)
    keep.append(pltpu.make_async_copy(r.part, part_o, r.sem_own.at[1]))
    keep[1].start()
    far.append(send(r.part, part_far, swaps.at[10], swaps.at[11], other))
    far[1].start()

    def gain_of(at, state):
        span = pl.ds(at, tile)
        term = (
            r.part[span, :].astype(single)
            * r.hid[span, :].astype(single)
            * r.scale[span, 0:1]
        )
        return state + fold(term)

    gain_sum = each(rows // tile, tile, gain_of, jnp.zeros((8, width), single))
    r.small[6:7, :width] = jnp.sum(gain_sum, axis=0, keepdims=True)

    smalls = []
    for k in range(1, n):
        copy = send(
            r.small, r.zsmall.at[s],
            r.sem_zsmall.at[0, k - 1], r.sem_zsmall.at[1, k - 1], {"seq": zt[k]},
        )
        copy.start()
        smalls.append(copy)
    r.zsmall[s] = r.small[...]
    rb.finish(sumb_o)
    for copy in smalls:
        copy.wait_recv()
    total_small = r.zsmall[0]
    for k in range(1, n):
        total_small = total_small + r.zsmall[k]
    r.dsmall[d] = total_small
    widely = []
    for k in range(3):
        copy = send(
            r.dsmall.at[d], r.dsmall.at[d],
            r.sem_dsmall.at[0, k], r.sem_dsmall.at[1, k], others[k],
        )
        copy.start()
        widely.append(copy)
    for place_, j in enumerate(ra.order):
        ra.middle(j)
        if place_:
            ra.join(ra.order[place_ - 1], suma_o)
    ra.join(0, suma_o)
    for copy in widely:
        copy.wait_recv()
    total_small = r.dsmall[0] + r.dsmall[1] + r.dsmall[2] + r.dsmall[3]
    r.dsmall[4] = total_small
    last_trade = send(r.dsmall.at[4], r.tsmall, r.sem_last.at[0], r.sem_last.at[1], other)
    last_trade.start()
    ra.finish(suma_o)
    last_trade.wait()
    small_o[...] = total_small
    small_o[6:7, :] = r.dsmall[4, 6:7, :] + r.tsmall[6:7, :]

    ga.close()
    gb.close()
    ra.close()
    rb.close()
    carry_close(n - 1, r.enter, r.leave, 0, after)
    carry_close(0, r.gend, r.gout, 2, before)

    @pl.when(s != n - 1)
    def _():
        tails.wait_send()

    @pl.when(s != 0)
    def _():
        tails2.wait_send()

    for copy in [trade, trade2] + trades:
        copy.wait_send()
    for copy in keep:
        copy.wait()
    for copy in far:
        copy.wait()
    for copy in smalls + widely:
        copy.wait_send()


def finish_kernel(
    heads, hid, cot, gain, branch, branch_far, part, part_far, suma, sumb,
    gat, val, sel, stp, out, gat_m, val_m, sel_m, stp_m, out_m,
    result, hidden_grad, gat_g, val_g, sel_g, stp_g, out_g,
    gat_n, val_n, sel_n, stp_n, out_n, gat_s, val_s, sel_s, stp_s, out_s,
):
    single = jnp.float32
    rows, width = hid.shape
    inner, pick = gat.shape[1], sel.shape[1]
    tile = 32

    def one(at, state):
        span = pl.ds(at, tile)
        wide = hid[span, :].astype(single)
        result[span, :] = (
            wide + branch[span, :].astype(single) + branch_far[span, :].astype(single)
        )
        mean = jnp.sum(wide * wide, axis=1, keepdims=True) * (1.0 / width)
        scale = lax.rsqrt(mean + epsilon)
        hat = (part[span, :].astype(single) + part_far[span, :].astype(single)) * gain[0:1, :]
        dots = jnp.sum(hat * wide, axis=1, keepdims=True) * (1.0 / width)
        hidden_grad[span, :] = (
            cot[span, :].astype(single) + scale * hat - wide * (scale * scale * scale * dots)
        )
        return state

    each(rows // tile, tile, one)

    def update(grad, param, moments, grad_o, next_o, state_o):
        grad_o[...] = grad
        fresh, first, second = step_of(param[...], moments[0], moments[1], grad)
        next_o[...] = fresh
        state_o[0] = first
        state_o[1] = second

    own = gat.shape[0]
    update(sumb[:, :inner], gat, gat_m, gat_g, gat_n, gat_s)
    update(suma[:, :inner], val, val_m, val_g, val_n, val_s)
    update(suma[:, inner : inner + pick], sel, sel_m, sel_g, sel_n, sel_s)
    update(suma[:, inner + pick : inner + pick + heads], stp, stp_m, stp_g, stp_n, stp_s)
    tall = jnp.concatenate(
        [sumb[:, inner:], jnp.zeros((LANES - own, inner), single)], axis=0
    ).T[:, :own]
    update(tall, out, out_m, out_g, out_n, out_s)


def step_of(param, first, second, grad):
    first = first_decay * first + (1.0 - first_decay) * grad
    second = second_decay * second + (1.0 - second_decay) * grad * grad
    first_hat = first / (1.0 - first_decay**STEP)
    second_hat = second / (1.0 - second_decay**STEP)
    fresh = param - learn_rate * (
        first_hat / (jnp.sqrt(second_hat) + adam_epsilon) + weight_decay * param
    )
    return fresh, first, second


def fast(
    hidden, cotangent, gating, values, selector, timestep, output, prenorm, postnorm,
    filters, kernels, scalars, gating_adam, values_adam, selector_adam, timestep_adam,
    output_adam, prenorm_adam, postnorm_adam, filters_adam, kernels_adam, scalars_adam,
):
    half, single = jnp.bfloat16, jnp.float32
    n = lax.axis_size("seq")
    seqs, length, width = hidden.shape
    rows = seqs * length
    own, inner = gating.shape
    pick, heads = selector.shape[1], timestep.shape[1]
    conv = inner + pick
    step_own = jnp.concatenate(
        [timestep, prenorm[:, None], jnp.zeros((own, LANES - heads - 1), single)], axis=1
    )
    vec = jnp.concatenate(
        [
            jnp.concatenate([filters, kernels], axis=1),
            jnp.pad(postnorm, (0, pick))[None],
            jnp.zeros((2, conv), single),
            jnp.pad(scalars, ((0, 5), (0, conv - heads))),
        ],
        axis=0,
    )
    scratch = plan(n, seqs, length, width, inner, pick, own, STATE)
    hid, cot = hidden.reshape(rows, width), cotangent.reshape(rows, width)
    shape = jax.ShapeDtypeStruct
    token = shape((rows, width), half)
    suma, sumb, small, gain, branch, branch_far, part, part_far = pl.pallas_call(
        functools.partial(main_kernel, n, seqs, length, heads),
        out_shape=(
            shape((own, conv + LANES), single),
            shape((own, 2 * inner), single),
            shape((16, conv), single),
            shape((8, width), single),
            token,
            token,
            token,
            token,
        ),
        in_specs=[ANY] * 5 + [VMEM] * 3,
        out_specs=(VMEM,) * 4 + (ANY,) * 4,
        scratch_shapes=list(scratch),
        compiler_params=pltpu.CompilerParams(
            collective_id=0, has_side_effects=True, vmem_limit_bytes=VMEM_BYTES
        ),
    )(hid, cot, gating, values, selector, step_own, output.T.astype(half), vec)

    weights = (gating, values, selector, timestep, output)
    moments = (gating_adam, values_adam, selector_adam, timestep_adam, output_adam)
    done = pl.pallas_call(
        functools.partial(finish_kernel, heads),
        out_shape=(shape((rows, width), single),) * 2
        + tuple(shape(w.shape, single) for w in weights) * 2
        + tuple(shape(m.shape, single) for m in moments),
        in_specs=[VMEM] * 19,
        out_specs=(VMEM,) * 17,
        compiler_params=pltpu.CompilerParams(vmem_limit_bytes=VMEM_BYTES),
    )(hid, cot, gain, branch, branch_far, part, part_far, suma, sumb, *weights, *moments)
    result, hidden_grad = (value.reshape(hidden.shape) for value in done[:2])

    at = lax.axis_index("dp") * n + lax.axis_index("seq")
    grads = (
        lax.dynamic_slice_in_dim(small[6, :width], at * own, own),
        small[5, :inner],
        small[:5, :inner],
        small[:5, inner:conv],
        small[8:11, :heads],
    )
    params = (prenorm, postnorm, filters, kernels, scalars)
    moments = (prenorm_adam, postnorm_adam, filters_adam, kernels_adam, scalars_adam)
    updated = [adamw(param, moment, grad) for param, moment, grad in zip(params, moments, grads)]
    return (
        (result, hidden_grad)
        + tuple(done[2:7])
        + grads
        + tuple(done[7:12])
        + tuple(pair[0] for pair in updated)
        + tuple(done[12:17])
        + tuple(pair[1] for pair in updated)
    )


def shards(*arrays):
    if (lax.axis_size("dp"), lax.axis_size("seq")) == (4, 4):
        return fast(*arrays)
    return general(*arrays)


def solution(mesh):
    placed = (
        P("dp", "seq", None),
        P("dp", "seq", None),
        P(("dp", "seq"), "tensor"),
        P(("dp", "seq"), "tensor"),
        P(("dp", "seq"), "tensor"),
        P(("dp", "seq"), "tensor"),
        P("tensor", ("dp", "seq")),
        P(("dp", "seq")),
        P("tensor"),
        P(None, "tensor"),
        P(None, "tensor"),
        P(None, "tensor"),
        P(None, ("dp", "seq"), "tensor"),
        P(None, ("dp", "seq"), "tensor"),
        P(None, ("dp", "seq"), "tensor"),
        P(None, ("dp", "seq"), "tensor"),
        P(None, "tensor", ("dp", "seq")),
        P(None, ("dp", "seq")),
        P(None, "tensor"),
        P(None, None, "tensor"),
        P(None, None, "tensor"),
        P(None, None, "tensor"),
    )
    return jax.shard_map(
        shards,
        mesh=mesh,
        in_specs=placed,
        out_specs=(
            P("dp", "seq", None),
            P("dp", "seq", None),
            P(("dp", "seq"), "tensor"),
            P(("dp", "seq"), "tensor"),
            P(("dp", "seq"), "tensor"),
            P(("dp", "seq"), "tensor"),
            P("tensor", ("dp", "seq")),
            P(("dp", "seq")),
            P("tensor"),
            P(None, "tensor"),
            P(None, "tensor"),
            P(None, "tensor"),
            P(("dp", "seq"), "tensor"),
            P(("dp", "seq"), "tensor"),
            P(("dp", "seq"), "tensor"),
            P(("dp", "seq"), "tensor"),
            P("tensor", ("dp", "seq")),
            P(("dp", "seq")),
            P("tensor"),
            P(None, "tensor"),
            P(None, "tensor"),
            P(None, "tensor"),
            P(None, ("dp", "seq"), "tensor"),
            P(None, ("dp", "seq"), "tensor"),
            P(None, ("dp", "seq"), "tensor"),
            P(None, ("dp", "seq"), "tensor"),
            P(None, "tensor", ("dp", "seq")),
            P(None, ("dp", "seq")),
            P(None, "tensor"),
            P(None, None, "tensor"),
            P(None, None, "tensor"),
            P(None, None, "tensor"),
        ),
        check_vma=False,
    )
```

```python
import functools
from typing import NamedTuple
import jax
import jax.numpy as jnp
from jax import lax
from jax.experimental import pallas as pl
from jax.experimental.pallas import tpu as pltpu
from jax.sharding import PartitionSpec as P

INNER = 1536
STATE = 128
HEADDIM = 64
STEP = 2


epsilon = 1e-05
highest = lax.Precision.HIGHEST
learn_rate = 0.01
first_decay = 0.9
second_decay = 0.999
adam_epsilon = 1e-08
weight_decay = 0.1


def from_behind(block, axis, distance):
    devices = range(lax.axis_size(axis))
    route = [(i - distance, i) for i in devices if i - distance in devices]
    return lax.ppermute(block, axis, route)


MESH = pl.DeviceIdType.MESH
VMEM = pl.BlockSpec(memory_space=pltpu.VMEM)
ANY = pl.BlockSpec(memory_space=pl.ANY)
LANES = 128
PARTS = 12
VMEM_BYTES = 60 * 2**20


def send(src, dst, send_sem, recv_sem, device):
    return pltpu.make_async_remote_copy(
        src_ref=src,
        dst_ref=dst,
        send_sem=send_sem,
        recv_sem=recv_sem,
        device_id=device,
        device_id_type=MESH,
    )


def greet(devices):
    barrier = pltpu.get_barrier_semaphore()
    for device in devices:
        pl.semaphore_signal(barrier, inc=1, device_id=device, device_id_type=MESH)
    pl.semaphore_wait(barrier, len(devices))


def params_of(collective_id):
    return pltpu.CompilerParams(collective_id=collective_id, has_side_effects=True)


def swap_kernel(x_ref, o_ref, send_sem, recv_sem):
    other = {"tensor": 1 - lax.axis_index("tensor")}
    greet([other])
    copy = send(x_ref, o_ref, send_sem, recv_sem, other)
    copy.start()
    copy.wait()


def swap(value, collective_id):
    return pl.pallas_call(
        swap_kernel,
        out_shape=jax.ShapeDtypeStruct(value.shape, value.dtype),
        in_specs=[VMEM],
        out_specs=VMEM,
        scratch_shapes=[pltpu.SemaphoreType.DMA, pltpu.SemaphoreType.DMA],
        compiler_params=params_of(collective_id),
    )(value)


def carry_kernel(count, step, parts, decay_ref, local_ref, o_ref, out_buf, in_buf, send_sem, recv_sem):
    me = lax.axis_index("seq")
    target = lax.rem(me + count + step, count)
    source = lax.rem(me + count - step, count)
    first, last = (0, count - 1) if step > 0 else (count - 1, 0)
    greet([{"seq": target}, {"seq": source}])
    size = local_ref.shape[0] // parts

    def copy_of(part):
        return send(
            out_buf.at[part],
            in_buf.at[part],
            send_sem.at[part],
            recv_sem.at[part],
            {"seq": target},
        )

    for part in range(parts):
        rows = pl.ds(part * size, size)

        @pl.when(me == first)
        def _():
            o_ref[rows] = jnp.zeros((size,) + o_ref.shape[1:], o_ref.dtype)
            out_buf[part] = local_ref[rows].astype(jnp.bfloat16)

        @pl.when(me != first)
        def _():
            copy_of(part).wait_recv()
            entering = in_buf[part]
            o_ref[rows] = entering
            out_buf[part] = (
                decay_ref[rows] * entering.astype(jnp.float32) + local_ref[rows]
            ).astype(jnp.bfloat16)

        @pl.when(me != last)
        def _():
            copy_of(part).start()

    @pl.when(me != last)
    def _():
        for part in range(parts):
            copy_of(part).wait_send()


def carry(decay, local, count, step, collective_id):
    seqs, heads, wide, deep = local.shape
    total = seqs * heads
    parts = 6 if total % 6 == 0 else 1
    size = total // parts
    spread = jnp.broadcast_to(decay.reshape(total, 1, 1), (total, 1, deep))
    result = pl.pallas_call(
        functools.partial(carry_kernel, count, step, parts),
        out_shape=jax.ShapeDtypeStruct((total, wide, deep), jnp.bfloat16),
        in_specs=[VMEM, VMEM],
        out_specs=VMEM,
        scratch_shapes=[
            pltpu.VMEM((parts, size, wide, deep), jnp.bfloat16),
            pltpu.VMEM((parts, size, wide, deep), jnp.bfloat16),
            pltpu.SemaphoreType.DMA((parts,)),
            pltpu.SemaphoreType.DMA((parts,)),
        ],
        compiler_params=params_of(collective_id),
    )(spread, local.reshape(total, wide, deep))
    return result.reshape(local.shape)


def swish_parts(value):
    sigmoid = jax.nn.sigmoid(value)
    return (value * sigmoid, sigmoid * (1.0 + value * (1.0 - sigmoid)))


def conv_apply(padded, taps):
    tap_count = taps.shape[0] - 1
    length = padded.shape[1] - tap_count + 1
    wide = padded.astype(jnp.float32)
    total = taps[tap_count] + taps[0] * wide[:, 0:length]
    for index in range(1, tap_count):
        total = total + taps[index] * wide[:, index : index + length]
    return total


def conv_back(padded, taps, grad_pre):
    tap_count = taps.shape[0] - 1
    length = grad_pre.shape[1]
    wide = padded.astype(jnp.float32)
    tap_rows = [
        jnp.sum(grad_pre * wide[:, index : index + length], axis=(0, 1))
        for index in range(tap_count)
    ]
    tap_rows.append(jnp.sum(grad_pre, axis=(0, 1)))
    grad_pad = jnp.zeros(padded.shape, jnp.float32)
    for index in range(tap_count):
        grad_pad = grad_pad + jnp.pad(
            taps[index] * grad_pre, ((0, 0), (index, tap_count - 1 - index), (0, 0))
        )
    return (jnp.stack(tap_rows), grad_pad)


def adamw(param, moments, grad):
    first = first_decay * moments[0] + (1.0 - first_decay) * grad
    second = second_decay * moments[1] + (1.0 - second_decay) * grad * grad
    first_hat = first / (1.0 - first_decay**STEP)
    second_hat = second / (1.0 - second_decay**STEP)
    fresh = param - learn_rate * (
        first_hat / (jnp.sqrt(second_hat) + adam_epsilon) + weight_decay * param
    )
    return (fresh, jnp.stack([first, second]))


def general(
    hidden,
    cotangent,
    gating,
    values,
    selector,
    timestep,
    output,
    prenorm,
    postnorm,
    filters,
    kernels,
    scalars,
    gating_adam,
    values_adam,
    selector_adam,
    timestep_adam,
    output_adam,
    prenorm_adam,
    postnorm_adam,
    filters_adam,
    kernels_adam,
    scalars_adam,
):
    half = jnp.bfloat16
    single = jnp.float32
    n_seq = lax.axis_size("seq")
    core = lax.axis_index("tensor")
    seqs_dev, length, width = hidden.shape
    rows = seqs_dev * length
    own_rows = gating.shape[0]
    lead = filters.shape[0] - 2
    heads_here = timestep.shape[1]
    inner_here = gating.shape[1]
    select_here = selector.shape[1]
    conv_end = 2 * inner_here + select_here
    step_wide = 128
    in_wide = conv_end + step_wide
    packed = jnp.concatenate(
        [
            gating.astype(half),
            values.astype(half),
            selector.astype(half),
            timestep.astype(half),
            prenorm.astype(half)[:, None],
            jnp.zeros((own_rows, step_wide - heads_here - 1), half),
            output.T.astype(half),
        ],
        axis=1,
    )
    weights = lax.all_gather(packed, ("dp", "seq"), axis=0, tiled=True)
    in_weight = weights[:, :in_wide]
    out_weight = weights[:, in_wide:]
    bias = scalars[0]
    rate = -jnp.exp(scalars[1])
    skip = scalars[2]
    entry_gain = weights[:, conv_end + heads_here].astype(single)
    residual = hidden.astype(single)
    entry_scale = lax.rsqrt(jnp.mean(residual * residual, axis=-1, keepdims=True) + epsilon)
    normed = (residual * entry_scale * entry_gain).astype(half)
    flat = normed.reshape(rows, width)
    raw = jnp.dot(flat, in_weight, preferred_element_type=single)
    gate_raw = raw[:, :inner_here].astype(half).reshape(seqs_dev, length, inner_here)
    conv_raw = raw[:, inner_here:conv_end].astype(half).reshape(seqs_dev, length, -1)
    delta_raw = raw[:, conv_end : conv_end + heads_here].reshape(seqs_dev, length, heads_here)
    tails = from_behind(conv_raw[:, length - lead :], "seq", 1)
    conv_pad = jnp.concatenate([tails, conv_raw], axis=1)
    taps = jnp.concatenate([filters, kernels], axis=1)
    conv_value, conv_slope = swish_parts(conv_apply(conv_pad, taps))
    conv_act = conv_value.astype(half)
    inner_act = conv_act[:, :, :inner_here]
    mine = conv_act[:, :, inner_here:]
    theirs = swap(mine.reshape(rows, select_here), 1).reshape(mine.shape)
    write_vec = jnp.where(core == 0, mine, theirs)
    read_vec = jnp.where(core == 0, theirs, mine)
    delta = jax.nn.softplus(delta_raw + bias)
    lower = jnp.tril(jnp.ones((length, length), single))
    running = jnp.einsum("tu,buh->bth", lower, delta * rate, precision=highest)
    inner_h = inner_act.reshape(seqs_dev, length, heads_here, HEADDIM)
    inner_f = inner_h.astype(single)
    weight_end = jnp.exp(running[:, -1:, :] - running) * delta
    carry_decay = jnp.exp(running[:, -1, :])
    growth = jnp.exp(running)
    inner_w = (inner_f * weight_end[..., None]).astype(half)
    local_state = jnp.einsum("bthp,btn->bhpn", inner_w, write_vec, preferred_element_type=single)
    entering = carry(carry_decay, local_state, n_seq, 1, 7)
    scores = jnp.einsum("btn,bun->btu", read_vec, write_vec, preferred_element_type=single)
    causal = jnp.arange(length)[:, None] >= jnp.arange(length)[None, :]
    by_head = jnp.transpose(running, (0, 2, 1))
    gap = by_head[:, :, :, None] - by_head[:, :, None, :]
    decays = jnp.exp(jnp.where(causal, gap, -jnp.inf))
    step_head = jnp.transpose(delta, (0, 2, 1))
    mixing_b = (scores[:, None] * decays * step_head[:, :, None, :]).astype(half)
    within = jnp.einsum("bhtu,buhp->bthp", mixing_b, inner_h, preferred_element_type=single)
    across = jnp.einsum("btn,bhpn->bthp", read_vec, entering, preferred_element_type=single)
    mixer_out = (within + growth[..., None] * across + skip[None, None, :, None] * inner_f).reshape(
        seqs_dev, length, inner_here
    )
    gate_act, gate_slope = swish_parts(gate_raw.astype(single))
    gated = mixer_out * gate_act
    upstream = cotangent.reshape(rows, width)
    grad_mixed = jnp.dot(upstream, out_weight, preferred_element_type=single).reshape(
        seqs_dev, length, inner_here
    )
    hat_gated = grad_mixed * postnorm
    sums = jnp.stack([jnp.sum(gated * gated, axis=-1), jnp.sum(hat_gated * gated, axis=-1)])
    lanes = sums.reshape(-1, 128)
    sums = (lanes + swap(lanes, 2)).reshape(sums.shape)
    squares, dots = sums[0], sums[1]
    gate_scale = lax.rsqrt(squares / INNER + epsilon)[..., None]
    mixed_flat = (gated * gate_scale * postnorm).astype(half).reshape(rows, inner_here)
    branch = lax.dot_general(
        mixed_flat, out_weight, (((1,), (1,)), ((), ())), preferred_element_type=single
    ).astype(half)
    output_grad = lax.dot_general(
        upstream, mixed_flat, (((0,), (0,)), ((), ())), preferred_element_type=single
    )
    postnorm_grad = jnp.sum(grad_mixed * gated * gate_scale, axis=(0, 1))
    cube = gate_scale * gate_scale * gate_scale
    grad_gated = gate_scale * hat_gated - gated * cube * (dots / INNER)[..., None]
    grad_mixer = (grad_gated * gate_act).reshape(seqs_dev, length, heads_here, HEADDIM)
    grad_gate = (grad_gated * mixer_out * gate_slope).astype(half).reshape(rows, inner_here)

    scaled = (grad_mixer * growth[..., None]).astype(half)
    pushed = jnp.einsum("bthp,btn->bhpn", scaled, read_vec, preferred_element_type=single)
    end_grad = carry(carry_decay, pushed, n_seq, -1, 8)

    grad_half = grad_mixer.astype(half)
    skip_grad = jnp.sum(grad_mixer * inner_f, axis=(0, 1, 3))
    grad_inner = skip[None, None, :, None] * grad_mixer + jnp.einsum(
        "bhtu,bthp->buhp", mixing_b, grad_half, preferred_element_type=single
    )
    grad_mix = jnp.einsum("bthp,buhp->bhtu", grad_half, inner_h, preferred_element_type=single)
    spread_mix = grad_mix * decays
    kernel = spread_mix * scores[:, None]
    grad_delta = jnp.transpose(jnp.sum(kernel, axis=2), (0, 2, 1))
    weighted = kernel * step_head[:, :, None, :]
    grad_running = jnp.transpose(jnp.sum(weighted, axis=3) - jnp.sum(weighted, axis=2), (0, 2, 1))
    grad_scores = jnp.sum(spread_mix * step_head[:, :, None, :], axis=1).astype(half)
    grad_read = jnp.einsum("btu,bun->btn", grad_scores, write_vec, preferred_element_type=single)
    grad_write = jnp.einsum("btu,btn->bun", grad_scores, read_vec, preferred_element_type=single)
    grad_running = grad_running + jnp.sum(grad_mixer * across, axis=3) * growth
    grad_read = grad_read + jnp.einsum(
        "bthp,bhpn->btn", scaled, entering, preferred_element_type=single
    )

    decay_grad = jnp.sum(end_grad.astype(single) * entering.astype(single), axis=(2, 3))
    end_extra = decay_grad * carry_decay
    grad_xw = jnp.einsum("bhpn,btn->bthp", end_grad, write_vec, preferred_element_type=single)
    grad_write = grad_write + jnp.einsum(
        "bhpn,bthp->btn", end_grad, inner_w, preferred_element_type=single
    )
    grad_inner = grad_inner + grad_xw * weight_end[..., None]
    grad_weight = jnp.sum(grad_xw * inner_f, axis=3)
    grad_delta = grad_delta + grad_weight * jnp.exp(running[:, -1:, :] - running)
    spread = grad_weight * weight_end
    end_extra = end_extra + jnp.sum(spread, axis=1)
    grad_running = grad_running - spread
    grad_running = jnp.concatenate(
        [grad_running[:, :-1], grad_running[:, -1:] + end_extra[:, None]], axis=1
    )
    grad_log = jnp.einsum("tu,bth->buh", lower, grad_running, precision=highest)

    grad_delta = grad_delta + grad_log * rate
    alog_grad = jnp.sum(grad_log * delta, axis=(0, 1)) * rate
    grad_delta_pre = grad_delta * jax.nn.sigmoid(delta_raw + bias)
    bias_grad = jnp.sum(grad_delta_pre, axis=(0, 1))
    kept = jnp.where(core == 0, grad_write, grad_read)
    given = jnp.where(core == 0, grad_read, grad_write)
    grad_select = kept + swap(given.reshape(rows, select_here), 4).reshape(kept.shape)
    grad_conv = jnp.concatenate(
        [grad_inner.reshape(seqs_dev, length, inner_here), grad_select], axis=2
    )
    taps_grad, conv_pad_grad = conv_back(conv_pad, taps, grad_conv * conv_slope)
    back = from_behind(conv_pad_grad[:, :lead], "seq", -1)
    conv_raw_grad = (
        jnp.concatenate(
            [conv_pad_grad[:, lead:length], conv_pad_grad[:, length:] + back], axis=1
        )
        .astype(half)
        .reshape(rows, -1)
    )
    grad_all = jnp.concatenate(
        [
            grad_gate,
            conv_raw_grad,
            grad_delta_pre.astype(half).reshape(rows, heads_here),
            jnp.zeros((rows, step_wide - heads_here), half),
        ],
        axis=1,
    )
    grad_part = lax.dot_general(
        grad_all, in_weight, (((1,), (1,)), ((), ())), preferred_element_type=single
    ).astype(half)
    in_grad = lax.dot_general(
        flat, grad_all, (((0,), (0,)), ((), ())), preferred_element_type=single
    )
    prenorm_part = jnp.sum(
        grad_part.astype(single).reshape(seqs_dev, length, width) * residual * entry_scale,
        axis=(0, 1),
    )
    gain_column = conv_end + heads_here
    packed_grad = jnp.concatenate(
        [
            in_grad.astype(half),
            output_grad.astype(half),
        ],
        axis=1,
    )
    tap_rows = filters.shape[0]
    scalars_local = jnp.stack([bias_grad, alog_grad, skip_grad])
    loose = jnp.concatenate([taps_grad[:, inner_here:].reshape(-1), scalars_local.reshape(-1)])
    small = jnp.concatenate(
        [
            taps_grad[:, :inner_here],
            postnorm_grad[None],
            jnp.pad(loose, (0, inner_here - loose.shape[0]))[None],
            prenorm_part[None],
        ],
        axis=0,
    )
    summed = lax.psum_scatter(
        packed_grad.astype(single), ("dp", "seq"), scatter_dimension=0, tiled=True
    )
    small = lax.psum(small, ("dp", "seq"))
    prenorm_grad = lax.psum(small[-1], "tensor")
    branch_far, part_far = swap(branch, 3), swap(grad_part, 5)
    own = lax.axis_index("dp") * n_seq + lax.axis_index("seq")
    prenorm_grad = lax.dynamic_slice_in_dim(prenorm_grad, own * own_rows, own_rows)
    branch = branch.astype(single) + branch_far.astype(single)
    result = residual + branch.reshape(seqs_dev, length, width)
    grad_part = grad_part.astype(single) + part_far.astype(single)
    grad_normed = grad_part.reshape(seqs_dev, length, width)
    hat = grad_normed * entry_gain
    hidden_grad = (
        cotangent.astype(single)
        + entry_scale * hat
        - residual
        * entry_scale
        * entry_scale
        * entry_scale
        * jnp.mean(hat * residual, axis=-1, keepdims=True)
    )
    loose_end = tap_rows * select_here
    grads = (
        summed[:, :inner_here],
        summed[:, inner_here : 2 * inner_here],
        summed[:, 2 * inner_here : conv_end],
        summed[:, conv_end:gain_column],
        summed[:, in_wide:].T,
        prenorm_grad,
        small[tap_rows],
        small[:tap_rows],
        small[tap_rows + 1, :loose_end].reshape(tap_rows, select_here),
        small[tap_rows + 1, loose_end : loose_end + 3 * heads_here].reshape(3, heads_here),
    )
    params = (
        gating,
        values,
        selector,
        timestep,
        output,
        prenorm,
        postnorm,
        filters,
        kernels,
        scalars,
    )
    moments = (
        gating_adam,
        values_adam,
        selector_adam,
        timestep_adam,
        output_adam,
        prenorm_adam,
        postnorm_adam,
        filters_adam,
        kernels_adam,
        scalars_adam,
    )
    updated = [adamw(param, moment, grad) for param, moment, grad in zip(params, moments, grads)]
    return (
        result,
        hidden_grad,
        grads[0],
        grads[1],
        grads[2],
        grads[3],
        grads[4],
        grads[5],
        grads[6],
        grads[7],
        grads[8],
        grads[9],
        updated[0][0],
        updated[1][0],
        updated[2][0],
        updated[3][0],
        updated[4][0],
        updated[5][0],
        updated[6][0],
        updated[7][0],
        updated[8][0],
        updated[9][0],
        updated[0][1],
        updated[1][1],
        updated[2][1],
        updated[3][1],
        updated[4][1],
        updated[5][1],
        updated[6][1],
        updated[7][1],
        updated[8][1],
        updated[9][1],
    )


def split(value, parts):
    pieces = []
    for _ in range(parts):
        piece = value.astype(jnp.bfloat16)
        pieces.append(piece)
        value = value - piece.astype(jnp.float32)
    return pieces


def mul(left, right):
    return jnp.dot(left, right, preferred_element_type=jnp.float32)


def mul_nt(left, right):
    return lax.dot_general(
        left, right, (((1,), (1,)), ((), ())), preferred_element_type=jnp.float32
    )


def mul_tn(left, right):
    return lax.dot_general(
        left, right, (((0,), (0,)), ((), ())), preferred_element_type=jnp.float32
    )


def wide_mul(value, table, parts):
    total = None
    for piece in split(value, parts):
        term = mul(piece, table)
        total = term if total is None else total + term
    return total


def table_mul(table, value, parts):
    total = None
    for piece in split(value, parts):
        term = mul(table, piece)
        total = term if total is None else total + term
    return total


def iota(shape, axis):
    return lax.broadcasted_iota(jnp.int32, shape, axis)


def each(count, step, body, start=None):
    def one(index, state):
        return body(pl.multiple_of(index * step, step), state)

    return lax.fori_loop(0, count, one, 0 if start is None else start)


def fold(value):
    rows, columns = value.shape
    return jnp.sum(value.reshape(rows // 8, 8, columns), axis=0)


class Table(NamedTuple):
    gat: object
    val: object
    sel: object
    hid: object
    cot: object
    outt: object
    pad: object
    spad: object
    ws: object
    wv: object
    wb: object
    wo: object
    scale: object
    normed: object
    raw: object
    draw: object
    delta: object
    run: object
    run3: object
    delta3: object
    scores_t: object
    wend: object
    runt: object
    deltat: object
    gdt: object
    growth: object
    ending: object
    x: object
    xw: object
    slope: object
    mine: object
    theirs: object
    bvec: object
    cvec: object
    scores: object
    local: object
    decay: object
    enter: object
    leave: object
    gend: object
    gout: object
    mixer: object
    across: object
    z: object
    gmix: object
    sums: object
    sums_far: object
    mixed: object
    gz: object
    gmh: object
    scaled: object
    gin: object
    gsc: object
    gdel: object
    seg: object
    gread: object
    kept: object
    given: object
    given_far: object
    gpre: object
    ga: object
    da: object
    db: object
    branch: object
    part: object
    branch_far: object
    part_far: object
    small: object
    zsmall: object
    dsmall: object
    tsmall: object
    rxa_a: object
    rya_a: object
    ryb_a: object
    rxb_a: object
    ta_a: object
    tb_a: object
    zb_a: object
    zin_a: object
    rxa_b: object
    rya_b: object
    ryb_b: object
    rxb_b: object
    ta_b: object
    tb_b: object
    zb_b: object
    zin_b: object
    sem_load: object
    sem_own: object
    sem_tail: object
    sem_swap: object
    sem_last: object
    sem_carry: object
    sem_zsmall: object
    sem_dsmall: object
    sem_gzs: object
    sem_gathers: object
    sem_gzv: object
    sem_gatherv: object
    sem_gzb: object
    sem_gatherb: object
    sem_gzo: object
    sem_gathero: object
    sem_reducea: object
    sem_rza: object
    sem_reduceb: object
    sem_rzb: object


def half(*shape):
    return pltpu.VMEM(shape, jnp.bfloat16)


def single(*shape):
    return pltpu.VMEM(shape, jnp.float32)


def dma(*shape):
    return pltpu.SemaphoreType.DMA(shape)


def plan(n, seqs, length, width, inner, pick, own, deep):
    rows = seqs * length
    total = seqs * inner
    first, second = inner + pick + LANES, 2 * inner
    return Table(
        gat=single(own, inner),
        val=single(own, inner),
        sel=single(own, pick),
        hid=half(rows, width),
        cot=half(rows, width),
        outt=single(own, inner),
        pad=single(LANES, LANES),
        spad=single(8, LANES),
        ws=half(4, n, own, pick + LANES),
        wv=half(4, n, own, inner),
        wb=half(4, n, own, inner),
        wo=half(4, n, own, inner),
        scale=single(rows, LANES),
        normed=half(rows, width),
        raw=single(seqs, length + 8, inner + pick),
        draw=single(rows, LANES),
        delta=single(rows, LANES),
        run=single(rows, LANES),
        run3=half(rows, 3 * LANES),
        delta3=half(rows, 3 * LANES),
        scores_t=single(rows, length),
        wend=single(rows, LANES),
        runt=single(seqs * 16, length),
        deltat=single(seqs * 16, length),
        gdt=single(LANES, length),
        growth=single(rows, inner),
        ending=single(rows, inner),
        x=half(rows, inner),
        xw=half(rows, inner),
        slope=single(rows, inner + pick),
        mine=half(rows, pick),
        theirs=half(rows, pick),
        bvec=half(rows, pick),
        cvec=half(rows, pick),
        scores=single(rows, length),
        local=single(total, deep),
        decay=single(total, deep),
        enter=half(total, deep),
        leave=half(total, deep),
        gend=half(total, deep),
        gout=half(total, deep),
        mixer=single(rows, inner),
        across=single(rows, inner),
        z=half(rows, inner),
        gmix=single(rows, inner),
        sums=single(rows, LANES),
        sums_far=single(rows, LANES),
        mixed=half(rows, inner),
        gz=half(rows, inner),
        gmh=half(rows, inner),
        scaled=half(rows, inner),
        gin=single(rows, inner),
        gsc=single(rows, length),
        gdel=single(rows, LANES),
        seg=single(rows, LANES),
        gread=single(rows, pick),
        kept=single(rows, pick),
        given=single(rows, pick),
        given_far=single(rows, pick),
        gpre=single(seqs, length + 8, inner + pick),
        ga=half(rows, first),
        da=half(2, 2, n, own, first),
        db=half(2, 2, n, own, second),
        branch=half(rows, width),
        part=half(rows, width),
        branch_far=half(rows, width),
        part_far=half(rows, width),
        small=single(16, inner + pick),
        zsmall=single(n, 16, inner + pick),
        dsmall=single(5, 16, inner + pick),
        tsmall=single(16, inner + pick),
        rxa_a=half(n, 2, own, first // 2),
        rya_a=half(n, own, first // 2),
        ryb_a=half(n, 2, own, first // 2),
        rxb_a=half(n, own, first // 2),
        ta_a=half(n, own, first // 2),
        tb_a=half(n, own, first // 2),
        zb_a=half(n - 1, own, first),
        zin_a=half(n - 1, own, first),
        rxa_b=half(n, 2, own, second // 2),
        rya_b=half(n, own, second // 2),
        ryb_b=half(n, 2, own, second // 2),
        rxb_b=half(n, own, second // 2),
        ta_b=half(n, own, second // 2),
        tb_b=half(n, own, second // 2),
        zb_b=half(n - 1, own, second),
        zin_b=half(n - 1, own, second),
        sem_load=dma(6),
        sem_own=dma(2),
        sem_tail=dma(4),
        sem_swap=dma(12),
        sem_last=dma(2),
        sem_carry=dma(4, PARTS),
        sem_zsmall=dma(2, n - 1),
        sem_dsmall=dma(2, 3),
        sem_gzs=dma(2, n - 1),
        sem_gathers=dma(8, n),
        sem_gzv=dma(2, n - 1),
        sem_gatherv=dma(8, n),
        sem_gzb=dma(2, n - 1),
        sem_gatherb=dma(8, n),
        sem_gzo=dma(2, n - 1),
        sem_gathero=dma(8, n),
        sem_reducea=dma(8, n),
        sem_rza=dma(2, n - 1),
        sem_reduceb=dma(8, n),
        sem_rzb=dma(2, n - 1),
    )


class Gather:
    def __init__(self, n, block, near, far, place):
        self.n, (self.d, self.s, x, y) = n, place
        self.xn, self.yn = y * 2 + (1 - x), (1 - y) * 2 + x
        self.block, self.near, self.far = block, near, far
        self.zf = [lax.rem(self.s + n - k, n) for k in range(n)]
        self.zt = [lax.rem(self.s + k, n) for k in range(n)]

    def deep(self, k):
        piece = self.block.at[self.d, self.s]
        sems = self.near.at[0, k - 1], self.near.at[1, k - 1]
        return send(piece, piece, *sems, {"seq": self.zt[k]})

    def side(self, j, axis):
        piece = self.block.at[self.d, self.zf[j]]
        sems = self.far.at[2 * axis, j], self.far.at[2 * axis + 1, j]
        return send(piece, piece, *sems, {"dp": (self.xn, self.yn)[axis]})

    def cross(self, j, axis):
        h = self.block.shape[3] // 2
        source, target = (self.yn, self.xn) if axis == 0 else (self.xn, self.yn)
        piece = self.block.at[source, self.zf[j], :, pl.ds(h if axis == 0 else 0, h)]
        sems = self.far.at[4 + 2 * axis, j], self.far.at[5 + 2 * axis, j]
        return send(piece, piece, *sems, {"dp": target})

    def begin(self):
        for k in range(1, self.n):
            self.deep(k).start()
        self.spread(0)

    def spread(self, j):
        if j:
            self.deep(j).wait_recv()
        self.side(j, 0).start()
        self.side(j, 1).start()

    def forward(self, j):
        self.side(j, 0).wait_recv()
        self.cross(j, 1).start()
        self.side(j, 1).wait_recv()
        self.cross(j, 0).start()

    def finish(self):
        for j in range(self.n):
            self.cross(j, 0).wait_recv()
            self.cross(j, 1).wait_recv()

    def close(self):
        for j in range(self.n):
            if j:
                self.deep(j).wait_send()
            for axis in range(2):
                self.side(j, axis).wait_send()
                self.cross(j, axis).wait_send()


class Reduce:
    def __init__(self, n, grad, bufs, sems, near, place):
        self.n, (self.d, self.s, self.x, self.y) = n, place
        self.grad, self.sems, self.near = grad, sems, near
        self.rxa, self.rya, self.ryb, self.rxb, self.ta, self.tb, self.zb, self.zin = bufs
        self.xn = self.y * 2 + (1 - self.x)
        self.yn = (1 - self.y) * 2 + self.x
        self.zt = [lax.rem(self.s + k, n) for k in range(n)]
        h = grad.shape[4] // 2
        self.left, self.right = pl.ds(0, h), pl.ds(h, h)
        self.order = list(range(1, n)) + [0]

    def copy(self, kind, j):
        sems = self.sems.at[2 * kind, j], self.sems.at[2 * kind + 1, j]
        z = self.zt[j]
        if kind == 0:
            source, target = self.grad.at[:, 1 - self.x, z, :, self.left], self.rxa.at[j]
        elif kind == 1:
            source, target = self.grad.at[1 - self.y, :, z, :, self.right], self.ryb.at[j]
        elif kind == 2:
            source, target = self.ta.at[j], self.rya.at[j]
        else:
            source, target = self.tb.at[j], self.rxb.at[j]
        return send(source, target, *sems, {"dp": self.xn if kind in (0, 3) else self.yn})

    def deep(self, j):
        sems = self.near.at[0, j - 1], self.near.at[1, j - 1]
        return send(self.zb.at[j - 1], self.zin.at[j - 1], *sems, {"seq": self.zt[j]})

    def launch(self, j):
        self.copy(0, j).start()
        self.copy(1, j).start()

    def begin(self):
        for j in self.order:
            self.launch(j)

    def middle(self, j):
        x, y, z = self.x, self.y, self.zt[j]
        single, half = jnp.float32, jnp.bfloat16
        self.copy(0, j).wait_recv()
        self.ta[j] = (
            self.grad[1 - y, x, z, :, self.left].astype(single)
            + self.rxa[j, 1 - y].astype(single)
        ).astype(half)
        self.copy(2, j).start()
        self.copy(1, j).wait_recv()
        self.tb[j] = (
            self.grad[y, 1 - x, z, :, self.right].astype(single)
            + self.ryb[j, 1 - x].astype(single)
        ).astype(half)
        self.copy(3, j).start()

    def join(self, j, out):
        x, y, z = self.x, self.y, self.zt[j]
        single, half = jnp.float32, jnp.bfloat16
        self.copy(2, j).wait_recv()
        low = (
            self.grad[y, x, z, :, self.left].astype(single)
            + self.rxa[j, y].astype(single)
            + self.rya[j].astype(single)
        )
        self.copy(3, j).wait_recv()
        high = (
            self.grad[y, x, z, :, self.right].astype(single)
            + self.ryb[j, x].astype(single)
            + self.rxb[j].astype(single)
        )
        if j == 0:
            out[:, self.left] = low
            out[:, self.right] = high
        else:
            self.zb[j - 1, :, self.left] = low.astype(half)
            self.zb[j - 1, :, self.right] = high.astype(half)
            self.deep(j).start()

    def finish(self, out):
        for j in range(1, self.n):
            self.deep(j).wait_recv()
            out[...] = out[...] + self.zin[j - 1].astype(jnp.float32)

    def close(self):
        for j in range(self.n):
            for kind in range(4):
                self.copy(kind, j).wait_send()
            if j:
                self.deep(j).wait_send()


def main_kernel(n, seqs, length, heads, *refs):
    inputs, refs = refs[:12], refs[12:]
    hid_h, cot_h, gat_h, val_h, sel_h, out_h = inputs[:6]
    step_ref, pre_ref, post_ref, filt_ref, kern_ref, scal_ref = inputs[6:]
    outputs, refs = refs[:5], refs[5:]
    suma_o, sumb_o, small_o, result_o, hidden_o = outputs
    r = Table(*refs)
    half, single = jnp.bfloat16, jnp.float32
    d, s = lax.axis_index("dp"), lax.axis_index("seq")
    core = lax.axis_index("tensor")
    y, x = d // 2, lax.rem(d, 2)
    place = (d, s, x, y)
    rows, width = r.hid.shape
    inner, pick = r.x.shape[1], r.mine.shape[1]
    conv = inner + pick
    pairs = inner // LANES
    deep = r.enter.shape[1]
    other = {"tensor": 1 - core}
    zt = [lax.rem(s + k, n) for k in range(n)]
    others = [{"dp": lax.rem(d + k, 4)} for k in range(1, 4)]
    after, before = {"seq": lax.rem(s + 1, n)}, {"seq": lax.rem(s + n - 1, n)}

    loads = [
        pltpu.make_async_copy(src, dst, r.sem_load.at[i])
        for i, (src, dst) in enumerate(
            [(sel_h, r.sel), (val_h, r.val), (hid_h, r.hid), (gat_h, r.gat), (out_h, r.outt), (cot_h, r.cot)]
        )
    ]
    for copy in loads:
        copy.start()
    own = r.val.shape[0]
    r.pad[...] = jnp.zeros(r.pad.shape, single)
    r.pad[:heads, :own] = step_ref[...]
    r.pad[heads : heads + 1, :own] = pre_ref[...].reshape(1, own)
    r.spad[...] = jnp.zeros(r.spad.shape, single)
    r.spad[:3, :heads] = scal_ref[...]
    ws, wv, wb, wo = r.ws, r.wv, r.wb, r.wo
    loads[0].wait()
    ws[d, s, :, :pick] = r.sel[...].astype(half)
    ws[d, s, :, pick:] = r.pad[...].T[:own].astype(half)
    loads[1].wait()
    wv[d, s] = r.val[...].astype(half)
    loads[3].wait()
    wb[d, s] = r.gat[...].astype(half)
    loads[4].wait()
    wo[d, s] = r.outt[...].astype(half)
    gs = Gather(n, ws, r.sem_gzs, r.sem_gathers, place)
    gv = Gather(n, wv, r.sem_gzv, r.sem_gatherv, place)
    gb = Gather(n, wb, r.sem_gzb, r.sem_gatherb, place)
    go = Gather(n, wo, r.sem_gzo, r.sem_gathero, place)
    greet([{"seq": zt[k]} for k in range(1, n)] + others + [other])
    gs.begin()
    gv.begin()
    loads[2].wait()
    loads[5].wait()
    tile = 32

    def scale_of(at, state):
        wide = r.hid[pl.ds(at, tile), :].astype(single)
        mean = jnp.sum(wide * wide, axis=1, keepdims=True) * (1.0 / width)
        r.scale[pl.ds(at, tile), :] = jnp.broadcast_to(
            lax.rsqrt(mean + epsilon), (tile, LANES)
        )
        return state

    each(rows // tile, tile, scale_of)

    heads_table = (iota((LANES, inner), 1) // HEADDIM == iota((LANES, inner), 0)).astype(half)
    table_heads = (iota((inner, LANES), 0) // HEADDIM == iota((inner, LANES), 1)).astype(half)
    lane = iota((1, LANES), 1)
    real = lane < heads
    bias = r.spad[0:1]
    rate = jnp.where(real, -jnp.exp(r.spad[1:2]), 0.0)
    skip = wide_mul(jnp.broadcast_to(r.spad[2:3], (8, LANES)), heads_table, 3)[0:1]
    post = post_ref[...].reshape(1, inner)

    for j in range(1, n):
        gs.spread(j)
        gs.forward(j - 1)
    gs.forward(n - 1)
    gv.spread(1)
    gb.begin()
    go.begin()
    gs.finish()

    step_t = ws[:, :, :, pick:].astype(single).reshape(width, LANES).T
    gain = step_t[heads : heads + 1, :]

    def norm_of(at, state):
        wide = r.hid[pl.ds(at, tile), :].astype(single)
        scale = r.scale[pl.ds(at, tile), 0:1]
        r.normed[pl.ds(at, tile), :] = (wide * scale * gain).astype(half)
        return state

    each(rows // tile, tile, norm_of)

    gv.spread(2)
    gv.forward(0)

    def weight_of(block, at, wide):
        return block[:, :, :, pl.ds(at, wide)].reshape(width, wide)

    tail = mul(r.normed[...], ws[...].reshape(width, pick + LANES))
    r.draw[...] = jnp.where(real, tail[:, pick:], 0.0)
    for q in range(seqs):
        r.raw[q, 8:, inner:] = (
            tail[q * length : (q + 1) * length, :pick].astype(half).astype(single)
        )

    gv.spread(3)
    gv.forward(1)

    low = (iota((length, length), 0) >= iota((length, length), 1)).astype(half)
    high = (iota((length, length), 0) <= iota((length, length), 1)).astype(half)
    cdecays = []
    for q in range(seqs):
        span = pl.ds(q * length, length)
        value = r.draw[span, :] + bias
        delta = jnp.maximum(value, 0.0) + jnp.log1p(jnp.exp(-jnp.abs(value)))
        delta = jnp.where(real, delta, 0.0)
        run = table_mul(low, delta * rate, 3)
        last = run[length - 1 : length, :]
        r.delta[span, :] = delta
        r.run[span, :] = run
        for target, whole in ((r.run3, run), (r.delta3, delta)):
            for i, piece in enumerate(split(whole, 3)):
                target[span, i * LANES : (i + 1) * LANES] = piece
        wend = jnp.exp(last - run) * delta
        r.wend[span, :] = wend
        r.runt[q * 16 : (q + 1) * 16, :] = run.T[:16]
        r.deltat[q * 16 : (q + 1) * 16, :] = delta.T[:16]
        cdecay = jnp.exp(last)
        cdecays.append(cdecay)
        pickrow = iota((inner, LANES), 0) // HEADDIM == iota((inner, LANES), 1)
        column = jnp.sum(jnp.where(pickrow, cdecay, 0.0), axis=1, keepdims=True)
        r.decay[q * inner : (q + 1) * inner, :] = jnp.broadcast_to(column, (inner, deep))
        r.growth[span, :] = wide_mul(jnp.exp(run), heads_table, 2)
        r.ending[span, :] = wide_mul(wend, heads_table, 2)

    gv.forward(2)
    gb.spread(1)
    gv.forward(3)
    gb.spread(2)
    gv.finish()

    def raw_of(at, state):
        value = mul(r.normed[...], weight_of(wv, at, 256)).astype(half).astype(single)
        for q in range(seqs):
            r.raw[q, 8:, pl.ds(at, 256)] = value[q * length : (q + 1) * length]
        return state

    each(inner // 256, 256, raw_of)

    tails = send(
        r.raw.at[:, pl.ds(length, 8)], r.raw.at[:, pl.ds(0, 8)],
        r.sem_tail.at[0], r.sem_tail.at[1], after,
    )

    @pl.when(s == 0)
    def _():
        r.raw[:, 0:8] = jnp.zeros((seqs, 8, conv), single)

    @pl.when(s != n - 1)
    def _():
        tails.start()

    gb.spread(3)
    gb.forward(0)
    gb.forward(1)
    go.spread(1)

    @pl.when(s != 0)
    def _():
        tails.wait_recv()

    def conv_of(first, wide):
        taps = [(kern_ref if first else filt_ref)[k : k + 1, :] for k in range(5)]
        for q in range(seqs):

            def one(at, state):
                padded = r.raw[q, pl.ds(at, tile + 8), first : first + wide]
                total = taps[4] + taps[3] * padded[8:]
                for k in range(3):
                    total = total + taps[k] * pltpu.roll(padded, 3 - k, 0)[8:]
                sigmoid = jax.nn.sigmoid(total)
                span = pl.ds(pl.multiple_of(q * length + at, tile), tile)
                act = (total * sigmoid).astype(half)
                if first:
                    r.mine[span, :] = act
                else:
                    r.x[span, :] = act
                    r.xw[span, :] = (act.astype(single) * r.ending[span, :]).astype(half)
                r.slope[span, first : first + wide] = sigmoid * (
                    1.0 + total * (1.0 - sigmoid)
                )
                return state

            each(length // tile, tile, one)

    conv_of(inner, pick)
    swaps = r.sem_swap
    trade = send(r.mine, r.theirs, swaps.at[0], swaps.at[1], other)
    trade.start()
    conv_of(0, inner)
    go.spread(2)
    gb.forward(2)
    trade.wait_recv()
    mine, theirs = r.mine[...], r.theirs[...]
    r.bvec[...] = jnp.where(core == 0, mine, theirs)
    r.cvec[...] = jnp.where(core == 0, theirs, mine)
    total = seqs * inner
    size = total // PARTS
    for q in range(seqs):
        span = pl.ds(q * length, length)
        r.local[q * inner : (q + 1) * inner, :] = mul_tn(r.xw[span, :], r.bvec[span, :])
        r.scores[span, :] = mul_nt(r.cvec[span, :], r.bvec[span, :])
        r.scores_t[span, :] = mul_nt(r.bvec[span, :], r.cvec[span, :])

    def carry_step(part, first, last, came, went, sem, target):
        span = pl.ds(pl.multiple_of(part * size, size), size)
        copy = send(
            went.at[span], came.at[span],
            r.sem_carry.at[sem, part], r.sem_carry.at[sem + 1, part], target,
        )

        @pl.when(s == first)
        def _():
            came[span, :] = jnp.zeros((size, deep), half)
            went[span, :] = r.local[span, :].astype(half)

        @pl.when(s != first)
        def _():
            copy.wait_recv()
            went[span, :] = (
                r.decay[span, :] * came[span, :].astype(single) + r.local[span, :]
            ).astype(half)

        @pl.when(s != last)
        def _():
            copy.start()

    def carry_close(last, came, went, sem, target):
        @pl.when(s != last)
        def _():
            for part in range(PARTS):
                span = pl.ds(part * size, size)
                send(
                    went.at[span], came.at[span],
                    r.sem_carry.at[sem, part], r.sem_carry.at[sem + 1, part], target,
                ).wait_send()

    causal = iota((length, length), 0) >= iota((length, length), 1)
    side = iota((1, LANES), 1) // HEADDIM

    def decays_of(q, h):
        span = pl.ds(pl.multiple_of(q * length, length), length)
        choose = ((iota((3 * LANES, LANES), 0) & (LANES - 1)) == h).astype(half)
        column = mul(r.run3[span, :], choose)
        row = r.runt[pl.ds(q * 16 + h, 1), :]
        gap = jnp.concatenate([column] * (length // LANES), axis=1) - row
        return jnp.exp(jnp.where(causal, gap, -1e30))

    def within_of(index, state):
        q, p = index // pairs, lax.rem(index, pairs)
        span = pl.ds(pl.multiple_of(q * length, length), length)
        lanes = pl.ds(pl.multiple_of(p * LANES, LANES), LANES)
        value = r.x[span, lanes]
        scores = r.scores[span, :]
        out = None
        for a in range(2):
            h = 2 * p + a
            step = r.deltat[pl.ds(q * 16 + h, 1), :]
            mixing = (scores * decays_of(q, h) * step).astype(half)
            term = mul(mixing, jnp.where(side == a, value, jnp.zeros_like(value)))
            out = term if out is None else out + term
        r.mixer[span, lanes] = out
        @pl.when(s != 0)
        def _():
            forth(index - lag)

        for at, pump in enumerate(pumps):
            pl.when(index == 3 * at + 1)(pump)
        return state

    def pump_b():
        gb.forward(3)
        go.spread(3)
        go.forward(0)

    def pump_c():
        go.forward(1)

    def pump_d():
        go.forward(2)

    pumps = [pump_b, pump_c, pump_d]
    lag = jnp.where(s == n - 1, PARTS, jnp.minimum(3 * s - 1, PARTS))

    def forth(part):
        @pl.when(part >= 0)
        def _():
            carry_step(part, 0, n - 1, r.enter, r.leave, 0, after)

    def forth_one(part, state):
        forth(part)
        return state

    @pl.when(s == 0)
    def _():
        lax.fori_loop(0, PARTS, forth_one, 0)

    lax.fori_loop(0, PARTS, within_of, 0)
    middle = jnp.where((s == n - 1) | (s == 0), 0, lag)
    lax.fori_loop(PARTS - middle, PARTS, forth_one, 0)
    go.forward(n - 1)
    gb.finish()

    def gate_of(at, state):
        r.z[:, pl.ds(at, 256)] = mul(r.normed[...], weight_of(wb, at, 256)).astype(half)
        return state

    each(inner // 256, 256, gate_of)
    go.finish()

    def down_of(at, state):
        r.gmix[:, pl.ds(at, 256)] = mul(r.cot[...], weight_of(wo, at, 256))
        return state

    each(inner // 256, 256, down_of)
    lax.fori_loop(jnp.where(s == n - 1, 0, PARTS), PARTS, forth_one, 0)

    trades = []
    for q in range(seqs):
        span = pl.ds(q * length, length)
        r.across[span, :] = mul_nt(
            r.cvec[span, :], r.enter[q * inner : (q + 1) * inner, :]
        )

        def mixer_of(at, state):
            span = pl.ds(pl.multiple_of(q * length + at, tile), tile)
            mixer = (
                r.mixer[span, :]
                + r.growth[span, :] * r.across[span, :]
                + skip * r.x[span, :].astype(single)
            )
            r.mixer[span, :] = mixer
            z = r.z[span, :].astype(single)
            gated = mixer * (z * jax.nn.sigmoid(z))
            squares = jnp.sum(gated * gated, axis=1, keepdims=True)
            dots = jnp.sum(r.gmix[span, :] * post * gated, axis=1, keepdims=True)
            r.sums[span, :] = jnp.where(lane == 0, squares, jnp.where(lane == 1, dots, 0.0))
            return state

        each(length // tile, tile, mixer_of)
        copy = send(
            r.sums.at[span], r.sums_far.at[span],
            swaps.at[2 + 2 * q], swaps.at[3 + 2 * q], other,
        )
        copy.start()
        trades.append(copy)

    full = 2 * inner

    def back_of(q):
        def one(at, state):
            span = pl.ds(pl.multiple_of(q * length + at, tile), tile)
            both = r.sums[span, :] + r.sums_far[span, :]
            scale = lax.rsqrt(both[:, 0:1] * (1.0 / full) + epsilon)
            dots = both[:, 1:2] * (1.0 / full)
            mixer, z = r.mixer[span, :], r.z[span, :].astype(single)
            sigmoid = jax.nn.sigmoid(z)
            act, slope = z * sigmoid, sigmoid * (1.0 + z * (1.0 - sigmoid))
            gated = mixer * act
            gmixed = r.gmix[span, :]
            r.mixed[span, :] = (gated * scale * post).astype(half)
            ggated = scale * (gmixed * post) - gated * (scale * scale * scale * dots)
            gmixer = ggated * act
            r.gz[span, :] = (ggated * mixer * slope).astype(half)
            r.gmh[span, :] = gmixer.astype(half)
            scaled = gmixer * r.growth[span, :]
            r.scaled[span, :] = scaled.astype(half)
            r.gmix[span, :] = gmixer
            r.across[span, :] = scaled * r.across[span, :]
            return (
                state[0] + fold(gmixed * gated * scale),
                state[1] + fold(gmixer * r.x[span, :].astype(single)),
            )

        return one

    state = (jnp.zeros((8, inner), single), jnp.zeros((8, inner), single))
    push = []
    for q in range(seqs):
        trades[q].wait_recv()
        state = each(length // tile, tile, back_of(q), state)
        span = pl.ds(q * length, length)
        r.local[q * inner : (q + 1) * inner, :] = mul_tn(r.scaled[span, :], r.cvec[span, :])

    def back(part):
        @pl.when((part >= 0) & (part < PARTS))
        def _():
            carry_step(part, n - 1, 0, r.gend, r.gout, 2, before)

    def back_one(part, state):
        back(part)
        return state

    @pl.when(s == n - 1)
    def _():
        lax.fori_loop(0, PARTS, back_one, 0)

    r.small[...] = jnp.zeros(r.small.shape, single)
    r.small[5:6, :inner] = jnp.sum(state[0], axis=0, keepdims=True)
    r.small[10:11, :LANES] = jnp.sum(wide_mul(state[1], table_heads, 3), axis=0, keepdims=True)

    ra = Reduce(
        n, r.da, (r.rxa_a, r.rya_a, r.ryb_a, r.rxb_a, r.ta_a, r.tb_a, r.zb_a, r.zin_a),
        r.sem_reducea, r.sem_rza, place,
    )
    rb = Reduce(
        n, r.db, (r.rxa_b, r.rya_b, r.ryb_b, r.rxb_b, r.ta_b, r.tb_b, r.zb_b, r.zin_b),
        r.sem_reduceb, r.sem_rzb, place,
    )

    span_y = width // 2

    def grad_b(index, state):
        lanes = pl.ds(pl.multiple_of(index * span_y, span_y), span_y)
        own = r.db.shape[3]
        r.db[index, :, :, :, pl.ds(0, inner)] = (
            mul_tn(r.normed[:, lanes], r.gz[...]).astype(half).reshape(2, n, own, inner)
        )
        r.db[index, :, :, :, pl.ds(inner, inner)] = (
            mul_tn(r.cot[:, lanes], r.mixed[...]).astype(half).reshape(2, n, own, inner)
        )
        return state

    lax.fori_loop(0, 2, grad_b, 0)

    def branch_of(index, state):
        lanes = pl.ds(pl.multiple_of(index * span_y, span_y), span_y)
        weight = wo[pl.ds(2 * index, 2)].reshape(span_y, inner)
        r.branch[:, lanes] = mul_nt(r.mixed[...], weight).astype(half)
        return state

    lax.fori_loop(0, 2, branch_of, 0)
    far = [send(r.branch, r.branch_far, swaps.at[6], swaps.at[7], other)]
    far[0].start()

    r.gsc[...] = jnp.zeros(r.gsc.shape, single)
    r.gdel[...] = jnp.zeros(r.gdel.shape, single)
    r.gdt[...] = jnp.zeros(r.gdt.shape, single)

    later = iota((length, length), 0) <= iota((length, length), 1)

    def intra_of(index, state):
        q, p = index // pairs, lax.rem(index, pairs)
        span = pl.ds(pl.multiple_of(q * length, length), length)
        lanes = pl.ds(pl.multiple_of(p * LANES, LANES), LANES)
        value, upper = r.x[span, lanes], r.gmh[span, lanes]
        scores = r.scores_t[span, :]
        out = None
        for a in range(2):
            h = 2 * p + a
            choose = ((iota((3 * LANES, LANES), 0) & (LANES - 1)) == h).astype(half)
            column = mul(r.run3[span, :], choose)
            step = mul(r.delta3[span, :], choose)
            step = jnp.concatenate([step] * (length // LANES), axis=1)
            row = r.runt[pl.ds(q * 16 + h, 1), :]
            gap = row - jnp.concatenate([column] * (length // LANES), axis=1)
            decays = jnp.exp(jnp.where(later, gap, -1e30))
            masked = jnp.where(side == a, upper, jnp.zeros_like(upper))
            mixing = (scores * decays * step).astype(half)
            term = mul(mixing, masked)
            out = term if out is None else out + term
            spread = mul_nt(value, masked) * decays
            kernel = spread * scores
            fall = jnp.sum(kernel, axis=1, keepdims=True)
            r.gdel[span, :] += jnp.where(lane == h, fall, 0.0)
            r.gsc[span, :] += spread * step
            r.gdt[pl.ds(q * 16 + h, 1), :] = jnp.sum(kernel * step, axis=0, keepdims=True)
        r.gin[span, lanes] = out
        @pl.when(s != n - 1)
        def _():
            back(2 * (index - delay))
            back(2 * (index - delay) + 1)

        for at, j in enumerate(rb.order):

            @pl.when(index == 2 * at)
            def _():
                rb.launch(j)

            @pl.when(index == 2 * at + 5)
            def _():
                rb.middle(j)

        return state

    delay = 2 * (n - 2 - s)
    lax.fori_loop(0, PARTS, intra_of, 0)

    def gate_part(index, state):
        lanes = pl.ds(pl.multiple_of(index * span_y, span_y), span_y)
        gate = wb[pl.ds(2 * index, 2)].reshape(span_y, inner)
        r.mixer[:, lanes] = mul_nt(r.gz[...], gate)
        return state

    lax.fori_loop(0, 2, gate_part, 0)

    gdt = r.gdt[...].T
    bias_row, log_row = jnp.zeros((1, LANES), single), jnp.zeros((1, LANES), single)
    seg = [wide_mul(r.across[pl.ds(q * length, length), :], table_heads, 2) for q in range(seqs)]
    for q in range(seqs):
        span = pl.ds(q * length, length)
        states = pl.ds(q * inner, inner)
        r.across[span, :] = mul_nt(r.bvec[span, :], r.gend[states, :])
        r.gread[span, :] = mul(r.scaled[span, :], r.enter[states, :])
        gsc = r.gsc[span, :].astype(half)
        gread = r.gread[span, :] + mul_tn(gsc, r.bvec[span, :])
        gwrite = mul(gsc, r.cvec[span, :]) + mul(r.xw[span, :], r.gend[states, :])
        r.kept[span, :] = jnp.where(core == 0, gwrite, gread)
        r.given[span, :] = jnp.where(core == 0, gread, gwrite)
    trade2 = send(r.given, r.given_far, swaps.at[8], swaps.at[9], other)
    trade2.start()

    def inner_of(at, state):
        span = pl.ds(at, tile)
        back = r.across[span, :]
        total = (
            r.gin[span, :] + skip * r.gmix[span, :] + back * r.ending[span, :]
        )
        r.gin[span, :] = total
        r.across[span, :] = back * r.x[span, :].astype(single)
        return state

    each(rows // tile, tile, inner_of)

    for q in range(seqs):
        span = pl.ds(q * length, length)
        states = pl.ds(q * inner, inner)
        weight = wide_mul(r.across[span, :], table_heads, 2)
        product = r.gend[states, :].astype(single) * r.enter[states, :].astype(single)
        ones = jnp.ones((8, deep), half)
        across = sum(mul_nt(ones, piece) for piece in split(product, 2))
        end_row = wide_mul(across, table_heads, 3)[0:1] * cdecays[q]
        delta, run, wend = r.delta[span, :], r.run[span, :], r.wend[span, :]
        grun = jnp.where(
            lane < heads, pltpu.roll(gdt, LANES - 16 * q, 1) if q else gdt, 0.0
        )
        gdelta = r.gdel[span, :]
        grun = grun - delta * gdelta + seg[q]
        last = run[length - 1 : length, :]
        gdelta = gdelta + weight * jnp.exp(last - run)
        spread = weight * wend
        end_row = end_row + jnp.sum(spread, axis=0, keepdims=True)
        grun = grun - spread + jnp.where(iota((length, 1), 0) == length - 1, end_row, 0.0)
        glog = table_mul(high, grun, 3)
        gdelta = gdelta + glog * rate
        log_row = log_row + jnp.sum(glog * delta, axis=0, keepdims=True) * rate
        gdraw = jnp.where(real, gdelta * jax.nn.sigmoid(r.draw[span, :] + bias), 0.0)
        bias_row = bias_row + jnp.sum(gdraw, axis=0, keepdims=True)
        r.ga[span, conv:] = gdraw.astype(half)
    r.small[8:9, :LANES] = bias_row
    r.small[9:10, :LANES] = log_row

    trade2.wait_recv()
    for q in range(seqs):

        def pre_of(at, state):
            span = pl.ds(pl.multiple_of(q * length + at, tile), tile)
            r.gpre[q, pl.ds(at, tile), :inner] = r.gin[span, :] * r.slope[span, :inner]
            r.gpre[q, pl.ds(at, tile), inner:] = (
                r.kept[span, :] + r.given_far[span, :]
            ) * r.slope[span, inner:]
            return state

        each(length // tile, tile, pre_of)

    tails2 = send(
        r.gpre.at[:, pl.ds(0, 8)], r.gpre.at[:, pl.ds(length, 8)],
        r.sem_tail.at[2], r.sem_tail.at[3], before,
    )

    @pl.when(s == n - 1)
    def _():
        r.gpre[:, length:] = jnp.zeros((seqs, 8, conv), single)

    @pl.when(s != 0)
    def _():
        tails2.start()

    @pl.when(s != n - 1)
    def _():
        tails2.wait_recv()

    for j in rb.order:
        rb.join(j, sumb_o)

    taps = [
        jnp.concatenate([filt_ref[k : k + 1, :], kern_ref[k : k + 1, :]], axis=1)
        for k in range(4)
    ]
    for q in range(seqs):

        def raw_grad(at, state):
            padded = r.gpre[q, pl.ds(at, tile + 8), :]
            total = taps[3] * padded[:tile]
            for k in range(3):
                total = total + taps[k] * pltpu.roll(padded, tile + 8 - (3 - k), 0)[:tile]
            span = pl.ds(pl.multiple_of(q * length + at, tile), tile)
            r.ga[span, :conv] = total.astype(half)
            return state

        each(length // tile, tile, raw_grad)

    def grad_a(index, state):
        lanes = pl.ds(pl.multiple_of(index * span_y, span_y), span_y)
        own, wide = r.da.shape[3:]
        r.da[index] = (
            mul_tn(r.normed[:, lanes], r.ga[...]).astype(half).reshape(2, n, own, wide)
        )
        return state

    lax.fori_loop(0, 2, grad_a, 0)
    ra.begin()

    def part_of(index, state):
        lanes = pl.ds(pl.multiple_of(index * span_y, span_y), span_y)
        block = pl.ds(2 * index, 2)
        value = wv[block].reshape(span_y, inner)
        select = ws[block].reshape(span_y, pick + LANES)
        r.part[:, lanes] = (
            r.mixer[:, lanes]
            + mul_nt(r.ga[:, :inner], value)
            + mul_nt(r.ga[:, inner:], select)
        ).astype(half)
        return state

    lax.fori_loop(0, 2, part_of, 0)
    far.append(send(r.part, r.part_far, swaps.at[10], swaps.at[11], other))
    far[1].start()

    def gain_of(at, state):
        span = pl.ds(at, tile)
        term = (
            r.part[span, :].astype(single)
            * r.hid[span, :].astype(single)
            * r.scale[span, 0:1]
        )
        return state + fold(term)

    gain_sum = each(rows // tile, tile, gain_of, jnp.zeros((8, width), single))
    r.small[6:7, :width] = jnp.sum(gain_sum, axis=0, keepdims=True)

    taps_sum = tuple(jnp.zeros((8, conv), single) for _ in range(5))
    for q in range(seqs):

        def taps_of(at, state):
            pre = r.gpre[q, pl.ds(at, tile), :]
            padded = r.raw[q, pl.ds(at, tile + 8), :]
            terms = [pre * pltpu.roll(padded, 3 - k, 0)[8:] for k in range(3)]
            terms += [pre * padded[8:], pre]
            return tuple(total + fold(term) for total, term in zip(state, terms))

        taps_sum = each(length // tile, tile, taps_of, taps_sum)
    for k in range(5):
        r.small[k : k + 1, :] = jnp.sum(taps_sum[k], axis=0, keepdims=True)

    smalls = []
    for k in range(1, n):
        copy = send(
            r.small, r.zsmall.at[s],
            r.sem_zsmall.at[0, k - 1], r.sem_zsmall.at[1, k - 1], {"seq": zt[k]},
        )
        copy.start()
        smalls.append(copy)
    r.zsmall[s] = r.small[...]
    far[0].wait_recv()
    far[1].wait_recv()

    def result_of(at, state):
        span = pl.ds(at, tile)
        wide = r.hid[span, :].astype(single)
        scale = r.scale[span, 0:1]
        r.gmix[span, :] = (
            wide + r.branch[span, :].astype(single) + r.branch_far[span, :].astype(single)
        )
        hat = (r.part[span, :].astype(single) + r.part_far[span, :].astype(single)) * gain
        dots = jnp.sum(hat * wide, axis=1, keepdims=True) * (1.0 / width)
        r.gin[span, :] = (
            r.cot[span, :].astype(single)
            + scale * hat
            - wide * (scale * scale * scale * dots)
        )
        return state

    each(rows // tile, tile, result_of)
    keep = [
        pltpu.make_async_copy(r.gmix, result_o, r.sem_own.at[0]),
        pltpu.make_async_copy(r.gin, hidden_o, r.sem_own.at[1]),
    ]
    for copy in keep:
        copy.start()
    for copy in smalls:
        copy.wait_recv()
    total_small = r.zsmall[0]
    for k in range(1, n):
        total_small = total_small + r.zsmall[k]
    r.dsmall[d] = total_small
    widely = []
    for k in range(3):
        copy = send(
            r.dsmall.at[d], r.dsmall.at[d],
            r.sem_dsmall.at[0, k], r.sem_dsmall.at[1, k], others[k],
        )
        copy.start()
        widely.append(copy)
    for place_, j in enumerate(ra.order):
        ra.middle(j)
        if place_:
            ra.join(ra.order[place_ - 1], suma_o)
    ra.join(0, suma_o)
    for copy in widely:
        copy.wait_recv()
    total_small = r.dsmall[0] + r.dsmall[1] + r.dsmall[2] + r.dsmall[3]
    r.dsmall[4] = total_small
    last_trade = send(r.dsmall.at[4], r.tsmall, r.sem_last.at[0], r.sem_last.at[1], other)
    last_trade.start()
    rb.finish(sumb_o)
    ra.finish(suma_o)
    last_trade.wait()
    small_o[...] = total_small
    gains = jnp.broadcast_to(r.dsmall[4, 6:7, :width] + r.tsmall[6:7, :width], (8, width))
    turn = lax.rem(width - (d * n + s) * own, width)
    small_o[7:8, :width] = pltpu.roll(gains, turn, 1)[0:1]

    for group in (gs, gv, gb, go):
        group.close()
    ra.close()
    rb.close()
    carry_close(n - 1, r.enter, r.leave, 0, after)
    carry_close(0, r.gend, r.gout, 2, before)

    @pl.when(s != n - 1)
    def _():
        tails.wait_send()

    @pl.when(s != 0)
    def _():
        tails2.wait_send()

    for copy in [trade, trade2] + trades:
        copy.wait_send()
    for copy in keep:
        copy.wait()
    for copy in far:
        copy.wait_send()
    for copy in smalls + widely:
        copy.wait_send()


def finish_kernel(heads, *refs):
    single = jnp.float32
    suma, sumb, small = refs[:3]
    tokens, weights, moments = refs[3:5], refs[5:15], refs[15:25]
    outputs, scratch = refs[25:57], refs[57:]
    weight_v, moment_v, grad_v, next_v, state_v = (
        scratch[:5], scratch[5:10], scratch[10:15], scratch[15:20], scratch[20:25]
    )
    sems = scratch[25:28]
    result_o, grad_o, next_o, state_o = (
        outputs[:2], outputs[2:12], outputs[12:22], outputs[22:32],
    )
    inner, pick = weight_v[0].shape[1], weight_v[2].shape[1]
    own = weight_v[0].shape[0]
    gone = []

    def leave(src, dst, sem):
        copy = pltpu.make_async_copy(src, dst, sem)
        copy.start()
        gone.append(copy)

    arrive = [
        [
            pltpu.make_async_copy(weights[i], weight_v[i], sems[0].at[0, i]),
            pltpu.make_async_copy(moments[i], moment_v[i], sems[0].at[1, i]),
        ]
        for i in range(5)
    ]
    for group in arrive:
        for copy in group:
            copy.start()
    token_v = scratch[28:]
    size = tokens[0].shape[0] // 2
    through = []
    for i in range(2):
        for k in range(2):
            span = pl.ds(k * size, size)
            copy = pltpu.make_async_copy(
                tokens[i].at[span], token_v[i].at[span], sems[1].at[0, 2 * i + k]
            )
            copy.start()
            through.append((copy, token_v[i].at[span], result_o[i].at[span]))

    def pass_on(at):
        copy, src, dst = through[at]
        copy.wait()
        leave(src, dst, sems[1].at[1, at])

    tall = jnp.concatenate([suma[:, inner + pick :], jnp.zeros((LANES - own, LANES), single)], axis=0).T
    grads = (sumb[:, :inner], suma[:, :inner], suma[:, inner : inner + pick], tall[:heads, :own], sumb[:, inner:])
    for i, grad in enumerate(grads):
        grad_v[i][...] = grad
        leave(grad_v[i], grad_o[i], sems[2].at[0, i])
    smalls = (
        small[7:8, :own],
        small[5:6, :inner],
        small[:5, :inner],
        small[:5, inner:],
        small[8:11, :heads],
    )
    for i, grad in enumerate(smalls):
        k = 5 + i
        flat = i < 2
        first_at = slice(0, 1) if flat else (slice(None), 0)
        second_at = slice(1, 2) if flat else (slice(None), 1)
        param = weights[k][...].reshape(grad.shape)
        fresh, first, second = step_of(param, moments[k][first_at], moments[k][second_at], grad)
        grad_o[k][...] = grad.reshape(grad_o[k].shape)
        next_o[k][...] = fresh.reshape(next_o[k].shape)
        state_o[k][first_at] = first
        state_o[k][second_at] = second
    pass_on(0)
    pass_on(1)
    for i, grad in enumerate(grads):
        for copy in arrive[i]:
            copy.wait()
        apart = i == 3
        first_at = (slice(None), 0) if apart else 0
        second_at = (slice(None), 1) if apart else 1
        fresh, first, second = step_of(
            weight_v[i][...], moment_v[i][first_at], moment_v[i][second_at], grad
        )
        next_v[i][...] = fresh
        state_v[i][first_at] = first
        state_v[i][second_at] = second
        leave(next_v[i], next_o[i], sems[2].at[1, i])
        leave(state_v[i], state_o[i], sems[2].at[2, i])
    pass_on(2)
    pass_on(3)
    for copy in gone:
        copy.wait()


def step_of(param, first, second, grad):
    first = first_decay * first + (1.0 - first_decay) * grad
    second = second_decay * second + (1.0 - second_decay) * grad * grad
    first_hat = first / (1.0 - first_decay**STEP)
    second_hat = second / (1.0 - second_decay**STEP)
    fresh = param - learn_rate * (
        first_hat / (jnp.sqrt(second_hat) + adam_epsilon) + weight_decay * param
    )
    return fresh, first, second


def fast(
    hidden, cotangent, gating, values, selector, timestep, output, prenorm, postnorm,
    filters, kernels, scalars, gating_adam, values_adam, selector_adam, timestep_adam,
    output_adam, prenorm_adam, postnorm_adam, filters_adam, kernels_adam, scalars_adam,
):
    half, single = jnp.bfloat16, jnp.float32
    n = lax.axis_size("seq")
    seqs, length, width = hidden.shape
    rows = seqs * length
    own, inner = gating.shape
    pick, heads = selector.shape[1], timestep.shape[1]
    conv = inner + pick
    scratch = plan(n, seqs, length, width, inner, pick, own, STATE)
    hid, cot = hidden.reshape(rows, width), cotangent.reshape(rows, width)
    shape = jax.ShapeDtypeStruct
    token = shape((rows, width), single)
    suma, sumb, small, *tokens = pl.pallas_call(
        functools.partial(main_kernel, n, seqs, length, heads),
        out_shape=(
            shape((own, conv + LANES), single),
            shape((own, 2 * inner), single),
            shape((16, conv), single),
            token,
            token,
        ),
        in_specs=[ANY] * 6 + [VMEM] * 6,
        out_specs=(VMEM,) * 3 + (ANY,) * 2,
        scratch_shapes=list(scratch),
        compiler_params=pltpu.CompilerParams(
            collective_id=0, has_side_effects=True, vmem_limit_bytes=VMEM_BYTES
        ),
    )(
        hid, cot, gating, values, selector, output.T, timestep.T, prenorm,
        postnorm, filters, kernels, scalars,
    )

    weights = (
        gating, values, selector, timestep.T, output.T, prenorm, postnorm,
        filters, kernels, scalars,
    )
    swapped = [jnp.transpose(m, (1, 0, 2)) for m in (filters_adam, kernels_adam, scalars_adam)]
    moments = (
        gating_adam, values_adam, selector_adam, jnp.transpose(timestep_adam, (2, 0, 1)),
        jnp.transpose(output_adam, (0, 2, 1)), prenorm_adam, postnorm_adam, *swapped,
    )
    out_shape = [shape((rows, width), single)] * 2
    out_shape += [shape(w.shape, single) for w in weights] * 2
    out_shape += [shape(m.shape, single) for m in moments]
    dma_shape = pltpu.SemaphoreType.DMA
    kinds = [ANY] * 5 + [VMEM] * 5
    done = pl.pallas_call(
        functools.partial(finish_kernel, heads),
        out_shape=out_shape,
        in_specs=[VMEM] * 3 + [ANY] * 2 + kinds * 2,
        out_specs=[ANY] * 2 + kinds * 3,
        scratch_shapes=[pltpu.VMEM(w.shape, single) for w in weights[:5]]
        + [pltpu.VMEM(m.shape, single) for m in moments[:5]]
        + [pltpu.VMEM(w.shape, single) for w in weights[:5]] * 2
        + [pltpu.VMEM(m.shape, single) for m in moments[:5]]
        + [dma_shape((2, 5)), dma_shape((2, 4)), dma_shape((3, 5))]
        + [pltpu.VMEM((rows, width), single)] * 2,
        compiler_params=pltpu.CompilerParams(vmem_limit_bytes=VMEM_BYTES),
    )(suma, sumb, small, *tokens, *weights, *moments)
    result, hidden_grad = (value.reshape(hidden.shape) for value in done[:2])

    def whole(group):
        big, tiny = group[:3], group[7:]
        return (*big, group[3].T, group[4].T, group[5], group[6], *tiny)

    states = done[22:]
    return (
        (result, hidden_grad)
        + whole(done[2:12])
        + whole(done[12:22])
        + (
            *states[:3],
            jnp.transpose(states[3], (1, 2, 0)),
            jnp.transpose(states[4], (0, 2, 1)),
            *states[5:7],
            *(jnp.transpose(m, (1, 0, 2)) for m in states[7:]),
        )
    )


def shards(*arrays):
    if (lax.axis_size("dp"), lax.axis_size("seq")) == (4, 4):
        return fast(*arrays)
    return general(*arrays)


def solution(mesh):
    placed = (
        P("dp", "seq", None),
        P("dp", "seq", None),
        P(("dp", "seq"), "tensor"),
        P(("dp", "seq"), "tensor"),
        P(("dp", "seq"), "tensor"),
        P(("dp", "seq"), "tensor"),
        P("tensor", ("dp", "seq")),
        P(("dp", "seq")),
        P("tensor"),
        P(None, "tensor"),
        P(None, "tensor"),
        P(None, "tensor"),
        P(None, ("dp", "seq"), "tensor"),
        P(None, ("dp", "seq"), "tensor"),
        P(None, ("dp", "seq"), "tensor"),
        P(None, ("dp", "seq"), "tensor"),
        P(None, "tensor", ("dp", "seq")),
        P(None, ("dp", "seq")),
        P(None, "tensor"),
        P(None, None, "tensor"),
        P(None, None, "tensor"),
        P(None, None, "tensor"),
    )
    return jax.shard_map(
        shards,
        mesh=mesh,
        in_specs=placed,
        out_specs=(
            P("dp", "seq", None),
            P("dp", "seq", None),
            P(("dp", "seq"), "tensor"),
            P(("dp", "seq"), "tensor"),
            P(("dp", "seq"), "tensor"),
            P(("dp", "seq"), "tensor"),
            P("tensor", ("dp", "seq")),
            P(("dp", "seq")),
            P("tensor"),
            P(None, "tensor"),
            P(None, "tensor"),
            P(None, "tensor"),
            P(("dp", "seq"), "tensor"),
            P(("dp", "seq"), "tensor"),
            P(("dp", "seq"), "tensor"),
            P(("dp", "seq"), "tensor"),
            P("tensor", ("dp", "seq")),
            P(("dp", "seq")),
            P("tensor"),
            P(None, "tensor"),
            P(None, "tensor"),
            P(None, "tensor"),
            P(None, ("dp", "seq"), "tensor"),
            P(None, ("dp", "seq"), "tensor"),
            P(None, ("dp", "seq"), "tensor"),
            P(None, ("dp", "seq"), "tensor"),
            P(None, "tensor", ("dp", "seq")),
            P(None, ("dp", "seq")),
            P(None, "tensor"),
            P(None, None, "tensor"),
            P(None, None, "tensor"),
            P(None, None, "tensor"),
        ),
        check_vma=False,
    )
```

```python
import functools
from typing import NamedTuple
import jax
import jax.numpy as jnp
from jax import lax
from jax.experimental import pallas as pl
from jax.experimental.pallas import tpu as pltpu
from jax.sharding import PartitionSpec as P

INNER = 1536
STATE = 128
HEADDIM = 64
STEP = 2


epsilon = 1e-05
highest = lax.Precision.HIGHEST
learn_rate = 0.01
first_decay = 0.9
second_decay = 0.999
adam_epsilon = 1e-08
weight_decay = 0.1


def from_behind(block, axis, distance):
    devices = range(lax.axis_size(axis))
    route = [(i - distance, i) for i in devices if i - distance in devices]
    return lax.ppermute(block, axis, route)


MESH = pl.DeviceIdType.MESH
VMEM = pl.BlockSpec(memory_space=pltpu.VMEM)
ANY = pl.BlockSpec(memory_space=pl.ANY)
LANES = 128
PARTS = 12
VMEM_BYTES = 60 * 2**20


def send(src, dst, send_sem, recv_sem, device):
    return pltpu.make_async_remote_copy(
        src_ref=src,
        dst_ref=dst,
        send_sem=send_sem,
        recv_sem=recv_sem,
        device_id=device,
        device_id_type=MESH,
    )


def greet(devices):
    barrier = pltpu.get_barrier_semaphore()
    for device in devices:
        pl.semaphore_signal(barrier, inc=1, device_id=device, device_id_type=MESH)
    pl.semaphore_wait(barrier, len(devices))


def params_of(collective_id):
    return pltpu.CompilerParams(collective_id=collective_id, has_side_effects=True)


def swap_kernel(x_ref, o_ref, send_sem, recv_sem):
    other = {"tensor": 1 - lax.axis_index("tensor")}
    greet([other])
    copy = send(x_ref, o_ref, send_sem, recv_sem, other)
    copy.start()
    copy.wait()


def swap(value, collective_id):
    return pl.pallas_call(
        swap_kernel,
        out_shape=jax.ShapeDtypeStruct(value.shape, value.dtype),
        in_specs=[VMEM],
        out_specs=VMEM,
        scratch_shapes=[pltpu.SemaphoreType.DMA, pltpu.SemaphoreType.DMA],
        compiler_params=params_of(collective_id),
    )(value)


def carry_kernel(count, step, parts, decay_ref, local_ref, o_ref, out_buf, in_buf, send_sem, recv_sem):
    me = lax.axis_index("seq")
    target = lax.rem(me + count + step, count)
    source = lax.rem(me + count - step, count)
    first, last = (0, count - 1) if step > 0 else (count - 1, 0)
    greet([{"seq": target}, {"seq": source}])
    size = local_ref.shape[0] // parts

    def copy_of(part):
        return send(
            out_buf.at[part],
            in_buf.at[part],
            send_sem.at[part],
            recv_sem.at[part],
            {"seq": target},
        )

    for part in range(parts):
        rows = pl.ds(part * size, size)

        @pl.when(me == first)
        def _():
            o_ref[rows] = jnp.zeros((size,) + o_ref.shape[1:], o_ref.dtype)
            out_buf[part] = local_ref[rows].astype(jnp.bfloat16)

        @pl.when(me != first)
        def _():
            copy_of(part).wait_recv()
            entering = in_buf[part]
            o_ref[rows] = entering
            out_buf[part] = (
                decay_ref[rows] * entering.astype(jnp.float32) + local_ref[rows]
            ).astype(jnp.bfloat16)

        @pl.when(me != last)
        def _():
            copy_of(part).start()

    @pl.when(me != last)
    def _():
        for part in range(parts):
            copy_of(part).wait_send()


def carry(decay, local, count, step, collective_id):
    seqs, heads, wide, deep = local.shape
    total = seqs * heads
    parts = 6 if total % 6 == 0 else 1
    size = total // parts
    spread = jnp.broadcast_to(decay.reshape(total, 1, 1), (total, 1, deep))
    result = pl.pallas_call(
        functools.partial(carry_kernel, count, step, parts),
        out_shape=jax.ShapeDtypeStruct((total, wide, deep), jnp.bfloat16),
        in_specs=[VMEM, VMEM],
        out_specs=VMEM,
        scratch_shapes=[
            pltpu.VMEM((parts, size, wide, deep), jnp.bfloat16),
            pltpu.VMEM((parts, size, wide, deep), jnp.bfloat16),
            pltpu.SemaphoreType.DMA((parts,)),
            pltpu.SemaphoreType.DMA((parts,)),
        ],
        compiler_params=params_of(collective_id),
    )(spread, local.reshape(total, wide, deep))
    return result.reshape(local.shape)


def swish_parts(value):
    sigmoid = jax.nn.sigmoid(value)
    return (value * sigmoid, sigmoid * (1.0 + value * (1.0 - sigmoid)))


def conv_apply(padded, taps):
    tap_count = taps.shape[0] - 1
    length = padded.shape[1] - tap_count + 1
    wide = padded.astype(jnp.float32)
    total = taps[tap_count] + taps[0] * wide[:, 0:length]
    for index in range(1, tap_count):
        total = total + taps[index] * wide[:, index : index + length]
    return total


def conv_back(padded, taps, grad_pre):
    tap_count = taps.shape[0] - 1
    length = grad_pre.shape[1]
    wide = padded.astype(jnp.float32)
    tap_rows = [
        jnp.sum(grad_pre * wide[:, index : index + length], axis=(0, 1))
        for index in range(tap_count)
    ]
    tap_rows.append(jnp.sum(grad_pre, axis=(0, 1)))
    grad_pad = jnp.zeros(padded.shape, jnp.float32)
    for index in range(tap_count):
        grad_pad = grad_pad + jnp.pad(
            taps[index] * grad_pre, ((0, 0), (index, tap_count - 1 - index), (0, 0))
        )
    return (jnp.stack(tap_rows), grad_pad)


def adamw(param, moments, grad):
    first = first_decay * moments[0] + (1.0 - first_decay) * grad
    second = second_decay * moments[1] + (1.0 - second_decay) * grad * grad
    first_hat = first / (1.0 - first_decay**STEP)
    second_hat = second / (1.0 - second_decay**STEP)
    fresh = param - learn_rate * (
        first_hat / (jnp.sqrt(second_hat) + adam_epsilon) + weight_decay * param
    )
    return (fresh, jnp.stack([first, second]))


def general(
    hidden,
    cotangent,
    gating,
    values,
    selector,
    timestep,
    output,
    prenorm,
    postnorm,
    filters,
    kernels,
    scalars,
    gating_adam,
    values_adam,
    selector_adam,
    timestep_adam,
    output_adam,
    prenorm_adam,
    postnorm_adam,
    filters_adam,
    kernels_adam,
    scalars_adam,
):
    half = jnp.bfloat16
    single = jnp.float32
    n_seq = lax.axis_size("seq")
    core = lax.axis_index("tensor")
    seqs_dev, length, width = hidden.shape
    rows = seqs_dev * length
    own_rows = gating.shape[0]
    lead = filters.shape[0] - 2
    heads_here = timestep.shape[1]
    inner_here = gating.shape[1]
    select_here = selector.shape[1]
    conv_end = 2 * inner_here + select_here
    step_wide = 128
    in_wide = conv_end + step_wide
    packed = jnp.concatenate(
        [
            gating.astype(half),
            values.astype(half),
            selector.astype(half),
            timestep.astype(half),
            prenorm.astype(half)[:, None],
            jnp.zeros((own_rows, step_wide - heads_here - 1), half),
            output.T.astype(half),
        ],
        axis=1,
    )
    weights = lax.all_gather(packed, ("dp", "seq"), axis=0, tiled=True)
    in_weight = weights[:, :in_wide]
    out_weight = weights[:, in_wide:]
    bias = scalars[0]
    rate = -jnp.exp(scalars[1])
    skip = scalars[2]
    entry_gain = weights[:, conv_end + heads_here].astype(single)
    residual = hidden.astype(single)
    entry_scale = lax.rsqrt(jnp.mean(residual * residual, axis=-1, keepdims=True) + epsilon)
    normed = (residual * entry_scale * entry_gain).astype(half)
    flat = normed.reshape(rows, width)
    raw = jnp.dot(flat, in_weight, preferred_element_type=single)
    gate_raw = raw[:, :inner_here].astype(half).reshape(seqs_dev, length, inner_here)
    conv_raw = raw[:, inner_here:conv_end].astype(half).reshape(seqs_dev, length, -1)
    delta_raw = raw[:, conv_end : conv_end + heads_here].reshape(seqs_dev, length, heads_here)
    tails = from_behind(conv_raw[:, length - lead :], "seq", 1)
    conv_pad = jnp.concatenate([tails, conv_raw], axis=1)
    taps = jnp.concatenate([filters, kernels], axis=1)
    conv_value, conv_slope = swish_parts(conv_apply(conv_pad, taps))
    conv_act = conv_value.astype(half)
    inner_act = conv_act[:, :, :inner_here]
    mine = conv_act[:, :, inner_here:]
    theirs = swap(mine.reshape(rows, select_here), 1).reshape(mine.shape)
    write_vec = jnp.where(core == 0, mine, theirs)
    read_vec = jnp.where(core == 0, theirs, mine)
    delta = jax.nn.softplus(delta_raw + bias)
    lower = jnp.tril(jnp.ones((length, length), single))
    running = jnp.einsum("tu,buh->bth", lower, delta * rate, precision=highest)
    inner_h = inner_act.reshape(seqs_dev, length, heads_here, HEADDIM)
    inner_f = inner_h.astype(single)
    weight_end = jnp.exp(running[:, -1:, :] - running) * delta
    carry_decay = jnp.exp(running[:, -1, :])
    growth = jnp.exp(running)
    inner_w = (inner_f * weight_end[..., None]).astype(half)
    local_state = jnp.einsum("bthp,btn->bhpn", inner_w, write_vec, preferred_element_type=single)
    entering = carry(carry_decay, local_state, n_seq, 1, 7)
    scores = jnp.einsum("btn,bun->btu", read_vec, write_vec, preferred_element_type=single)
    causal = jnp.arange(length)[:, None] >= jnp.arange(length)[None, :]
    by_head = jnp.transpose(running, (0, 2, 1))
    gap = by_head[:, :, :, None] - by_head[:, :, None, :]
    decays = jnp.exp(jnp.where(causal, gap, -jnp.inf))
    step_head = jnp.transpose(delta, (0, 2, 1))
    mixing_b = (scores[:, None] * decays * step_head[:, :, None, :]).astype(half)
    within = jnp.einsum("bhtu,buhp->bthp", mixing_b, inner_h, preferred_element_type=single)
    across = jnp.einsum("btn,bhpn->bthp", read_vec, entering, preferred_element_type=single)
    mixer_out = (within + growth[..., None] * across + skip[None, None, :, None] * inner_f).reshape(
        seqs_dev, length, inner_here
    )
    gate_act, gate_slope = swish_parts(gate_raw.astype(single))
    gated = mixer_out * gate_act
    upstream = cotangent.reshape(rows, width)
    grad_mixed = jnp.dot(upstream, out_weight, preferred_element_type=single).reshape(
        seqs_dev, length, inner_here
    )
    hat_gated = grad_mixed * postnorm
    sums = jnp.stack([jnp.sum(gated * gated, axis=-1), jnp.sum(hat_gated * gated, axis=-1)])
    lanes = sums.reshape(-1, 128)
    sums = (lanes + swap(lanes, 2)).reshape(sums.shape)
    squares, dots = sums[0], sums[1]
    gate_scale = lax.rsqrt(squares / INNER + epsilon)[..., None]
    mixed_flat = (gated * gate_scale * postnorm).astype(half).reshape(rows, inner_here)
    branch = lax.dot_general(
        mixed_flat, out_weight, (((1,), (1,)), ((), ())), preferred_element_type=single
    ).astype(half)
    output_grad = lax.dot_general(
        upstream, mixed_flat, (((0,), (0,)), ((), ())), preferred_element_type=single
    )
    postnorm_grad = jnp.sum(grad_mixed * gated * gate_scale, axis=(0, 1))
    cube = gate_scale * gate_scale * gate_scale
    grad_gated = gate_scale * hat_gated - gated * cube * (dots / INNER)[..., None]
    grad_mixer = (grad_gated * gate_act).reshape(seqs_dev, length, heads_here, HEADDIM)
    grad_gate = (grad_gated * mixer_out * gate_slope).astype(half).reshape(rows, inner_here)

    scaled = (grad_mixer * growth[..., None]).astype(half)
    pushed = jnp.einsum("bthp,btn->bhpn", scaled, read_vec, preferred_element_type=single)
    end_grad = carry(carry_decay, pushed, n_seq, -1, 8)

    grad_half = grad_mixer.astype(half)
    skip_grad = jnp.sum(grad_mixer * inner_f, axis=(0, 1, 3))
    grad_inner = skip[None, None, :, None] * grad_mixer + jnp.einsum(
        "bhtu,bthp->buhp", mixing_b, grad_half, preferred_element_type=single
    )
    grad_mix = jnp.einsum("bthp,buhp->bhtu", grad_half, inner_h, preferred_element_type=single)
    spread_mix = grad_mix * decays
    kernel = spread_mix * scores[:, None]
    grad_delta = jnp.transpose(jnp.sum(kernel, axis=2), (0, 2, 1))
    weighted = kernel * step_head[:, :, None, :]
    grad_running = jnp.transpose(jnp.sum(weighted, axis=3) - jnp.sum(weighted, axis=2), (0, 2, 1))
    grad_scores = jnp.sum(spread_mix * step_head[:, :, None, :], axis=1).astype(half)
    grad_read = jnp.einsum("btu,bun->btn", grad_scores, write_vec, preferred_element_type=single)
    grad_write = jnp.einsum("btu,btn->bun", grad_scores, read_vec, preferred_element_type=single)
    grad_running = grad_running + jnp.sum(grad_mixer * across, axis=3) * growth
    grad_read = grad_read + jnp.einsum(
        "bthp,bhpn->btn", scaled, entering, preferred_element_type=single
    )

    decay_grad = jnp.sum(end_grad.astype(single) * entering.astype(single), axis=(2, 3))
    end_extra = decay_grad * carry_decay
    grad_xw = jnp.einsum("bhpn,btn->bthp", end_grad, write_vec, preferred_element_type=single)
    grad_write = grad_write + jnp.einsum(
        "bhpn,bthp->btn", end_grad, inner_w, preferred_element_type=single
    )
    grad_inner = grad_inner + grad_xw * weight_end[..., None]
    grad_weight = jnp.sum(grad_xw * inner_f, axis=3)
    grad_delta = grad_delta + grad_weight * jnp.exp(running[:, -1:, :] - running)
    spread = grad_weight * weight_end
    end_extra = end_extra + jnp.sum(spread, axis=1)
    grad_running = grad_running - spread
    grad_running = jnp.concatenate(
        [grad_running[:, :-1], grad_running[:, -1:] + end_extra[:, None]], axis=1
    )
    grad_log = jnp.einsum("tu,bth->buh", lower, grad_running, precision=highest)

    grad_delta = grad_delta + grad_log * rate
    alog_grad = jnp.sum(grad_log * delta, axis=(0, 1)) * rate
    grad_delta_pre = grad_delta * jax.nn.sigmoid(delta_raw + bias)
    bias_grad = jnp.sum(grad_delta_pre, axis=(0, 1))
    kept = jnp.where(core == 0, grad_write, grad_read)
    given = jnp.where(core == 0, grad_read, grad_write)
    grad_select = kept + swap(given.reshape(rows, select_here), 4).reshape(kept.shape)
    grad_conv = jnp.concatenate(
        [grad_inner.reshape(seqs_dev, length, inner_here), grad_select], axis=2
    )
    taps_grad, conv_pad_grad = conv_back(conv_pad, taps, grad_conv * conv_slope)
    back = from_behind(conv_pad_grad[:, :lead], "seq", -1)
    conv_raw_grad = (
        jnp.concatenate(
            [conv_pad_grad[:, lead:length], conv_pad_grad[:, length:] + back], axis=1
        )
        .astype(half)
        .reshape(rows, -1)
    )
    grad_all = jnp.concatenate(
        [
            grad_gate,
            conv_raw_grad,
            grad_delta_pre.astype(half).reshape(rows, heads_here),
            jnp.zeros((rows, step_wide - heads_here), half),
        ],
        axis=1,
    )
    grad_part = lax.dot_general(
        grad_all, in_weight, (((1,), (1,)), ((), ())), preferred_element_type=single
    ).astype(half)
    in_grad = lax.dot_general(
        flat, grad_all, (((0,), (0,)), ((), ())), preferred_element_type=single
    )
    prenorm_part = jnp.sum(
        grad_part.astype(single).reshape(seqs_dev, length, width) * residual * entry_scale,
        axis=(0, 1),
    )
    gain_column = conv_end + heads_here
    packed_grad = jnp.concatenate(
        [
            in_grad.astype(half),
            output_grad.astype(half),
        ],
        axis=1,
    )
    tap_rows = filters.shape[0]
    scalars_local = jnp.stack([bias_grad, alog_grad, skip_grad])
    loose = jnp.concatenate([taps_grad[:, inner_here:].reshape(-1), scalars_local.reshape(-1)])
    small = jnp.concatenate(
        [
            taps_grad[:, :inner_here],
            postnorm_grad[None],
            jnp.pad(loose, (0, inner_here - loose.shape[0]))[None],
            prenorm_part[None],
        ],
        axis=0,
    )
    summed = lax.psum_scatter(
        packed_grad.astype(single), ("dp", "seq"), scatter_dimension=0, tiled=True
    )
    small = lax.psum(small, ("dp", "seq"))
    prenorm_grad = lax.psum(small[-1], "tensor")
    branch_far, part_far = swap(branch, 3), swap(grad_part, 5)
    own = lax.axis_index("dp") * n_seq + lax.axis_index("seq")
    prenorm_grad = lax.dynamic_slice_in_dim(prenorm_grad, own * own_rows, own_rows)
    branch = branch.astype(single) + branch_far.astype(single)
    result = residual + branch.reshape(seqs_dev, length, width)
    grad_part = grad_part.astype(single) + part_far.astype(single)
    grad_normed = grad_part.reshape(seqs_dev, length, width)
    hat = grad_normed * entry_gain
    hidden_grad = (
        cotangent.astype(single)
        + entry_scale * hat
        - residual
        * entry_scale
        * entry_scale
        * entry_scale
        * jnp.mean(hat * residual, axis=-1, keepdims=True)
    )
    loose_end = tap_rows * select_here
    grads = (
        summed[:, :inner_here],
        summed[:, inner_here : 2 * inner_here],
        summed[:, 2 * inner_here : conv_end],
        summed[:, conv_end:gain_column],
        summed[:, in_wide:].T,
        prenorm_grad,
        small[tap_rows],
        small[:tap_rows],
        small[tap_rows + 1, :loose_end].reshape(tap_rows, select_here),
        small[tap_rows + 1, loose_end : loose_end + 3 * heads_here].reshape(3, heads_here),
    )
    params = (
        gating,
        values,
        selector,
        timestep,
        output,
        prenorm,
        postnorm,
        filters,
        kernels,
        scalars,
    )
    moments = (
        gating_adam,
        values_adam,
        selector_adam,
        timestep_adam,
        output_adam,
        prenorm_adam,
        postnorm_adam,
        filters_adam,
        kernels_adam,
        scalars_adam,
    )
    updated = [adamw(param, moment, grad) for param, moment, grad in zip(params, moments, grads)]
    return (
        result,
        hidden_grad,
        grads[0],
        grads[1],
        grads[2],
        grads[3],
        grads[4],
        grads[5],
        grads[6],
        grads[7],
        grads[8],
        grads[9],
        updated[0][0],
        updated[1][0],
        updated[2][0],
        updated[3][0],
        updated[4][0],
        updated[5][0],
        updated[6][0],
        updated[7][0],
        updated[8][0],
        updated[9][0],
        updated[0][1],
        updated[1][1],
        updated[2][1],
        updated[3][1],
        updated[4][1],
        updated[5][1],
        updated[6][1],
        updated[7][1],
        updated[8][1],
        updated[9][1],
    )


def split(value, parts):
    pieces = []
    for _ in range(parts):
        piece = value.astype(jnp.bfloat16)
        pieces.append(piece)
        value = value - piece.astype(jnp.float32)
    return pieces


def mul(left, right):
    return jnp.dot(left, right, preferred_element_type=jnp.float32)


def mul_nt(left, right):
    return lax.dot_general(
        left, right, (((1,), (1,)), ((), ())), preferred_element_type=jnp.float32
    )


def mul_tn(left, right):
    return lax.dot_general(
        left, right, (((0,), (0,)), ((), ())), preferred_element_type=jnp.float32
    )


def wide_mul(value, table, parts):
    total = None
    for piece in split(value, parts):
        term = mul(piece, table)
        total = term if total is None else total + term
    return total


def table_mul(table, value, parts):
    total = None
    for piece in split(value, parts):
        term = mul(table, piece)
        total = term if total is None else total + term
    return total


def iota(shape, axis):
    return lax.broadcasted_iota(jnp.int32, shape, axis)


def each(count, step, body, start=None):
    def one(index, state):
        return body(pl.multiple_of(index * step, step), state)

    return lax.fori_loop(0, count, one, 0 if start is None else start)


def fold(value):
    rows, columns = value.shape
    return jnp.sum(value.reshape(rows // 8, 8, columns), axis=0)


class Table(NamedTuple):
    gat: object
    val: object
    sel: object
    hid: object
    cot: object
    outt: object
    pad: object
    spad: object
    ws: object
    wv: object
    wb: object
    wo: object
    scale: object
    normed: object
    raw: object
    draw: object
    delta: object
    run: object
    run3: object
    delta3: object
    scores_t: object
    wend: object
    runt: object
    deltat: object
    gdt: object
    growth: object
    ending: object
    x: object
    xw: object
    slope: object
    mine: object
    theirs: object
    bvec: object
    cvec: object
    scores: object
    local: object
    decay: object
    enter: object
    leave: object
    gend: object
    gout: object
    mixer: object
    across: object
    z: object
    gmix: object
    sums: object
    sums_far: object
    mixed: object
    gz: object
    gmh: object
    scaled: object
    gin: object
    gsc: object
    gdel: object
    seg: object
    gread: object
    kept: object
    given: object
    given_far: object
    gpre: object
    ga: object
    da: object
    db: object
    branch: object
    part: object
    branch_far: object
    part_far: object
    small: object
    zsmall: object
    dsmall: object
    tsmall: object
    rxa_a: object
    rya_a: object
    ryb_a: object
    rxb_a: object
    ta_a: object
    tb_a: object
    zb_a: object
    zin_a: object
    rxa_b: object
    rya_b: object
    ryb_b: object
    rxb_b: object
    ta_b: object
    tb_b: object
    zb_b: object
    zin_b: object
    sem_load: object
    sem_own: object
    sem_tail: object
    sem_swap: object
    sem_last: object
    sem_carry: object
    sem_zsmall: object
    sem_dsmall: object
    sem_gzs: object
    sem_gathers: object
    sem_gzv: object
    sem_gatherv: object
    sem_gzb: object
    sem_gatherb: object
    sem_gzo: object
    sem_gathero: object
    sem_reducea: object
    sem_rza: object
    sem_reduceb: object
    sem_rzb: object


def half(*shape):
    return pltpu.VMEM(shape, jnp.bfloat16)


def single(*shape):
    return pltpu.VMEM(shape, jnp.float32)


def dma(*shape):
    return pltpu.SemaphoreType.DMA(shape)


def plan(n, seqs, length, width, inner, pick, own, deep):
    rows = seqs * length
    total = seqs * inner
    first, second = inner + pick + LANES, 2 * inner
    return Table(
        gat=single(own, inner),
        val=single(own, inner),
        sel=single(own, pick),
        hid=half(rows, width),
        cot=half(rows, width),
        outt=single(own, inner),
        pad=single(LANES, LANES),
        spad=single(8, LANES),
        ws=half(4, n, own, pick + LANES),
        wv=half(4, n, own, inner),
        wb=half(4, n, own, inner),
        wo=half(4, n, own, inner),
        scale=single(rows, LANES),
        normed=half(rows, width),
        raw=single(seqs, length + 8, inner + pick),
        draw=single(rows, LANES),
        delta=single(rows, LANES),
        run=single(rows, LANES),
        run3=half(rows, 3 * LANES),
        delta3=half(rows, 3 * LANES),
        scores_t=single(rows, length),
        wend=single(rows, LANES),
        runt=single(seqs * 16, length),
        deltat=single(seqs * 16, length),
        gdt=single(LANES, length),
        growth=single(rows, inner),
        ending=single(rows, inner),
        x=half(rows, inner),
        xw=half(rows, inner),
        slope=single(rows, inner + pick),
        mine=half(rows, pick),
        theirs=half(rows, pick),
        bvec=half(rows, pick),
        cvec=half(rows, pick),
        scores=single(rows, length),
        local=single(total, deep),
        decay=single(total, deep),
        enter=half(total, deep),
        leave=half(total, deep),
        gend=half(total, deep),
        gout=half(total, deep),
        mixer=single(rows, inner),
        across=single(rows, inner),
        z=half(rows, inner),
        gmix=single(rows, inner),
        sums=single(rows, LANES),
        sums_far=single(rows, LANES),
        mixed=half(rows, inner),
        gz=half(rows, inner),
        gmh=half(rows, inner),
        scaled=half(rows, inner),
        gin=single(rows, inner),
        gsc=single(rows, length),
        gdel=single(rows, LANES),
        seg=single(rows, LANES),
        gread=single(rows, pick),
        kept=single(rows, pick),
        given=single(rows, pick),
        given_far=single(rows, pick),
        gpre=single(seqs, length + 8, inner + pick),
        ga=half(rows, first),
        da=half(2, 2, n, own, first),
        db=half(2, 2, n, own, second),
        branch=half(rows, width),
        part=half(rows, width),
        branch_far=half(rows, width),
        part_far=half(rows, width),
        small=single(56, LANES),
        zsmall=single(n, 56, LANES),
        dsmall=single(5, 56, LANES),
        tsmall=single(56, LANES),
        rxa_a=half(n, 2, own, first // 2),
        rya_a=half(n, own, first // 2),
        ryb_a=half(n, 2, own, first // 2),
        rxb_a=half(n, own, first // 2),
        ta_a=half(n, own, first // 2),
        tb_a=half(n, own, first // 2),
        zb_a=half(n - 1, own, first),
        zin_a=half(n - 1, own, first),
        rxa_b=half(n, 2, own, second // 2),
        rya_b=half(n, own, second // 2),
        ryb_b=half(n, 2, own, second // 2),
        rxb_b=half(n, own, second // 2),
        ta_b=half(n, own, second // 2),
        tb_b=half(n, own, second // 2),
        zb_b=half(n - 1, own, second),
        zin_b=half(n - 1, own, second),
        sem_load=dma(6),
        sem_own=dma(2),
        sem_tail=dma(4),
        sem_swap=dma(12),
        sem_last=dma(2),
        sem_carry=dma(4, PARTS),
        sem_zsmall=dma(2, n - 1),
        sem_dsmall=dma(2, 3),
        sem_gzs=dma(2, n - 1),
        sem_gathers=dma(8, n),
        sem_gzv=dma(2, n - 1),
        sem_gatherv=dma(8, n),
        sem_gzb=dma(2, n - 1),
        sem_gatherb=dma(8, n),
        sem_gzo=dma(2, n - 1),
        sem_gathero=dma(8, n),
        sem_reducea=dma(8, n),
        sem_rza=dma(2, n - 1),
        sem_reduceb=dma(8, n),
        sem_rzb=dma(2, n - 1),
    )


class Gather:
    def __init__(self, n, block, near, far, place):
        self.n, (self.d, self.s, x, y) = n, place
        self.xn, self.yn = y * 2 + (1 - x), (1 - y) * 2 + x
        self.block, self.near, self.far = block, near, far
        self.zf = [lax.rem(self.s + n - k, n) for k in range(n)]
        self.zt = [lax.rem(self.s + k, n) for k in range(n)]

    def deep(self, k):
        piece = self.block.at[self.d, self.s]
        sems = self.near.at[0, k - 1], self.near.at[1, k - 1]
        return send(piece, piece, *sems, {"seq": self.zt[k]})

    def side(self, j, axis):
        piece = self.block.at[self.d, self.zf[j]]
        sems = self.far.at[2 * axis, j], self.far.at[2 * axis + 1, j]
        return send(piece, piece, *sems, {"dp": (self.xn, self.yn)[axis]})

    def cross(self, j, axis):
        h = self.block.shape[3] // 2
        source, target = (self.yn, self.xn) if axis == 0 else (self.xn, self.yn)
        piece = self.block.at[source, self.zf[j], :, pl.ds(h if axis == 0 else 0, h)]
        sems = self.far.at[4 + 2 * axis, j], self.far.at[5 + 2 * axis, j]
        return send(piece, piece, *sems, {"dp": target})

    def begin(self):
        for k in range(1, self.n):
            self.deep(k).start()
        self.spread(0)

    def spread(self, j):
        if j:
            self.deep(j).wait_recv()
        self.side(j, 0).start()
        self.side(j, 1).start()

    def forward(self, j):
        self.side(j, 0).wait_recv()
        self.cross(j, 1).start()
        self.side(j, 1).wait_recv()
        self.cross(j, 0).start()

    def finish(self):
        for j in range(self.n):
            self.cross(j, 0).wait_recv()
            self.cross(j, 1).wait_recv()

    def close(self):
        for j in range(self.n):
            if j:
                self.deep(j).wait_send()
            for axis in range(2):
                self.side(j, axis).wait_send()
                self.cross(j, axis).wait_send()


class Reduce:
    def __init__(self, n, grad, bufs, sems, near, place):
        self.n, (self.d, self.s, self.x, self.y) = n, place
        self.grad, self.sems, self.near = grad, sems, near
        self.rxa, self.rya, self.ryb, self.rxb, self.ta, self.tb, self.zb, self.zin = bufs
        self.xn = self.y * 2 + (1 - self.x)
        self.yn = (1 - self.y) * 2 + self.x
        self.zt = [lax.rem(self.s + k, n) for k in range(n)]
        h = grad.shape[4] // 2
        self.left, self.right = pl.ds(0, h), pl.ds(h, h)
        self.order = list(range(1, n)) + [0]

    def copy(self, kind, j):
        sems = self.sems.at[2 * kind, j], self.sems.at[2 * kind + 1, j]
        z = self.zt[j]
        if kind == 0:
            source, target = self.grad.at[:, 1 - self.x, z, :, self.left], self.rxa.at[j]
        elif kind == 1:
            source, target = self.grad.at[1 - self.y, :, z, :, self.right], self.ryb.at[j]
        elif kind == 2:
            source, target = self.ta.at[j], self.rya.at[j]
        else:
            source, target = self.tb.at[j], self.rxb.at[j]
        return send(source, target, *sems, {"dp": self.xn if kind in (0, 3) else self.yn})

    def deep(self, j):
        sems = self.near.at[0, j - 1], self.near.at[1, j - 1]
        return send(self.zb.at[j - 1], self.zin.at[j - 1], *sems, {"seq": self.zt[j]})

    def launch(self, j):
        self.copy(0, j).start()
        self.copy(1, j).start()

    def begin(self):
        for j in self.order:
            self.launch(j)

    def middle(self, j):
        x, y, z = self.x, self.y, self.zt[j]
        single, half = jnp.float32, jnp.bfloat16
        self.copy(0, j).wait_recv()
        self.ta[j] = (
            self.grad[1 - y, x, z, :, self.left].astype(single)
            + self.rxa[j, 1 - y].astype(single)
        ).astype(half)
        self.copy(2, j).start()
        self.copy(1, j).wait_recv()
        self.tb[j] = (
            self.grad[y, 1 - x, z, :, self.right].astype(single)
            + self.ryb[j, 1 - x].astype(single)
        ).astype(half)
        self.copy(3, j).start()

    def join(self, j, out):
        x, y, z = self.x, self.y, self.zt[j]
        single, half = jnp.float32, jnp.bfloat16
        self.copy(2, j).wait_recv()
        low = (
            self.grad[y, x, z, :, self.left].astype(single)
            + self.rxa[j, y].astype(single)
            + self.rya[j].astype(single)
        )
        self.copy(3, j).wait_recv()
        high = (
            self.grad[y, x, z, :, self.right].astype(single)
            + self.ryb[j, x].astype(single)
            + self.rxb[j].astype(single)
        )
        if j == 0:
            out[:, self.left] = low
            out[:, self.right] = high
        else:
            self.zb[j - 1, :, self.left] = low.astype(half)
            self.zb[j - 1, :, self.right] = high.astype(half)
            self.deep(j).start()

    def finish(self, out):
        for j in range(1, self.n):
            self.deep(j).wait_recv()
            out[...] = out[...] + self.zin[j - 1].astype(jnp.float32)

    def close(self):
        for j in range(self.n):
            for kind in range(4):
                self.copy(kind, j).wait_send()
            if j:
                self.deep(j).wait_send()


def main_kernel(n, seqs, length, heads, *refs):
    inputs, refs = refs[:12], refs[12:]
    hid_h, cot_h, gat_h, val_h, sel_h, out_h = inputs[:6]
    step_ref, pre_ref, post_ref, filt_ref, kern_ref, scal_ref = inputs[6:]
    outputs, refs = refs[:5], refs[5:]
    suma_o, sumb_o, small_o, result_o, hidden_o = outputs
    r = Table(*refs)
    half, single = jnp.bfloat16, jnp.float32
    d, s = lax.axis_index("dp"), lax.axis_index("seq")
    core = lax.axis_index("tensor")
    y, x = d // 2, lax.rem(d, 2)
    place = (d, s, x, y)
    rows, width = r.hid.shape
    inner, pick = r.x.shape[1], r.mine.shape[1]
    conv = inner + pick
    pairs = inner // LANES
    deep = r.enter.shape[1]
    other = {"tensor": 1 - core}
    zt = [lax.rem(s + k, n) for k in range(n)]
    others = [{"dp": lax.rem(d + k, 4)} for k in range(1, 4)]
    after, before = {"seq": lax.rem(s + 1, n)}, {"seq": lax.rem(s + n - 1, n)}

    loads = [
        pltpu.make_async_copy(src, dst, r.sem_load.at[i])
        for i, (src, dst) in enumerate(
            [(sel_h, r.sel), (val_h, r.val), (hid_h, r.hid), (gat_h, r.gat), (out_h, r.outt), (cot_h, r.cot)]
        )
    ]
    for copy in loads:
        copy.start()
    own = r.val.shape[0]
    r.pad[...] = jnp.zeros(r.pad.shape, single)
    r.pad[:heads, :own] = step_ref[...]
    r.pad[heads : heads + 1, :own] = pre_ref[...].reshape(1, own)
    r.spad[...] = jnp.zeros(r.spad.shape, single)
    r.spad[:3, :heads] = scal_ref[...]
    ws, wv, wb, wo = r.ws, r.wv, r.wb, r.wo
    loads[0].wait()
    ws[d, s, :, :pick] = r.sel[...].astype(half)
    ws[d, s, :, pick:] = r.pad[...].T[:own].astype(half)
    loads[1].wait()
    wv[d, s] = r.val[...].astype(half)
    loads[3].wait()
    wb[d, s] = r.gat[...].astype(half)
    loads[4].wait()
    wo[d, s] = r.outt[...].astype(half)
    gs = Gather(n, ws, r.sem_gzs, r.sem_gathers, place)
    gv = Gather(n, wv, r.sem_gzv, r.sem_gatherv, place)
    gb = Gather(n, wb, r.sem_gzb, r.sem_gatherb, place)
    go = Gather(n, wo, r.sem_gzo, r.sem_gathero, place)
    greet([{"seq": zt[k]} for k in range(1, n)] + others + [other])
    gs.begin()
    gv.begin()
    loads[2].wait()
    loads[5].wait()
    tile = 32

    def scale_of(at, state):
        wide = r.hid[pl.ds(at, tile), :].astype(single)
        mean = jnp.sum(wide * wide, axis=1, keepdims=True) * (1.0 / width)
        r.scale[pl.ds(at, tile), :] = jnp.broadcast_to(
            lax.rsqrt(mean + epsilon), (tile, LANES)
        )
        return state

    each(rows // tile, tile, scale_of)

    heads_table = (iota((LANES, inner), 1) // HEADDIM == iota((LANES, inner), 0)).astype(half)
    table_heads = (iota((inner, LANES), 0) // HEADDIM == iota((inner, LANES), 1)).astype(half)
    lane = iota((1, LANES), 1)
    real = lane < heads
    bias = r.spad[0:1]
    rate = jnp.where(real, -jnp.exp(r.spad[1:2]), 0.0)
    skip = wide_mul(jnp.broadcast_to(r.spad[2:3], (8, LANES)), heads_table, 3)[0:1]
    post = post_ref[...].reshape(1, inner)

    for j in range(1, n):
        gs.spread(j)
        gs.forward(j - 1)
    gs.forward(n - 1)
    gv.spread(1)
    gb.begin()
    go.begin()
    gs.finish()

    step_t = ws[:, :, :, pick:].astype(single).reshape(width, LANES).T
    gain = step_t[heads : heads + 1, :]

    def norm_of(at, state):
        wide = r.hid[pl.ds(at, tile), :].astype(single)
        scale = r.scale[pl.ds(at, tile), 0:1]
        r.normed[pl.ds(at, tile), :] = (wide * scale * gain).astype(half)
        return state

    each(rows // tile, tile, norm_of)

    gv.spread(2)
    gv.forward(0)

    def weight_of(block, at, wide):
        return block[:, :, :, pl.ds(at, wide)].reshape(width, wide)

    tail = mul(r.normed[...], ws[...].reshape(width, pick + LANES))
    r.draw[...] = jnp.where(real, tail[:, pick:], 0.0)
    for q in range(seqs):
        r.raw[q, 8:, inner:] = (
            tail[q * length : (q + 1) * length, :pick].astype(half).astype(single)
        )

    gv.spread(3)
    gv.forward(1)

    low = (iota((length, length), 0) >= iota((length, length), 1)).astype(half)
    high = (iota((length, length), 0) <= iota((length, length), 1)).astype(half)
    cdecays = []
    for q in range(seqs):
        span = pl.ds(q * length, length)
        value = r.draw[span, :] + bias
        delta = jnp.maximum(value, 0.0) + jnp.log1p(jnp.exp(-jnp.abs(value)))
        delta = jnp.where(real, delta, 0.0)
        run = table_mul(low, delta * rate, 3)
        last = run[length - 1 : length, :]
        r.delta[span, :] = delta
        r.run[span, :] = run
        for target, whole in ((r.run3, run), (r.delta3, delta)):
            for i, piece in enumerate(split(whole, 3)):
                target[span, i * LANES : (i + 1) * LANES] = piece
        wend = jnp.exp(last - run) * delta
        r.wend[span, :] = wend
        r.runt[q * 16 : (q + 1) * 16, :] = run.T[:16]
        r.deltat[q * 16 : (q + 1) * 16, :] = delta.T[:16]
        cdecay = jnp.exp(last)
        cdecays.append(cdecay)
        pickrow = iota((inner, LANES), 0) // HEADDIM == iota((inner, LANES), 1)
        column = jnp.sum(jnp.where(pickrow, cdecay, 0.0), axis=1, keepdims=True)
        r.decay[q * inner : (q + 1) * inner, :] = jnp.broadcast_to(column, (inner, deep))
        r.growth[span, :] = wide_mul(jnp.exp(run), heads_table, 2)
        r.ending[span, :] = wide_mul(wend, heads_table, 2)

    gv.forward(2)
    gb.spread(1)
    gv.forward(3)
    gb.spread(2)
    gv.finish()

    def raw_of(at, state):
        value = mul(r.normed[...], weight_of(wv, at, 256)).astype(half).astype(single)
        for q in range(seqs):
            r.raw[q, 8:, pl.ds(at, 256)] = value[q * length : (q + 1) * length]
        return state

    each(inner // 256, 256, raw_of)

    tails = send(
        r.raw.at[:, pl.ds(length, 8)], r.raw.at[:, pl.ds(0, 8)],
        r.sem_tail.at[0], r.sem_tail.at[1], after,
    )

    @pl.when(s == 0)
    def _():
        r.raw[:, 0:8] = jnp.zeros((seqs, 8, conv), single)

    @pl.when(s != n - 1)
    def _():
        tails.start()

    gb.spread(3)
    gb.forward(0)
    gb.forward(1)
    go.spread(1)

    @pl.when(s != 0)
    def _():
        tails.wait_recv()

    def conv_of(first, wide):
        taps = [(kern_ref if first else filt_ref)[k : k + 1, :] for k in range(5)]
        for q in range(seqs):

            def one(at, state):
                padded = r.raw[q, pl.ds(at, tile + 8), first : first + wide]
                total = taps[4] + taps[3] * padded[8:]
                for k in range(3):
                    total = total + taps[k] * pltpu.roll(padded, 3 - k, 0)[8:]
                sigmoid = jax.nn.sigmoid(total)
                span = pl.ds(pl.multiple_of(q * length + at, tile), tile)
                act = (total * sigmoid).astype(half)
                if first:
                    r.mine[span, :] = act
                else:
                    r.x[span, :] = act
                    r.xw[span, :] = (act.astype(single) * r.ending[span, :]).astype(half)
                r.slope[span, first : first + wide] = sigmoid * (
                    1.0 + total * (1.0 - sigmoid)
                )
                return state

            each(length // tile, tile, one)

    conv_of(inner, pick)
    swaps = r.sem_swap
    trade = send(r.mine, r.theirs, swaps.at[0], swaps.at[1], other)
    trade.start()
    conv_of(0, inner)
    go.spread(2)
    gb.forward(2)
    trade.wait_recv()
    mine, theirs = r.mine[...], r.theirs[...]
    r.bvec[...] = jnp.where(core == 0, mine, theirs)
    r.cvec[...] = jnp.where(core == 0, theirs, mine)
    total = seqs * inner
    size = total // PARTS
    for q in range(seqs):
        span = pl.ds(q * length, length)
        r.local[q * inner : (q + 1) * inner, :] = mul_tn(r.xw[span, :], r.bvec[span, :])
        r.scores[span, :] = mul_nt(r.cvec[span, :], r.bvec[span, :])
        r.scores_t[span, :] = mul_nt(r.bvec[span, :], r.cvec[span, :])

    def carry_step(part, first, last, came, went, sem, target):
        span = pl.ds(pl.multiple_of(part * size, size), size)
        copy = send(
            went.at[span], came.at[span],
            r.sem_carry.at[sem, part], r.sem_carry.at[sem + 1, part], target,
        )

        @pl.when(s == first)
        def _():
            came[span, :] = jnp.zeros((size, deep), half)
            went[span, :] = r.local[span, :].astype(half)

        @pl.when(s != first)
        def _():
            copy.wait_recv()
            went[span, :] = (
                r.decay[span, :] * came[span, :].astype(single) + r.local[span, :]
            ).astype(half)

        @pl.when(s != last)
        def _():
            copy.start()

    def carry_close(last, came, went, sem, target):
        @pl.when(s != last)
        def _():
            for part in range(PARTS):
                span = pl.ds(part * size, size)
                send(
                    went.at[span], came.at[span],
                    r.sem_carry.at[sem, part], r.sem_carry.at[sem + 1, part], target,
                ).wait_send()

    causal = iota((length, length), 0) >= iota((length, length), 1)
    side = iota((1, LANES), 1) // HEADDIM

    def decays_of(q, h):
        span = pl.ds(pl.multiple_of(q * length, length), length)
        choose = ((iota((3 * LANES, LANES), 0) & (LANES - 1)) == h).astype(half)
        column = mul(r.run3[span, :], choose)
        row = r.runt[pl.ds(q * 16 + h, 1), :]
        gap = jnp.concatenate([column] * (length // LANES), axis=1) - row
        return jnp.exp(jnp.where(causal, gap, -1e30))

    def within_of(index, state):
        q, p = index // pairs, lax.rem(index, pairs)
        span = pl.ds(pl.multiple_of(q * length, length), length)
        lanes = pl.ds(pl.multiple_of(p * LANES, LANES), LANES)
        value = r.x[span, lanes]
        scores = r.scores[span, :]
        out = None
        for a in range(2):
            h = 2 * p + a
            step = r.deltat[pl.ds(q * 16 + h, 1), :]
            mixing = (scores * decays_of(q, h) * step).astype(half)
            term = mul(mixing, jnp.where(side == a, value, jnp.zeros_like(value)))
            out = term if out is None else out + term
        r.mixer[span, lanes] = out
        @pl.when(s != 0)
        def _():
            forth(index - lag)

        for at, pump in enumerate(pumps):
            pl.when(index == 3 * at + 1)(pump)
        return state

    def pump_b():
        gb.forward(3)
        go.spread(3)
        go.forward(0)

    def pump_c():
        go.forward(1)

    def pump_d():
        go.forward(2)

    pumps = [pump_b, pump_c, pump_d]
    lag = jnp.where(s == n - 1, PARTS, jnp.minimum(3 * s - 1, PARTS))

    def forth(part):
        @pl.when(part >= 0)
        def _():
            carry_step(part, 0, n - 1, r.enter, r.leave, 0, after)

    def forth_one(part, state):
        forth(part)
        return state

    @pl.when(s == 0)
    def _():
        lax.fori_loop(0, PARTS, forth_one, 0)

    lax.fori_loop(0, PARTS, within_of, 0)
    middle = jnp.where((s == n - 1) | (s == 0), 0, lag)
    lax.fori_loop(PARTS - middle, PARTS, forth_one, 0)
    go.forward(n - 1)
    gb.finish()

    def gate_of(at, state):
        r.z[:, pl.ds(at, 256)] = mul(r.normed[...], weight_of(wb, at, 256)).astype(half)
        return state

    each(inner // 256, 256, gate_of)
    go.finish()

    def down_of(at, state):
        r.gmix[:, pl.ds(at, 256)] = mul(r.cot[...], weight_of(wo, at, 256))
        return state

    each(inner // 256, 256, down_of)
    lax.fori_loop(jnp.where(s == n - 1, 0, PARTS), PARTS, forth_one, 0)

    trades = []
    for q in range(seqs):
        span = pl.ds(q * length, length)
        r.across[span, :] = mul_nt(
            r.cvec[span, :], r.enter[q * inner : (q + 1) * inner, :]
        )

        def mixer_of(at, state):
            span = pl.ds(pl.multiple_of(q * length + at, tile), tile)
            mixer = (
                r.mixer[span, :]
                + r.growth[span, :] * r.across[span, :]
                + skip * r.x[span, :].astype(single)
            )
            r.mixer[span, :] = mixer
            z = r.z[span, :].astype(single)
            gated = mixer * (z * jax.nn.sigmoid(z))
            squares = jnp.sum(gated * gated, axis=1, keepdims=True)
            dots = jnp.sum(r.gmix[span, :] * post * gated, axis=1, keepdims=True)
            r.sums[span, :] = jnp.where(lane == 0, squares, jnp.where(lane == 1, dots, 0.0))
            return state

        each(length // tile, tile, mixer_of)
        copy = send(
            r.sums.at[span], r.sums_far.at[span],
            swaps.at[2 + 2 * q], swaps.at[3 + 2 * q], other,
        )
        copy.start()
        trades.append(copy)

    full = 2 * inner

    def back_of(q):
        def one(at, state):
            span = pl.ds(pl.multiple_of(q * length + at, tile), tile)
            both = r.sums[span, :] + r.sums_far[span, :]
            scale = lax.rsqrt(both[:, 0:1] * (1.0 / full) + epsilon)
            dots = both[:, 1:2] * (1.0 / full)
            mixer, z = r.mixer[span, :], r.z[span, :].astype(single)
            sigmoid = jax.nn.sigmoid(z)
            act, slope = z * sigmoid, sigmoid * (1.0 + z * (1.0 - sigmoid))
            gated = mixer * act
            gmixed = r.gmix[span, :]
            r.mixed[span, :] = (gated * scale * post).astype(half)
            ggated = scale * (gmixed * post) - gated * (scale * scale * scale * dots)
            gmixer = ggated * act
            r.gz[span, :] = (ggated * mixer * slope).astype(half)
            r.gmh[span, :] = gmixer.astype(half)
            scaled = gmixer * r.growth[span, :]
            r.scaled[span, :] = scaled.astype(half)
            r.gmix[span, :] = gmixer
            r.across[span, :] = scaled * r.across[span, :]
            return (
                state[0] + fold(gmixed * gated * scale),
                state[1] + fold(gmixer * r.x[span, :].astype(single)),
            )

        return one

    state = (jnp.zeros((8, inner), single), jnp.zeros((8, inner), single))
    push = []
    for q in range(seqs):
        trades[q].wait_recv()
        state = each(length // tile, tile, back_of(q), state)
        span = pl.ds(q * length, length)
        r.local[q * inner : (q + 1) * inner, :] = mul_tn(r.scaled[span, :], r.cvec[span, :])

    def back(part):
        @pl.when((part >= 0) & (part < PARTS))
        def _():
            carry_step(part, n - 1, 0, r.gend, r.gout, 2, before)

    def back_one(part, state):
        back(part)
        return state

    @pl.when(s == n - 1)
    def _():
        lax.fori_loop(0, PARTS, back_one, 0)

    r.small[...] = jnp.zeros(r.small.shape, single)
    post_at = 5 * (conv // LANES)
    gain_at = post_at + inner // LANES
    head_at = gain_at + width // LANES

    def put(at, row):
        for c in range(row.shape[1] // LANES):
            r.small[at + c : at + c + 1, :] = row[:, c * LANES : (c + 1) * LANES]

    put(post_at, jnp.sum(state[0], axis=0, keepdims=True))
    r.small[head_at + 2 : head_at + 3, :] = jnp.sum(wide_mul(state[1], table_heads, 3), axis=0, keepdims=True)

    ra = Reduce(
        n, r.da, (r.rxa_a, r.rya_a, r.ryb_a, r.rxb_a, r.ta_a, r.tb_a, r.zb_a, r.zin_a),
        r.sem_reducea, r.sem_rza, place,
    )
    rb = Reduce(
        n, r.db, (r.rxa_b, r.rya_b, r.ryb_b, r.rxb_b, r.ta_b, r.tb_b, r.zb_b, r.zin_b),
        r.sem_reduceb, r.sem_rzb, place,
    )

    span_y = width // 2

    def grad_b(index, state):
        lanes = pl.ds(pl.multiple_of(index * span_y, span_y), span_y)
        own = r.db.shape[3]
        r.db[index, :, :, :, pl.ds(0, inner)] = (
            mul_tn(r.normed[:, lanes], r.gz[...]).astype(half).reshape(2, n, own, inner)
        )
        r.db[index, :, :, :, pl.ds(inner, inner)] = (
            mul_tn(r.cot[:, lanes], r.mixed[...]).astype(half).reshape(2, n, own, inner)
        )
        return state

    lax.fori_loop(0, 2, grad_b, 0)

    def branch_of(index, state):
        lanes = pl.ds(pl.multiple_of(index * span_y, span_y), span_y)
        weight = wo[pl.ds(2 * index, 2)].reshape(span_y, inner)
        r.branch[:, lanes] = mul_nt(r.mixed[...], weight).astype(half)
        return state

    lax.fori_loop(0, 2, branch_of, 0)
    far = [send(r.branch, r.branch_far, swaps.at[6], swaps.at[7], other)]
    far[0].start()

    r.gsc[...] = jnp.zeros(r.gsc.shape, single)
    r.gdel[...] = jnp.zeros(r.gdel.shape, single)
    r.gdt[...] = jnp.zeros(r.gdt.shape, single)

    later = iota((length, length), 0) <= iota((length, length), 1)

    def intra_of(index, state):
        q, p = index // pairs, lax.rem(index, pairs)
        span = pl.ds(pl.multiple_of(q * length, length), length)
        lanes = pl.ds(pl.multiple_of(p * LANES, LANES), LANES)
        value, upper = r.x[span, lanes], r.gmh[span, lanes]
        scores = r.scores_t[span, :]
        out = None
        for a in range(2):
            h = 2 * p + a
            choose = ((iota((3 * LANES, LANES), 0) & (LANES - 1)) == h).astype(half)
            column = mul(r.run3[span, :], choose)
            step = mul(r.delta3[span, :], choose)
            step = jnp.concatenate([step] * (length // LANES), axis=1)
            row = r.runt[pl.ds(q * 16 + h, 1), :]
            gap = row - jnp.concatenate([column] * (length // LANES), axis=1)
            decays = jnp.exp(jnp.where(later, gap, -1e30))
            masked = jnp.where(side == a, upper, jnp.zeros_like(upper))
            mixing = (scores * decays * step).astype(half)
            term = mul(mixing, masked)
            out = term if out is None else out + term
            spread = mul_nt(value, masked) * decays
            kernel = spread * scores
            fall = jnp.sum(kernel, axis=1, keepdims=True)
            r.gdel[span, :] += jnp.where(lane == h, fall, 0.0)
            r.gsc[span, :] += spread * step
            r.gdt[pl.ds(q * 16 + h, 1), :] = jnp.sum(kernel * step, axis=0, keepdims=True)
        r.gin[span, lanes] = out
        @pl.when(s != n - 1)
        def _():
            back(2 * (index - delay))
            back(2 * (index - delay) + 1)

        for at, j in enumerate(rb.order):

            @pl.when(index == at)
            def _():
                rb.launch(j)

        return state

    delay = 2 * (n - 2 - s)
    lax.fori_loop(0, PARTS, intra_of, 0)

    def gate_part(index, state):
        lanes = pl.ds(pl.multiple_of(index * span_y, span_y), span_y)
        gate = wb[pl.ds(2 * index, 2)].reshape(span_y, inner)
        r.mixer[:, lanes] = mul_nt(r.gz[...], gate)
        return state

    lax.fori_loop(0, 2, gate_part, 0)
    rb.middle(1)
    rb.middle(2)

    gdt = r.gdt[...].T
    bias_row, log_row = jnp.zeros((1, LANES), single), jnp.zeros((1, LANES), single)
    seg = [wide_mul(r.across[pl.ds(q * length, length), :], table_heads, 2) for q in range(seqs)]
    for q in range(seqs):
        span = pl.ds(q * length, length)
        states = pl.ds(q * inner, inner)
        r.across[span, :] = mul_nt(r.bvec[span, :], r.gend[states, :])
        r.gread[span, :] = mul(r.scaled[span, :], r.enter[states, :])
        gsc = r.gsc[span, :].astype(half)
        gread = r.gread[span, :] + mul_tn(gsc, r.bvec[span, :])
        gwrite = mul(gsc, r.cvec[span, :]) + mul(r.xw[span, :], r.gend[states, :])
        r.kept[span, :] = jnp.where(core == 0, gwrite, gread)
        r.given[span, :] = jnp.where(core == 0, gread, gwrite)
    trade2 = send(r.given, r.given_far, swaps.at[8], swaps.at[9], other)
    trade2.start()
    rb.middle(3)
    rb.middle(0)

    def inner_of(at, state):
        span = pl.ds(at, tile)
        back = r.across[span, :]
        total = (
            r.gin[span, :] + skip * r.gmix[span, :] + back * r.ending[span, :]
        )
        r.gin[span, :] = total
        r.across[span, :] = back * r.x[span, :].astype(single)
        return state

    each(rows // tile, tile, inner_of)

    for q in range(seqs):
        span = pl.ds(q * length, length)
        states = pl.ds(q * inner, inner)
        weight = wide_mul(r.across[span, :], table_heads, 2)
        product = r.gend[states, :].astype(single) * r.enter[states, :].astype(single)
        ones = jnp.ones((8, deep), half)
        across = sum(mul_nt(ones, piece) for piece in split(product, 2))
        end_row = wide_mul(across, table_heads, 3)[0:1] * cdecays[q]
        delta, run, wend = r.delta[span, :], r.run[span, :], r.wend[span, :]
        grun = jnp.where(
            lane < heads, pltpu.roll(gdt, LANES - 16 * q, 1) if q else gdt, 0.0
        )
        gdelta = r.gdel[span, :]
        grun = grun - delta * gdelta + seg[q]
        last = run[length - 1 : length, :]
        gdelta = gdelta + weight * jnp.exp(last - run)
        spread = weight * wend
        end_row = end_row + jnp.sum(spread, axis=0, keepdims=True)
        grun = grun - spread + jnp.where(iota((length, 1), 0) == length - 1, end_row, 0.0)
        glog = table_mul(high, grun, 3)
        gdelta = gdelta + glog * rate
        log_row = log_row + jnp.sum(glog * delta, axis=0, keepdims=True) * rate
        gdraw = jnp.where(real, gdelta * jax.nn.sigmoid(r.draw[span, :] + bias), 0.0)
        bias_row = bias_row + jnp.sum(gdraw, axis=0, keepdims=True)
        r.ga[span, conv:] = gdraw.astype(half)
    r.small[head_at : head_at + 1, :] = bias_row
    r.small[head_at + 1 : head_at + 2, :] = log_row

    trade2.wait_recv()
    for q in range(seqs):

        def pre_of(at, state):
            span = pl.ds(pl.multiple_of(q * length + at, tile), tile)
            r.gpre[q, pl.ds(at, tile), :inner] = r.gin[span, :] * r.slope[span, :inner]
            r.gpre[q, pl.ds(at, tile), inner:] = (
                r.kept[span, :] + r.given_far[span, :]
            ) * r.slope[span, inner:]
            return state

        each(length // tile, tile, pre_of)

    tails2 = send(
        r.gpre.at[:, pl.ds(0, 8)], r.gpre.at[:, pl.ds(length, 8)],
        r.sem_tail.at[2], r.sem_tail.at[3], before,
    )

    @pl.when(s == n - 1)
    def _():
        r.gpre[:, length:] = jnp.zeros((seqs, 8, conv), single)

    @pl.when(s != 0)
    def _():
        tails2.start()

    @pl.when(s != n - 1)
    def _():
        tails2.wait_recv()


    taps = [
        jnp.concatenate([filt_ref[k : k + 1, :], kern_ref[k : k + 1, :]], axis=1)
        for k in range(4)
    ]
    for q in range(seqs):

        def raw_grad(at, state):
            padded = r.gpre[q, pl.ds(at, tile + 8), :]
            total = taps[3] * padded[:tile]
            for k in range(3):
                total = total + taps[k] * pltpu.roll(padded, tile + 8 - (3 - k), 0)[:tile]
            span = pl.ds(pl.multiple_of(q * length + at, tile), tile)
            r.ga[span, :conv] = total.astype(half)
            return state

        each(length // tile, tile, raw_grad)

    def grad_a(index, state):
        lanes = pl.ds(pl.multiple_of(index * span_y, span_y), span_y)
        own, wide = r.da.shape[3:]
        r.da[index] = (
            mul_tn(r.normed[:, lanes], r.ga[...]).astype(half).reshape(2, n, own, wide)
        )
        return state

    lax.fori_loop(0, 2, grad_a, 0)
    ra.begin()

    def part_of(index, state):
        lanes = pl.ds(pl.multiple_of(index * span_y, span_y), span_y)
        block = pl.ds(2 * index, 2)
        value = wv[block].reshape(span_y, inner)
        select = ws[block].reshape(span_y, pick + LANES)
        r.part[:, lanes] = (
            r.mixer[:, lanes]
            + mul_nt(r.ga[:, :inner], value)
            + mul_nt(r.ga[:, inner:], select)
        ).astype(half)
        return state

    lax.fori_loop(0, 2, part_of, 0)
    far.append(send(r.part, r.part_far, swaps.at[10], swaps.at[11], other))
    far[1].start()

    def gain_of(at, state):
        span = pl.ds(at, tile)
        term = (
            r.part[span, :].astype(single)
            * r.hid[span, :].astype(single)
            * r.scale[span, 0:1]
        )
        return state + fold(term)

    gain_sum = each(rows // tile, tile, gain_of, jnp.zeros((8, width), single))
    put(gain_at, jnp.sum(gain_sum, axis=0, keepdims=True))

    taps_sum = tuple(jnp.zeros((8, conv), single) for _ in range(5))
    for q in range(seqs):

        def taps_of(at, state):
            pre = r.gpre[q, pl.ds(at, tile), :]
            padded = r.raw[q, pl.ds(at, tile + 8), :]
            terms = [pre * pltpu.roll(padded, 3 - k, 0)[8:] for k in range(3)]
            terms += [pre * padded[8:], pre]
            return tuple(total + fold(term) for total, term in zip(state, terms))

        taps_sum = each(length // tile, tile, taps_of, taps_sum)
    for k in range(5):
        put(k * (conv // LANES), jnp.sum(taps_sum[k], axis=0, keepdims=True))

    smalls = []
    for k in range(1, n):
        copy = send(
            r.small, r.zsmall.at[s],
            r.sem_zsmall.at[0, k - 1], r.sem_zsmall.at[1, k - 1], {"seq": zt[k]},
        )
        copy.start()
        smalls.append(copy)
    r.zsmall[s] = r.small[...]
    for j in rb.order:
        rb.join(j, sumb_o)
    far[0].wait_recv()
    far[1].wait_recv()

    def result_of(at, state):
        span = pl.ds(at, tile)
        wide = r.hid[span, :].astype(single)
        scale = r.scale[span, 0:1]
        r.gmix[span, :] = (
            wide + r.branch[span, :].astype(single) + r.branch_far[span, :].astype(single)
        )
        hat = (r.part[span, :].astype(single) + r.part_far[span, :].astype(single)) * gain
        dots = jnp.sum(hat * wide, axis=1, keepdims=True) * (1.0 / width)
        r.gin[span, :] = (
            r.cot[span, :].astype(single)
            + scale * hat
            - wide * (scale * scale * scale * dots)
        )
        return state

    each(rows // tile, tile, result_of)
    keep = [
        pltpu.make_async_copy(r.gmix, result_o, r.sem_own.at[0]),
        pltpu.make_async_copy(r.gin, hidden_o, r.sem_own.at[1]),
    ]
    for copy in keep:
        copy.start()
    for place_, j in enumerate(ra.order):
        ra.middle(j)
        if place_:
            ra.join(ra.order[place_ - 1], suma_o)
    ra.join(0, suma_o)
    for copy in smalls:
        copy.wait_recv()
    total_small = r.zsmall[0]
    for k in range(1, n):
        total_small = total_small + r.zsmall[k]
    r.dsmall[d] = total_small
    widely = []
    for k in range(3):
        copy = send(
            r.dsmall.at[d], r.dsmall.at[d],
            r.sem_dsmall.at[0, k], r.sem_dsmall.at[1, k], others[k],
        )
        copy.start()
        widely.append(copy)
    for copy in widely:
        copy.wait_recv()
    total_small = r.dsmall[0] + r.dsmall[1] + r.dsmall[2] + r.dsmall[3]
    r.dsmall[4] = total_small
    last_trade = send(r.dsmall.at[4], r.tsmall, r.sem_last.at[0], r.sem_last.at[1], other)
    last_trade.start()
    rb.finish(sumb_o)
    ra.finish(suma_o)
    last_trade.wait()

    def take(value, at, count):
        return jnp.concatenate([value[at + c : at + c + 1] for c in range(count)], axis=1)

    small_o[...] = jnp.zeros(small_o.shape, single)
    for k in range(5):
        at = k * (conv // LANES)
        small_o[k : k + 1, :] = take(total_small, at, conv // LANES)
    small_o[5:6, :inner] = take(total_small, post_at, inner // LANES)
    small_o[8:11, :LANES] = total_small[head_at : head_at + 3]
    both = total_small + r.tsmall[...]
    gains = jnp.broadcast_to(take(both, gain_at, width // LANES), (8, width))
    turn = lax.rem(width - (d * n + s) * own, width)
    small_o[7:8, :width] = pltpu.roll(gains, turn, 1)[0:1]

    for group in (gs, gv, gb, go):
        group.close()
    ra.close()
    rb.close()
    carry_close(n - 1, r.enter, r.leave, 0, after)
    carry_close(0, r.gend, r.gout, 2, before)

    @pl.when(s != n - 1)
    def _():
        tails.wait_send()

    @pl.when(s != 0)
    def _():
        tails2.wait_send()

    for copy in [trade, trade2] + trades:
        copy.wait_send()
    for copy in keep:
        copy.wait()
    for copy in far:
        copy.wait_send()
    for copy in smalls + widely:
        copy.wait_send()


def finish_kernel(heads, *refs):
    single = jnp.float32
    suma, sumb, small = refs[:3]
    tokens, weights, moments = refs[3:5], refs[5:15], refs[15:25]
    outputs, scratch = refs[25:57], refs[57:]
    weight_v, moment_v, grad_v, next_v, state_v = (
        scratch[:5], scratch[5:10], scratch[10:15], scratch[15:20], scratch[20:25]
    )
    sems = scratch[25:28]
    result_o, grad_o, next_o, state_o = (
        outputs[:2], outputs[2:12], outputs[12:22], outputs[22:32],
    )
    inner, pick = weight_v[0].shape[1], weight_v[2].shape[1]
    own = weight_v[0].shape[0]
    gone = []

    def leave(src, dst, sem):
        copy = pltpu.make_async_copy(src, dst, sem)
        copy.start()
        gone.append(copy)

    arrive = [
        [
            pltpu.make_async_copy(weights[i], weight_v[i], sems[0].at[0, i]),
            pltpu.make_async_copy(moments[i], moment_v[i], sems[0].at[1, i]),
        ]
        for i in range(5)
    ]
    for group in arrive:
        for copy in group:
            copy.start()
    token_v = scratch[28:]
    size = tokens[0].shape[0] // 2
    through = []
    for i in range(2):
        for k in range(2):
            span = pl.ds(k * size, size)
            copy = pltpu.make_async_copy(
                tokens[i].at[span], token_v[i].at[span], sems[1].at[0, 2 * i + k]
            )
            copy.start()
            through.append((copy, token_v[i].at[span], result_o[i].at[span]))

    def pass_on(at):
        copy, src, dst = through[at]
        copy.wait()
        leave(src, dst, sems[1].at[1, at])

    tall = jnp.concatenate([suma[:, inner + pick :], jnp.zeros((LANES - own, LANES), single)], axis=0).T
    grads = (sumb[:, :inner], suma[:, :inner], suma[:, inner : inner + pick], tall[:heads, :own], sumb[:, inner:])
    for i, grad in enumerate(grads):
        grad_v[i][...] = grad
        leave(grad_v[i], grad_o[i], sems[2].at[0, i])
    smalls = (
        small[7:8, :own],
        small[5:6, :inner],
        small[:5, :inner],
        small[:5, inner:],
        small[8:11, :heads],
    )
    for i, grad in enumerate(smalls):
        k = 5 + i
        flat = i < 2
        first_at = slice(0, 1) if flat else (slice(None), 0)
        second_at = slice(1, 2) if flat else (slice(None), 1)
        param = weights[k][...].reshape(grad.shape)
        fresh, first, second = step_of(param, moments[k][first_at], moments[k][second_at], grad)
        grad_o[k][...] = grad.reshape(grad_o[k].shape)
        next_o[k][...] = fresh.reshape(next_o[k].shape)
        state_o[k][first_at] = first
        state_o[k][second_at] = second
    pass_on(0)
    pass_on(1)
    for i, grad in enumerate(grads):
        for copy in arrive[i]:
            copy.wait()
        apart = i == 3
        first_at = (slice(None), 0) if apart else 0
        second_at = (slice(None), 1) if apart else 1
        fresh, first, second = step_of(
            weight_v[i][...], moment_v[i][first_at], moment_v[i][second_at], grad
        )
        next_v[i][...] = fresh
        state_v[i][first_at] = first
        state_v[i][second_at] = second
        leave(next_v[i], next_o[i], sems[2].at[1, i])
        leave(state_v[i], state_o[i], sems[2].at[2, i])
    pass_on(2)
    pass_on(3)
    for copy in gone:
        copy.wait()


def step_of(param, first, second, grad):
    first = first_decay * first + (1.0 - first_decay) * grad
    second = second_decay * second + (1.0 - second_decay) * grad * grad
    first_hat = first / (1.0 - first_decay**STEP)
    second_hat = second / (1.0 - second_decay**STEP)
    fresh = param - learn_rate * (
        first_hat / (jnp.sqrt(second_hat) + adam_epsilon) + weight_decay * param
    )
    return fresh, first, second


def fast(
    hidden, cotangent, gating, values, selector, timestep, output, prenorm, postnorm,
    filters, kernels, scalars, gating_adam, values_adam, selector_adam, timestep_adam,
    output_adam, prenorm_adam, postnorm_adam, filters_adam, kernels_adam, scalars_adam,
):
    half, single = jnp.bfloat16, jnp.float32
    n = lax.axis_size("seq")
    seqs, length, width = hidden.shape
    rows = seqs * length
    own, inner = gating.shape
    pick, heads = selector.shape[1], timestep.shape[1]
    conv = inner + pick
    scratch = plan(n, seqs, length, width, inner, pick, own, STATE)
    hid, cot = hidden.reshape(rows, width), cotangent.reshape(rows, width)
    shape = jax.ShapeDtypeStruct
    token = shape((rows, width), single)
    suma, sumb, small, *tokens = pl.pallas_call(
        functools.partial(main_kernel, n, seqs, length, heads),
        out_shape=(
            shape((own, conv + LANES), single),
            shape((own, 2 * inner), single),
            shape((16, conv), single),
            token,
            token,
        ),
        in_specs=[ANY] * 6 + [VMEM] * 6,
        out_specs=(VMEM,) * 3 + (ANY,) * 2,
        scratch_shapes=list(scratch),
        compiler_params=pltpu.CompilerParams(
            collective_id=0, has_side_effects=True, vmem_limit_bytes=VMEM_BYTES
        ),
    )(
        hid, cot, gating, values, selector, output.T, timestep.T, prenorm,
        postnorm, filters, kernels, scalars,
    )

    weights = (
        gating, values, selector, timestep.T, output.T, prenorm, postnorm,
        filters, kernels, scalars,
    )
    swapped = [jnp.transpose(m, (1, 0, 2)) for m in (filters_adam, kernels_adam, scalars_adam)]
    moments = (
        gating_adam, values_adam, selector_adam, jnp.transpose(timestep_adam, (2, 0, 1)),
        jnp.transpose(output_adam, (0, 2, 1)), prenorm_adam, postnorm_adam, *swapped,
    )
    out_shape = [shape((rows, width), single)] * 2
    out_shape += [shape(w.shape, single) for w in weights] * 2
    out_shape += [shape(m.shape, single) for m in moments]
    dma_shape = pltpu.SemaphoreType.DMA
    kinds = [ANY] * 5 + [VMEM] * 5
    done = pl.pallas_call(
        functools.partial(finish_kernel, heads),
        out_shape=out_shape,
        in_specs=[VMEM] * 3 + [ANY] * 2 + kinds * 2,
        out_specs=[ANY] * 2 + kinds * 3,
        scratch_shapes=[pltpu.VMEM(w.shape, single) for w in weights[:5]]
        + [pltpu.VMEM(m.shape, single) for m in moments[:5]]
        + [pltpu.VMEM(w.shape, single) for w in weights[:5]] * 2
        + [pltpu.VMEM(m.shape, single) for m in moments[:5]]
        + [dma_shape((2, 5)), dma_shape((2, 4)), dma_shape((3, 5))]
        + [pltpu.VMEM((rows, width), single)] * 2,
        compiler_params=pltpu.CompilerParams(vmem_limit_bytes=VMEM_BYTES),
    )(suma, sumb, small, *tokens, *weights, *moments)
    result, hidden_grad = (value.reshape(hidden.shape) for value in done[:2])

    def whole(group):
        big, tiny = group[:3], group[7:]
        return (*big, group[3].T, group[4].T, group[5], group[6], *tiny)

    states = done[22:]
    return (
        (result, hidden_grad)
        + whole(done[2:12])
        + whole(done[12:22])
        + (
            *states[:3],
            jnp.transpose(states[3], (1, 2, 0)),
            jnp.transpose(states[4], (0, 2, 1)),
            *states[5:7],
            *(jnp.transpose(m, (1, 0, 2)) for m in states[7:]),
        )
    )


def shards(*arrays):
    if (lax.axis_size("dp"), lax.axis_size("seq")) == (4, 4):
        return fast(*arrays)
    return general(*arrays)


def solution(mesh):
    placed = (
        P("dp", "seq", None),
        P("dp", "seq", None),
        P(("dp", "seq"), "tensor"),
        P(("dp", "seq"), "tensor"),
        P(("dp", "seq"), "tensor"),
        P(("dp", "seq"), "tensor"),
        P("tensor", ("dp", "seq")),
        P(("dp", "seq")),
        P("tensor"),
        P(None, "tensor"),
        P(None, "tensor"),
        P(None, "tensor"),
        P(None, ("dp", "seq"), "tensor"),
        P(None, ("dp", "seq"), "tensor"),
        P(None, ("dp", "seq"), "tensor"),
        P(None, ("dp", "seq"), "tensor"),
        P(None, "tensor", ("dp", "seq")),
        P(None, ("dp", "seq")),
        P(None, "tensor"),
        P(None, None, "tensor"),
        P(None, None, "tensor"),
        P(None, None, "tensor"),
    )
    return jax.shard_map(
        shards,
        mesh=mesh,
        in_specs=placed,
        out_specs=(
            P("dp", "seq", None),
            P("dp", "seq", None),
            P(("dp", "seq"), "tensor"),
            P(("dp", "seq"), "tensor"),
            P(("dp", "seq"), "tensor"),
            P(("dp", "seq"), "tensor"),
            P("tensor", ("dp", "seq")),
            P(("dp", "seq")),
            P("tensor"),
            P(None, "tensor"),
            P(None, "tensor"),
            P(None, "tensor"),
            P(("dp", "seq"), "tensor"),
            P(("dp", "seq"), "tensor"),
            P(("dp", "seq"), "tensor"),
            P(("dp", "seq"), "tensor"),
            P("tensor", ("dp", "seq")),
            P(("dp", "seq")),
            P("tensor"),
            P(None, "tensor"),
            P(None, "tensor"),
            P(None, "tensor"),
            P(None, ("dp", "seq"), "tensor"),
            P(None, ("dp", "seq"), "tensor"),
            P(None, ("dp", "seq"), "tensor"),
            P(None, ("dp", "seq"), "tensor"),
            P(None, "tensor", ("dp", "seq")),
            P(None, ("dp", "seq")),
            P(None, "tensor"),
            P(None, None, "tensor"),
            P(None, None, "tensor"),
            P(None, None, "tensor"),
        ),
        check_vma=False,
    )
```

```python
import functools
from typing import NamedTuple
import jax
import jax.numpy as jnp
from jax import lax
from jax.experimental import pallas as pl
from jax.experimental.pallas import tpu as pltpu
from jax.sharding import PartitionSpec as P

INNER = 1536
STATE = 128
HEADDIM = 64
STEP = 2


epsilon = 1e-05
highest = lax.Precision.HIGHEST
learn_rate = 0.01
first_decay = 0.9
second_decay = 0.999
adam_epsilon = 1e-08
weight_decay = 0.1


def from_behind(block, axis, distance):
    devices = range(lax.axis_size(axis))
    route = [(i - distance, i) for i in devices if i - distance in devices]
    return lax.ppermute(block, axis, route)


MESH = pl.DeviceIdType.MESH
VMEM = pl.BlockSpec(memory_space=pltpu.VMEM)
ANY = pl.BlockSpec(memory_space=pl.ANY)
LANES = 128
PARTS = 12
VMEM_BYTES = 60 * 2**20


def send(src, dst, send_sem, recv_sem, device):
    return pltpu.make_async_remote_copy(
        src_ref=src,
        dst_ref=dst,
        send_sem=send_sem,
        recv_sem=recv_sem,
        device_id=device,
        device_id_type=MESH,
    )


def greet(devices):
    barrier = pltpu.get_barrier_semaphore()
    for device in devices:
        pl.semaphore_signal(barrier, inc=1, device_id=device, device_id_type=MESH)
    pl.semaphore_wait(barrier, len(devices))


def params_of(collective_id):
    return pltpu.CompilerParams(collective_id=collective_id, has_side_effects=True)


def swap_kernel(x_ref, o_ref, send_sem, recv_sem):
    other = {"tensor": 1 - lax.axis_index("tensor")}
    greet([other])
    copy = send(x_ref, o_ref, send_sem, recv_sem, other)
    copy.start()
    copy.wait()


def swap(value, collective_id):
    return pl.pallas_call(
        swap_kernel,
        out_shape=jax.ShapeDtypeStruct(value.shape, value.dtype),
        in_specs=[VMEM],
        out_specs=VMEM,
        scratch_shapes=[pltpu.SemaphoreType.DMA, pltpu.SemaphoreType.DMA],
        compiler_params=params_of(collective_id),
    )(value)


def carry_kernel(count, step, parts, decay_ref, local_ref, o_ref, out_buf, in_buf, send_sem, recv_sem):
    me = lax.axis_index("seq")
    target = lax.rem(me + count + step, count)
    source = lax.rem(me + count - step, count)
    first, last = (0, count - 1) if step > 0 else (count - 1, 0)
    greet([{"seq": target}, {"seq": source}])
    size = local_ref.shape[0] // parts

    def copy_of(part):
        return send(
            out_buf.at[part],
            in_buf.at[part],
            send_sem.at[part],
            recv_sem.at[part],
            {"seq": target},
        )

    for part in range(parts):
        rows = pl.ds(part * size, size)

        @pl.when(me == first)
        def _():
            o_ref[rows] = jnp.zeros((size,) + o_ref.shape[1:], o_ref.dtype)
            out_buf[part] = local_ref[rows].astype(jnp.bfloat16)

        @pl.when(me != first)
        def _():
            copy_of(part).wait_recv()
            entering = in_buf[part]
            o_ref[rows] = entering
            out_buf[part] = (
                decay_ref[rows] * entering.astype(jnp.float32) + local_ref[rows]
            ).astype(jnp.bfloat16)

        @pl.when(me != last)
        def _():
            copy_of(part).start()

    @pl.when(me != last)
    def _():
        for part in range(parts):
            copy_of(part).wait_send()


def carry(decay, local, count, step, collective_id):
    seqs, heads, wide, deep = local.shape
    total = seqs * heads
    parts = 6 if total % 6 == 0 else 1
    size = total // parts
    spread = jnp.broadcast_to(decay.reshape(total, 1, 1), (total, 1, deep))
    result = pl.pallas_call(
        functools.partial(carry_kernel, count, step, parts),
        out_shape=jax.ShapeDtypeStruct((total, wide, deep), jnp.bfloat16),
        in_specs=[VMEM, VMEM],
        out_specs=VMEM,
        scratch_shapes=[
            pltpu.VMEM((parts, size, wide, deep), jnp.bfloat16),
            pltpu.VMEM((parts, size, wide, deep), jnp.bfloat16),
            pltpu.SemaphoreType.DMA((parts,)),
            pltpu.SemaphoreType.DMA((parts,)),
        ],
        compiler_params=params_of(collective_id),
    )(spread, local.reshape(total, wide, deep))
    return result.reshape(local.shape)


def swish_parts(value):
    sigmoid = jax.nn.sigmoid(value)
    return (value * sigmoid, sigmoid * (1.0 + value * (1.0 - sigmoid)))


def conv_apply(padded, taps):
    tap_count = taps.shape[0] - 1
    length = padded.shape[1] - tap_count + 1
    wide = padded.astype(jnp.float32)
    total = taps[tap_count] + taps[0] * wide[:, 0:length]
    for index in range(1, tap_count):
        total = total + taps[index] * wide[:, index : index + length]
    return total


def conv_back(padded, taps, grad_pre):
    tap_count = taps.shape[0] - 1
    length = grad_pre.shape[1]
    wide = padded.astype(jnp.float32)
    tap_rows = [
        jnp.sum(grad_pre * wide[:, index : index + length], axis=(0, 1))
        for index in range(tap_count)
    ]
    tap_rows.append(jnp.sum(grad_pre, axis=(0, 1)))
    grad_pad = jnp.zeros(padded.shape, jnp.float32)
    for index in range(tap_count):
        grad_pad = grad_pad + jnp.pad(
            taps[index] * grad_pre, ((0, 0), (index, tap_count - 1 - index), (0, 0))
        )
    return (jnp.stack(tap_rows), grad_pad)


def adamw(param, moments, grad):
    first = first_decay * moments[0] + (1.0 - first_decay) * grad
    second = second_decay * moments[1] + (1.0 - second_decay) * grad * grad
    first_hat = first / (1.0 - first_decay**STEP)
    second_hat = second / (1.0 - second_decay**STEP)
    fresh = param - learn_rate * (
        first_hat / (jnp.sqrt(second_hat) + adam_epsilon) + weight_decay * param
    )
    return (fresh, jnp.stack([first, second]))


def general(
    hidden,
    cotangent,
    gating,
    values,
    selector,
    timestep,
    output,
    prenorm,
    postnorm,
    filters,
    kernels,
    scalars,
    gating_adam,
    values_adam,
    selector_adam,
    timestep_adam,
    output_adam,
    prenorm_adam,
    postnorm_adam,
    filters_adam,
    kernels_adam,
    scalars_adam,
):
    half = jnp.bfloat16
    single = jnp.float32
    n_seq = lax.axis_size("seq")
    core = lax.axis_index("tensor")
    seqs_dev, length, width = hidden.shape
    rows = seqs_dev * length
    own_rows = gating.shape[0]
    lead = filters.shape[0] - 2
    heads_here = timestep.shape[1]
    inner_here = gating.shape[1]
    select_here = selector.shape[1]
    conv_end = 2 * inner_here + select_here
    step_wide = 128
    in_wide = conv_end + step_wide
    packed = jnp.concatenate(
        [
            gating.astype(half),
            values.astype(half),
            selector.astype(half),
            timestep.astype(half),
            prenorm.astype(half)[:, None],
            jnp.zeros((own_rows, step_wide - heads_here - 1), half),
            output.T.astype(half),
        ],
        axis=1,
    )
    weights = lax.all_gather(packed, ("dp", "seq"), axis=0, tiled=True)
    in_weight = weights[:, :in_wide]
    out_weight = weights[:, in_wide:]
    bias = scalars[0]
    rate = -jnp.exp(scalars[1])
    skip = scalars[2]
    entry_gain = weights[:, conv_end + heads_here].astype(single)
    residual = hidden.astype(single)
    entry_scale = lax.rsqrt(jnp.mean(residual * residual, axis=-1, keepdims=True) + epsilon)
    normed = (residual * entry_scale * entry_gain).astype(half)
    flat = normed.reshape(rows, width)
    raw = jnp.dot(flat, in_weight, preferred_element_type=single)
    gate_raw = raw[:, :inner_here].astype(half).reshape(seqs_dev, length, inner_here)
    conv_raw = raw[:, inner_here:conv_end].astype(half).reshape(seqs_dev, length, -1)
    delta_raw = raw[:, conv_end : conv_end + heads_here].reshape(seqs_dev, length, heads_here)
    tails = from_behind(conv_raw[:, length - lead :], "seq", 1)
    conv_pad = jnp.concatenate([tails, conv_raw], axis=1)
    taps = jnp.concatenate([filters, kernels], axis=1)
    conv_value, conv_slope = swish_parts(conv_apply(conv_pad, taps))
    conv_act = conv_value.astype(half)
    inner_act = conv_act[:, :, :inner_here]
    mine = conv_act[:, :, inner_here:]
    theirs = swap(mine.reshape(rows, select_here), 1).reshape(mine.shape)
    write_vec = jnp.where(core == 0, mine, theirs)
    read_vec = jnp.where(core == 0, theirs, mine)
    delta = jax.nn.softplus(delta_raw + bias)
    lower = jnp.tril(jnp.ones((length, length), single))
    running = jnp.einsum("tu,buh->bth", lower, delta * rate, precision=highest)
    inner_h = inner_act.reshape(seqs_dev, length, heads_here, HEADDIM)
    inner_f = inner_h.astype(single)
    weight_end = jnp.exp(running[:, -1:, :] - running) * delta
    carry_decay = jnp.exp(running[:, -1, :])
    growth = jnp.exp(running)
    inner_w = (inner_f * weight_end[..., None]).astype(half)
    local_state = jnp.einsum("bthp,btn->bhpn", inner_w, write_vec, preferred_element_type=single)
    entering = carry(carry_decay, local_state, n_seq, 1, 7)
    scores = jnp.einsum("btn,bun->btu", read_vec, write_vec, preferred_element_type=single)
    causal = jnp.arange(length)[:, None] >= jnp.arange(length)[None, :]
    by_head = jnp.transpose(running, (0, 2, 1))
    gap = by_head[:, :, :, None] - by_head[:, :, None, :]
    decays = jnp.exp(jnp.where(causal, gap, -jnp.inf))
    step_head = jnp.transpose(delta, (0, 2, 1))
    mixing_b = (scores[:, None] * decays * step_head[:, :, None, :]).astype(half)
    within = jnp.einsum("bhtu,buhp->bthp", mixing_b, inner_h, preferred_element_type=single)
    across = jnp.einsum("btn,bhpn->bthp", read_vec, entering, preferred_element_type=single)
    mixer_out = (within + growth[..., None] * across + skip[None, None, :, None] * inner_f).reshape(
        seqs_dev, length, inner_here
    )
    gate_act, gate_slope = swish_parts(gate_raw.astype(single))
    gated = mixer_out * gate_act
    upstream = cotangent.reshape(rows, width)
    grad_mixed = jnp.dot(upstream, out_weight, preferred_element_type=single).reshape(
        seqs_dev, length, inner_here
    )
    hat_gated = grad_mixed * postnorm
    sums = jnp.stack([jnp.sum(gated * gated, axis=-1), jnp.sum(hat_gated * gated, axis=-1)])
    lanes = sums.reshape(-1, 128)
    sums = (lanes + swap(lanes, 2)).reshape(sums.shape)
    squares, dots = sums[0], sums[1]
    gate_scale = lax.rsqrt(squares / INNER + epsilon)[..., None]
    mixed_flat = (gated * gate_scale * postnorm).astype(half).reshape(rows, inner_here)
    branch = lax.dot_general(
        mixed_flat, out_weight, (((1,), (1,)), ((), ())), preferred_element_type=single
    ).astype(half)
    output_grad = lax.dot_general(
        upstream, mixed_flat, (((0,), (0,)), ((), ())), preferred_element_type=single
    )
    postnorm_grad = jnp.sum(grad_mixed * gated * gate_scale, axis=(0, 1))
    cube = gate_scale * gate_scale * gate_scale
    grad_gated = gate_scale * hat_gated - gated * cube * (dots / INNER)[..., None]
    grad_mixer = (grad_gated * gate_act).reshape(seqs_dev, length, heads_here, HEADDIM)
    grad_gate = (grad_gated * mixer_out * gate_slope).astype(half).reshape(rows, inner_here)

    scaled = (grad_mixer * growth[..., None]).astype(half)
    pushed = jnp.einsum("bthp,btn->bhpn", scaled, read_vec, preferred_element_type=single)
    end_grad = carry(carry_decay, pushed, n_seq, -1, 8)

    grad_half = grad_mixer.astype(half)
    skip_grad = jnp.sum(grad_mixer * inner_f, axis=(0, 1, 3))
    grad_inner = skip[None, None, :, None] * grad_mixer + jnp.einsum(
        "bhtu,bthp->buhp", mixing_b, grad_half, preferred_element_type=single
    )
    grad_mix = jnp.einsum("bthp,buhp->bhtu", grad_half, inner_h, preferred_element_type=single)
    spread_mix = grad_mix * decays
    kernel = spread_mix * scores[:, None]
    grad_delta = jnp.transpose(jnp.sum(kernel, axis=2), (0, 2, 1))
    weighted = kernel * step_head[:, :, None, :]
    grad_running = jnp.transpose(jnp.sum(weighted, axis=3) - jnp.sum(weighted, axis=2), (0, 2, 1))
    grad_scores = jnp.sum(spread_mix * step_head[:, :, None, :], axis=1).astype(half)
    grad_read = jnp.einsum("btu,bun->btn", grad_scores, write_vec, preferred_element_type=single)
    grad_write = jnp.einsum("btu,btn->bun", grad_scores, read_vec, preferred_element_type=single)
    grad_running = grad_running + jnp.sum(grad_mixer * across, axis=3) * growth
    grad_read = grad_read + jnp.einsum(
        "bthp,bhpn->btn", scaled, entering, preferred_element_type=single
    )

    decay_grad = jnp.sum(end_grad.astype(single) * entering.astype(single), axis=(2, 3))
    end_extra = decay_grad * carry_decay
    grad_xw = jnp.einsum("bhpn,btn->bthp", end_grad, write_vec, preferred_element_type=single)
    grad_write = grad_write + jnp.einsum(
        "bhpn,bthp->btn", end_grad, inner_w, preferred_element_type=single
    )
    grad_inner = grad_inner + grad_xw * weight_end[..., None]
    grad_weight = jnp.sum(grad_xw * inner_f, axis=3)
    grad_delta = grad_delta + grad_weight * jnp.exp(running[:, -1:, :] - running)
    spread = grad_weight * weight_end
    end_extra = end_extra + jnp.sum(spread, axis=1)
    grad_running = grad_running - spread
    grad_running = jnp.concatenate(
        [grad_running[:, :-1], grad_running[:, -1:] + end_extra[:, None]], axis=1
    )
    grad_log = jnp.einsum("tu,bth->buh", lower, grad_running, precision=highest)

    grad_delta = grad_delta + grad_log * rate
    alog_grad = jnp.sum(grad_log * delta, axis=(0, 1)) * rate
    grad_delta_pre = grad_delta * jax.nn.sigmoid(delta_raw + bias)
    bias_grad = jnp.sum(grad_delta_pre, axis=(0, 1))
    kept = jnp.where(core == 0, grad_write, grad_read)
    given = jnp.where(core == 0, grad_read, grad_write)
    grad_select = kept + swap(given.reshape(rows, select_here), 4).reshape(kept.shape)
    grad_conv = jnp.concatenate(
        [grad_inner.reshape(seqs_dev, length, inner_here), grad_select], axis=2
    )
    taps_grad, conv_pad_grad = conv_back(conv_pad, taps, grad_conv * conv_slope)
    back = from_behind(conv_pad_grad[:, :lead], "seq", -1)
    conv_raw_grad = (
        jnp.concatenate(
            [conv_pad_grad[:, lead:length], conv_pad_grad[:, length:] + back], axis=1
        )
        .astype(half)
        .reshape(rows, -1)
    )
    grad_all = jnp.concatenate(
        [
            grad_gate,
            conv_raw_grad,
            grad_delta_pre.astype(half).reshape(rows, heads_here),
            jnp.zeros((rows, step_wide - heads_here), half),
        ],
        axis=1,
    )
    grad_part = lax.dot_general(
        grad_all, in_weight, (((1,), (1,)), ((), ())), preferred_element_type=single
    ).astype(half)
    in_grad = lax.dot_general(
        flat, grad_all, (((0,), (0,)), ((), ())), preferred_element_type=single
    )
    prenorm_part = jnp.sum(
        grad_part.astype(single).reshape(seqs_dev, length, width) * residual * entry_scale,
        axis=(0, 1),
    )
    gain_column = conv_end + heads_here
    packed_grad = jnp.concatenate(
        [
            in_grad.astype(half),
            output_grad.astype(half),
        ],
        axis=1,
    )
    tap_rows = filters.shape[0]
    scalars_local = jnp.stack([bias_grad, alog_grad, skip_grad])
    loose = jnp.concatenate([taps_grad[:, inner_here:].reshape(-1), scalars_local.reshape(-1)])
    small = jnp.concatenate(
        [
            taps_grad[:, :inner_here],
            postnorm_grad[None],
            jnp.pad(loose, (0, inner_here - loose.shape[0]))[None],
            prenorm_part[None],
        ],
        axis=0,
    )
    summed = lax.psum_scatter(
        packed_grad.astype(single), ("dp", "seq"), scatter_dimension=0, tiled=True
    )
    small = lax.psum(small, ("dp", "seq"))
    prenorm_grad = lax.psum(small[-1], "tensor")
    branch_far, part_far = swap(branch, 3), swap(grad_part, 5)
    own = lax.axis_index("dp") * n_seq + lax.axis_index("seq")
    prenorm_grad = lax.dynamic_slice_in_dim(prenorm_grad, own * own_rows, own_rows)
    branch = branch.astype(single) + branch_far.astype(single)
    result = residual + branch.reshape(seqs_dev, length, width)
    grad_part = grad_part.astype(single) + part_far.astype(single)
    grad_normed = grad_part.reshape(seqs_dev, length, width)
    hat = grad_normed * entry_gain
    hidden_grad = (
        cotangent.astype(single)
        + entry_scale * hat
        - residual
        * entry_scale
        * entry_scale
        * entry_scale
        * jnp.mean(hat * residual, axis=-1, keepdims=True)
    )
    loose_end = tap_rows * select_here
    grads = (
        summed[:, :inner_here],
        summed[:, inner_here : 2 * inner_here],
        summed[:, 2 * inner_here : conv_end],
        summed[:, conv_end:gain_column],
        summed[:, in_wide:].T,
        prenorm_grad,
        small[tap_rows],
        small[:tap_rows],
        small[tap_rows + 1, :loose_end].reshape(tap_rows, select_here),
        small[tap_rows + 1, loose_end : loose_end + 3 * heads_here].reshape(3, heads_here),
    )
    params = (
        gating,
        values,
        selector,
        timestep,
        output,
        prenorm,
        postnorm,
        filters,
        kernels,
        scalars,
    )
    moments = (
        gating_adam,
        values_adam,
        selector_adam,
        timestep_adam,
        output_adam,
        prenorm_adam,
        postnorm_adam,
        filters_adam,
        kernels_adam,
        scalars_adam,
    )
    updated = [adamw(param, moment, grad) for param, moment, grad in zip(params, moments, grads)]
    return (
        result,
        hidden_grad,
        grads[0],
        grads[1],
        grads[2],
        grads[3],
        grads[4],
        grads[5],
        grads[6],
        grads[7],
        grads[8],
        grads[9],
        updated[0][0],
        updated[1][0],
        updated[2][0],
        updated[3][0],
        updated[4][0],
        updated[5][0],
        updated[6][0],
        updated[7][0],
        updated[8][0],
        updated[9][0],
        updated[0][1],
        updated[1][1],
        updated[2][1],
        updated[3][1],
        updated[4][1],
        updated[5][1],
        updated[6][1],
        updated[7][1],
        updated[8][1],
        updated[9][1],
    )


def split(value, parts):
    pieces = []
    for _ in range(parts):
        piece = value.astype(jnp.bfloat16)
        pieces.append(piece)
        value = value - piece.astype(jnp.float32)
    return pieces


def mul(left, right):
    return jnp.dot(left, right, preferred_element_type=jnp.float32)


def mul_nt(left, right):
    return lax.dot_general(
        left, right, (((1,), (1,)), ((), ())), preferred_element_type=jnp.float32
    )


def mul_tn(left, right):
    return lax.dot_general(
        left, right, (((0,), (0,)), ((), ())), preferred_element_type=jnp.float32
    )


def wide_mul(value, table, parts):
    total = None
    for piece in split(value, parts):
        term = mul(piece, table)
        total = term if total is None else total + term
    return total


def table_mul(table, value, parts):
    total = None
    for piece in split(value, parts):
        term = mul(table, piece)
        total = term if total is None else total + term
    return total


def iota(shape, axis):
    return lax.broadcasted_iota(jnp.int32, shape, axis)


def each(count, step, body, start=None):
    def one(index, state):
        return body(pl.multiple_of(index * step, step), state)

    return lax.fori_loop(0, count, one, 0 if start is None else start)


def fold(value):
    rows, columns = value.shape
    return jnp.sum(value.reshape(rows // 8, 8, columns), axis=0)


class Table(NamedTuple):
    gat: object
    val: object
    sel: object
    hid: object
    cot: object
    outt: object
    pad: object
    spad: object
    ws: object
    wv: object
    wb: object
    wo: object
    scale: object
    normed: object
    raw: object
    draw: object
    delta: object
    run: object
    run3: object
    delta3: object
    scores_t: object
    wend: object
    runt: object
    deltat: object
    gdt: object
    growth: object
    ending: object
    x: object
    xw: object
    slope: object
    mine: object
    theirs: object
    bvec: object
    cvec: object
    scores: object
    local: object
    decay: object
    enter: object
    leave: object
    gend: object
    gout: object
    mixer: object
    across: object
    z: object
    gmix: object
    sums: object
    sums_far: object
    mixed: object
    gz: object
    gmh: object
    scaled: object
    gin: object
    gsc: object
    gdel: object
    seg: object
    gread: object
    kept: object
    given: object
    given_far: object
    gpre: object
    ga: object
    da: object
    db: object
    branch: object
    part: object
    branch_far: object
    part_far: object
    small: object
    zsmall: object
    dsmall: object
    tsmall: object
    rxa_a: object
    rya_a: object
    ryb_a: object
    rxb_a: object
    ta_a: object
    tb_a: object
    zb_a: object
    zin_a: object
    rxa_b: object
    rya_b: object
    ryb_b: object
    rxb_b: object
    ta_b: object
    tb_b: object
    zb_b: object
    zin_b: object
    sem_load: object
    sem_own: object
    sem_tail: object
    sem_swap: object
    sem_last: object
    sem_carry: object
    sem_zsmall: object
    sem_dsmall: object
    sem_gzs: object
    sem_gathers: object
    sem_gzv: object
    sem_gatherv: object
    sem_gzb: object
    sem_gatherb: object
    sem_gzo: object
    sem_gathero: object
    sem_reducea: object
    sem_rza: object
    sem_reduceb: object
    sem_rzb: object


def half(*shape):
    return pltpu.VMEM(shape, jnp.bfloat16)


def single(*shape):
    return pltpu.VMEM(shape, jnp.float32)


def dma(*shape):
    return pltpu.SemaphoreType.DMA(shape)


def plan(n, seqs, length, width, inner, pick, own, deep):
    rows = seqs * length
    total = seqs * inner
    first, second = inner + pick + LANES, 2 * inner
    return Table(
        gat=single(own, inner),
        val=single(own, inner),
        sel=single(own, pick),
        hid=half(rows, width),
        cot=half(rows, width),
        outt=single(own, inner),
        pad=single(LANES, LANES),
        spad=single(8, LANES),
        ws=half(4, n, own, pick + LANES),
        wv=half(4, n, own, inner),
        wb=half(4, n, own, inner),
        wo=half(4, n, own, inner),
        scale=single(rows, LANES),
        normed=half(rows, width),
        raw=single(seqs, length + 8, inner + pick),
        draw=single(rows, LANES),
        delta=single(rows, LANES),
        run=single(rows, LANES),
        run3=half(rows, 3 * LANES),
        delta3=half(rows, 3 * LANES),
        scores_t=single(rows, length),
        wend=single(rows, LANES),
        runt=single(seqs * 16, length),
        deltat=single(seqs * 16, length),
        gdt=single(LANES, length),
        growth=single(rows, inner),
        ending=single(rows, inner),
        x=half(rows, inner),
        xw=half(rows, inner),
        slope=single(rows, inner + pick),
        mine=half(rows, pick),
        theirs=half(rows, pick),
        bvec=half(rows, pick),
        cvec=half(rows, pick),
        scores=single(rows, length),
        local=single(total, deep),
        decay=single(total, deep),
        enter=half(total, deep),
        leave=half(total, deep),
        gend=half(total, deep),
        gout=half(total, deep),
        mixer=single(rows, inner),
        across=single(rows, inner),
        z=half(rows, inner),
        gmix=single(rows, inner),
        sums=single(rows, LANES),
        sums_far=single(rows, LANES),
        mixed=half(rows, inner),
        gz=half(rows, inner),
        gmh=half(rows, inner),
        scaled=half(rows, inner),
        gin=single(rows, inner),
        gsc=single(rows, length),
        gdel=single(rows, LANES),
        seg=single(rows, LANES),
        gread=single(rows, pick),
        kept=single(rows, pick),
        given=single(rows, pick),
        given_far=single(rows, pick),
        gpre=single(seqs, length + 8, inner + pick),
        ga=half(rows, first),
        da=half(2, 2, n, own, first),
        db=half(2, 2, n, own, second),
        branch=half(rows, width),
        part=half(rows, width),
        branch_far=half(rows, width),
        part_far=half(rows, width),
        small=single(56, LANES),
        zsmall=single(n, 56, LANES),
        dsmall=single(5, 56, LANES),
        tsmall=single(56, LANES),
        rxa_a=half(n, 2, own, first // 2),
        rya_a=half(n, own, first // 2),
        ryb_a=half(n, 2, own, first // 2),
        rxb_a=half(n, own, first // 2),
        ta_a=half(n, own, first // 2),
        tb_a=half(n, own, first // 2),
        zb_a=half(n - 1, own, first),
        zin_a=half(n - 1, own, first),
        rxa_b=half(n, 2, own, second // 2),
        rya_b=half(n, own, second // 2),
        ryb_b=half(n, 2, own, second // 2),
        rxb_b=half(n, own, second // 2),
        ta_b=half(n, own, second // 2),
        tb_b=half(n, own, second // 2),
        zb_b=half(n - 1, own, second),
        zin_b=half(n - 1, own, second),
        sem_load=dma(6),
        sem_own=dma(2),
        sem_tail=dma(4),
        sem_swap=dma(12),
        sem_last=dma(2),
        sem_carry=dma(4, PARTS),
        sem_zsmall=dma(2, n - 1),
        sem_dsmall=dma(2, 3),
        sem_gzs=dma(2, n - 1),
        sem_gathers=dma(8, n),
        sem_gzv=dma(2, n - 1),
        sem_gatherv=dma(8, n),
        sem_gzb=dma(2, n - 1),
        sem_gatherb=dma(8, n),
        sem_gzo=dma(2, n - 1),
        sem_gathero=dma(8, n),
        sem_reducea=dma(8, n),
        sem_rza=dma(2, n - 1),
        sem_reduceb=dma(8, n),
        sem_rzb=dma(2, n - 1),
    )


class Gather:
    def __init__(self, n, block, near, far, place):
        self.n, (self.d, self.s, x, y) = n, place
        self.xn, self.yn = y * 2 + (1 - x), (1 - y) * 2 + x
        self.block, self.near, self.far = block, near, far
        self.zf = [lax.rem(self.s + n - k, n) for k in range(n)]
        self.zt = [lax.rem(self.s + k, n) for k in range(n)]

    def deep(self, k):
        piece = self.block.at[self.d, self.s]
        sems = self.near.at[0, k - 1], self.near.at[1, k - 1]
        return send(piece, piece, *sems, {"seq": self.zt[k]})

    def side(self, j, axis):
        piece = self.block.at[self.d, self.zf[j]]
        sems = self.far.at[2 * axis, j], self.far.at[2 * axis + 1, j]
        return send(piece, piece, *sems, {"dp": (self.xn, self.yn)[axis]})

    def cross(self, j, axis):
        h = self.block.shape[3] // 2
        source, target = (self.yn, self.xn) if axis == 0 else (self.xn, self.yn)
        piece = self.block.at[source, self.zf[j], :, pl.ds(h if axis == 0 else 0, h)]
        sems = self.far.at[4 + 2 * axis, j], self.far.at[5 + 2 * axis, j]
        return send(piece, piece, *sems, {"dp": target})

    def begin(self):
        for k in range(1, self.n):
            self.deep(k).start()
        self.spread(0)

    def spread(self, j):
        if j:
            self.deep(j).wait_recv()
        self.side(j, 0).start()
        self.side(j, 1).start()

    def forward(self, j):
        self.side(j, 0).wait_recv()
        self.cross(j, 1).start()
        self.side(j, 1).wait_recv()
        self.cross(j, 0).start()

    def finish(self):
        for j in range(self.n):
            self.cross(j, 0).wait_recv()
            self.cross(j, 1).wait_recv()

    def close(self):
        for j in range(self.n):
            if j:
                self.deep(j).wait_send()
            for axis in range(2):
                self.side(j, axis).wait_send()
                self.cross(j, axis).wait_send()


class Reduce:
    def __init__(self, n, grad, bufs, sems, near, place):
        self.n, (self.d, self.s, self.x, self.y) = n, place
        self.grad, self.sems, self.near = grad, sems, near
        self.rxa, self.rya, self.ryb, self.rxb, self.ta, self.tb, self.zb, self.zin = bufs
        self.xn = self.y * 2 + (1 - self.x)
        self.yn = (1 - self.y) * 2 + self.x
        self.zt = [lax.rem(self.s + k, n) for k in range(n)]
        h = grad.shape[4] // 2
        self.left, self.right = pl.ds(0, h), pl.ds(h, h)
        self.order = list(range(1, n)) + [0]

    def copy(self, kind, j):
        sems = self.sems.at[2 * kind, j], self.sems.at[2 * kind + 1, j]
        z = self.zt[j]
        if kind == 0:
            source, target = self.grad.at[:, 1 - self.x, z, :, self.left], self.rxa.at[j]
        elif kind == 1:
            source, target = self.grad.at[1 - self.y, :, z, :, self.right], self.ryb.at[j]
        elif kind == 2:
            source, target = self.ta.at[j], self.rya.at[j]
        else:
            source, target = self.tb.at[j], self.rxb.at[j]
        return send(source, target, *sems, {"dp": self.xn if kind in (0, 3) else self.yn})

    def deep(self, j):
        sems = self.near.at[0, j - 1], self.near.at[1, j - 1]
        return send(self.zb.at[j - 1], self.zin.at[j - 1], *sems, {"seq": self.zt[j]})

    def launch(self, j):
        self.copy(0, j).start()
        self.copy(1, j).start()

    def begin(self):
        for j in self.order:
            self.launch(j)

    def middle(self, j):
        x, y, z = self.x, self.y, self.zt[j]
        single, half = jnp.float32, jnp.bfloat16
        self.copy(0, j).wait_recv()
        self.ta[j] = (
            self.grad[1 - y, x, z, :, self.left].astype(single)
            + self.rxa[j, 1 - y].astype(single)
        ).astype(half)
        self.copy(2, j).start()
        self.copy(1, j).wait_recv()
        self.tb[j] = (
            self.grad[y, 1 - x, z, :, self.right].astype(single)
            + self.ryb[j, 1 - x].astype(single)
        ).astype(half)
        self.copy(3, j).start()

    def join(self, j, out):
        x, y, z = self.x, self.y, self.zt[j]
        single, half = jnp.float32, jnp.bfloat16
        self.copy(2, j).wait_recv()
        low = (
            self.grad[y, x, z, :, self.left].astype(single)
            + self.rxa[j, y].astype(single)
            + self.rya[j].astype(single)
        )
        self.copy(3, j).wait_recv()
        high = (
            self.grad[y, x, z, :, self.right].astype(single)
            + self.ryb[j, x].astype(single)
            + self.rxb[j].astype(single)
        )
        if j == 0:
            out[:, self.left] = low
            out[:, self.right] = high
        else:
            self.zb[j - 1, :, self.left] = low.astype(half)
            self.zb[j - 1, :, self.right] = high.astype(half)
            self.deep(j).start()

    def finish(self, out):
        for j in range(1, self.n):
            self.deep(j).wait_recv()
            out[...] = out[...] + self.zin[j - 1].astype(jnp.float32)

    def close(self):
        for j in range(self.n):
            for kind in range(4):
                self.copy(kind, j).wait_send()
            if j:
                self.deep(j).wait_send()


def main_kernel(n, seqs, length, heads, *refs):
    inputs, refs = refs[:12], refs[12:]
    hid_h, cot_h, gat_h, val_h, sel_h, out_h = inputs[:6]
    step_ref, pre_ref, post_ref, filt_ref, kern_ref, scal_ref = inputs[6:]
    outputs, refs = refs[:5], refs[5:]
    suma_o, sumb_o, small_o, result_o, hidden_o = outputs
    r = Table(*refs)
    half, single = jnp.bfloat16, jnp.float32
    d, s = lax.axis_index("dp"), lax.axis_index("seq")
    core = lax.axis_index("tensor")
    y, x = d // 2, lax.rem(d, 2)
    place = (d, s, x, y)
    rows, width = r.hid.shape
    inner, pick = r.x.shape[1], r.mine.shape[1]
    conv = inner + pick
    pairs = inner // LANES
    deep = r.enter.shape[1]
    other = {"tensor": 1 - core}
    zt = [lax.rem(s + k, n) for k in range(n)]
    others = [{"dp": lax.rem(d + k, 4)} for k in range(1, 4)]
    after, before = {"seq": lax.rem(s + 1, n)}, {"seq": lax.rem(s + n - 1, n)}

    loads = [
        pltpu.make_async_copy(src, dst, r.sem_load.at[i])
        for i, (src, dst) in enumerate(
            [(sel_h, r.sel), (val_h, r.val), (hid_h, r.hid), (gat_h, r.gat), (out_h, r.outt), (cot_h, r.cot)]
        )
    ]
    for copy in loads:
        copy.start()
    own = r.val.shape[0]
    r.pad[...] = jnp.zeros(r.pad.shape, single)
    r.pad[:heads, :own] = step_ref[...]
    r.pad[heads : heads + 1, :own] = pre_ref[...].reshape(1, own)
    r.spad[...] = jnp.zeros(r.spad.shape, single)
    r.spad[:3, :heads] = scal_ref[...]
    ws, wv, wb, wo = r.ws, r.wv, r.wb, r.wo
    loads[0].wait()
    ws[d, s, :, :pick] = r.sel[...].astype(half)
    ws[d, s, :, pick:] = r.pad[...].T[:own].astype(half)
    loads[1].wait()
    wv[d, s] = r.val[...].astype(half)
    loads[3].wait()
    wb[d, s] = r.gat[...].astype(half)
    loads[4].wait()
    wo[d, s] = r.outt[...].astype(half)
    gs = Gather(n, ws, r.sem_gzs, r.sem_gathers, place)
    gv = Gather(n, wv, r.sem_gzv, r.sem_gatherv, place)
    gb = Gather(n, wb, r.sem_gzb, r.sem_gatherb, place)
    go = Gather(n, wo, r.sem_gzo, r.sem_gathero, place)
    greet([{"seq": zt[k]} for k in range(1, n)] + others + [other])
    gs.begin()
    gv.begin()
    loads[2].wait()
    loads[5].wait()
    tile = 32

    def scale_of(at, state):
        wide = r.hid[pl.ds(at, tile), :].astype(single)
        mean = jnp.sum(wide * wide, axis=1, keepdims=True) * (1.0 / width)
        r.scale[pl.ds(at, tile), :] = jnp.broadcast_to(
            lax.rsqrt(mean + epsilon), (tile, LANES)
        )
        return state

    each(rows // tile, tile, scale_of)

    heads_table = (iota((LANES, inner), 1) // HEADDIM == iota((LANES, inner), 0)).astype(half)
    table_heads = (iota((inner, LANES), 0) // HEADDIM == iota((inner, LANES), 1)).astype(half)
    lane = iota((1, LANES), 1)
    real = lane < heads
    bias = r.spad[0:1]
    rate = jnp.where(real, -jnp.exp(r.spad[1:2]), 0.0)
    skip = wide_mul(jnp.broadcast_to(r.spad[2:3], (8, LANES)), heads_table, 3)[0:1]
    post = post_ref[...].reshape(1, inner)

    for j in range(1, n):
        gs.spread(j)
        gs.forward(j - 1)
    gs.forward(n - 1)
    gv.spread(1)
    gb.begin()
    go.begin()
    gs.finish()

    step_t = ws[:, :, :, pick:].astype(single).reshape(width, LANES).T
    gain = step_t[heads : heads + 1, :]

    def norm_of(at, state):
        wide = r.hid[pl.ds(at, tile), :].astype(single)
        scale = r.scale[pl.ds(at, tile), 0:1]
        r.normed[pl.ds(at, tile), :] = (wide * scale * gain).astype(half)
        return state

    each(rows // tile, tile, norm_of)

    gv.spread(2)
    gv.forward(0)

    def weight_of(block, at, wide):
        return block[:, :, :, pl.ds(at, wide)].reshape(width, wide)

    tail = mul(r.normed[...], ws[...].reshape(width, pick + LANES))
    r.draw[...] = jnp.where(real, tail[:, pick:], 0.0)
    for q in range(seqs):
        r.raw[q, 8:, inner:] = (
            tail[q * length : (q + 1) * length, :pick].astype(half).astype(single)
        )

    gv.spread(3)
    gv.forward(1)

    low = (iota((length, length), 0) >= iota((length, length), 1)).astype(half)
    high = (iota((length, length), 0) <= iota((length, length), 1)).astype(half)
    cdecays = []
    for q in range(seqs):
        span = pl.ds(q * length, length)
        value = r.draw[span, :] + bias
        delta = jnp.maximum(value, 0.0) + jnp.log1p(jnp.exp(-jnp.abs(value)))
        delta = jnp.where(real, delta, 0.0)
        run = table_mul(low, delta * rate, 3)
        last = run[length - 1 : length, :]
        r.delta[span, :] = delta
        r.run[span, :] = run
        for target, whole in ((r.run3, run), (r.delta3, delta)):
            for i, piece in enumerate(split(whole, 3)):
                target[span, i * LANES : (i + 1) * LANES] = piece
        wend = jnp.exp(last - run) * delta
        r.wend[span, :] = wend
        r.runt[q * 16 : (q + 1) * 16, :] = run.T[:16]
        r.deltat[q * 16 : (q + 1) * 16, :] = delta.T[:16]
        cdecay = jnp.exp(last)
        cdecays.append(cdecay)
        pickrow = iota((inner, LANES), 0) // HEADDIM == iota((inner, LANES), 1)
        column = jnp.sum(jnp.where(pickrow, cdecay, 0.0), axis=1, keepdims=True)
        r.decay[q * inner : (q + 1) * inner, :] = jnp.broadcast_to(column, (inner, deep))
        r.growth[span, :] = wide_mul(jnp.exp(run), heads_table, 2)
        r.ending[span, :] = wide_mul(wend, heads_table, 2)

    gv.forward(2)
    gb.spread(1)
    gv.forward(3)
    gb.spread(2)
    gv.finish()

    def raw_of(at, state):
        value = mul(r.normed[...], weight_of(wv, at, 256)).astype(half).astype(single)
        for q in range(seqs):
            r.raw[q, 8:, pl.ds(at, 256)] = value[q * length : (q + 1) * length]
        return state

    each(inner // 256, 256, raw_of)

    tails = send(
        r.raw.at[:, pl.ds(length, 8)], r.raw.at[:, pl.ds(0, 8)],
        r.sem_tail.at[0], r.sem_tail.at[1], after,
    )

    @pl.when(s == 0)
    def _():
        r.raw[:, 0:8] = jnp.zeros((seqs, 8, conv), single)

    @pl.when(s != n - 1)
    def _():
        tails.start()

    gb.spread(3)
    gb.forward(0)
    gb.forward(1)
    go.spread(1)

    @pl.when(s != 0)
    def _():
        tails.wait_recv()

    def conv_of(first, wide):
        taps = [(kern_ref if first else filt_ref)[k : k + 1, :] for k in range(5)]
        for q in range(seqs):

            def one(at, state):
                padded = r.raw[q, pl.ds(at, tile + 8), first : first + wide]
                total = taps[4] + taps[3] * padded[8:]
                for k in range(3):
                    total = total + taps[k] * pltpu.roll(padded, 3 - k, 0)[8:]
                sigmoid = jax.nn.sigmoid(total)
                span = pl.ds(pl.multiple_of(q * length + at, tile), tile)
                act = (total * sigmoid).astype(half)
                if first:
                    r.mine[span, :] = act
                else:
                    r.x[span, :] = act
                    r.xw[span, :] = (act.astype(single) * r.ending[span, :]).astype(half)
                r.slope[span, first : first + wide] = sigmoid * (
                    1.0 + total * (1.0 - sigmoid)
                )
                return state

            each(length // tile, tile, one)

    conv_of(inner, pick)
    swaps = r.sem_swap
    trade = send(r.mine, r.theirs, swaps.at[0], swaps.at[1], other)
    trade.start()
    conv_of(0, inner)
    go.spread(2)
    gb.forward(2)
    trade.wait_recv()
    mine, theirs = r.mine[...], r.theirs[...]
    r.bvec[...] = jnp.where(core == 0, mine, theirs)
    r.cvec[...] = jnp.where(core == 0, theirs, mine)
    total = seqs * inner
    size = total // PARTS
    for q in range(seqs):
        span = pl.ds(q * length, length)
        r.local[q * inner : (q + 1) * inner, :] = mul_tn(r.xw[span, :], r.bvec[span, :])
        r.scores[span, :] = mul_nt(r.cvec[span, :], r.bvec[span, :])
        r.scores_t[span, :] = mul_nt(r.bvec[span, :], r.cvec[span, :])

    def carry_step(part, first, last, came, went, sem, target):
        span = pl.ds(pl.multiple_of(part * size, size), size)
        copy = send(
            went.at[span], came.at[span],
            r.sem_carry.at[sem, part], r.sem_carry.at[sem + 1, part], target,
        )

        @pl.when(s == first)
        def _():
            came[span, :] = jnp.zeros((size, deep), half)
            went[span, :] = r.local[span, :].astype(half)

        @pl.when(s != first)
        def _():
            copy.wait_recv()
            went[span, :] = (
                r.decay[span, :] * came[span, :].astype(single) + r.local[span, :]
            ).astype(half)

        @pl.when(s != last)
        def _():
            copy.start()

    def carry_close(last, came, went, sem, target):
        @pl.when(s != last)
        def _():
            for part in range(PARTS):
                span = pl.ds(part * size, size)
                send(
                    went.at[span], came.at[span],
                    r.sem_carry.at[sem, part], r.sem_carry.at[sem + 1, part], target,
                ).wait_send()

    causal = iota((length, length), 0) >= iota((length, length), 1)
    side = iota((1, LANES), 1) // HEADDIM

    def decays_of(q, h):
        span = pl.ds(pl.multiple_of(q * length, length), length)
        choose = ((iota((3 * LANES, LANES), 0) & (LANES - 1)) == h).astype(half)
        column = mul(r.run3[span, :], choose)
        row = r.runt[pl.ds(q * 16 + h, 1), :]
        gap = jnp.concatenate([column] * (length // LANES), axis=1) - row
        return jnp.exp(jnp.where(causal, gap, -1e30))

    def within_of(index, state):
        q, p = index // pairs, lax.rem(index, pairs)
        span = pl.ds(pl.multiple_of(q * length, length), length)
        lanes = pl.ds(pl.multiple_of(p * LANES, LANES), LANES)
        value = r.x[span, lanes]
        scores = r.scores[span, :]
        out = None
        for a in range(2):
            h = 2 * p + a
            step = r.deltat[pl.ds(q * 16 + h, 1), :]
            mixing = (scores * decays_of(q, h) * step).astype(half)
            term = mul(mixing, jnp.where(side == a, value, jnp.zeros_like(value)))
            out = term if out is None else out + term
        r.mixer[span, lanes] = out
        @pl.when(s != 0)
        def _():
            forth(index - lag)

        for at, pump in enumerate(pumps):
            pl.when(index == 3 * at + 1)(pump)
        return state

    def pump_b():
        gb.forward(3)
        go.spread(3)
        go.forward(0)

    def pump_c():
        go.forward(1)

    def pump_d():
        go.forward(2)

    pumps = [pump_b, pump_c, pump_d]
    lag = jnp.where(s == n - 1, PARTS, jnp.minimum(3 * s - 1, PARTS))

    def forth(part):
        @pl.when(part >= 0)
        def _():
            carry_step(part, 0, n - 1, r.enter, r.leave, 0, after)

    def forth_one(part, state):
        forth(part)
        return state

    @pl.when(s == 0)
    def _():
        lax.fori_loop(0, PARTS, forth_one, 0)

    lax.fori_loop(0, PARTS, within_of, 0)
    middle = jnp.where((s == n - 1) | (s == 0), 0, lag)
    lax.fori_loop(PARTS - middle, PARTS, forth_one, 0)
    go.forward(n - 1)
    gb.finish()

    def gate_of(at, state):
        r.z[:, pl.ds(at, 256)] = mul(r.normed[...], weight_of(wb, at, 256)).astype(half)
        return state

    each(inner // 256, 256, gate_of)
    go.finish()

    def down_of(at, state):
        r.gmix[:, pl.ds(at, 256)] = mul(r.cot[...], weight_of(wo, at, 256))
        return state

    each(inner // 256, 256, down_of)
    lax.fori_loop(jnp.where(s == n - 1, 0, PARTS), PARTS, forth_one, 0)

    trades = []
    for q in range(seqs):
        span = pl.ds(q * length, length)
        r.across[span, :] = mul_nt(
            r.cvec[span, :], r.enter[q * inner : (q + 1) * inner, :]
        )

        def mixer_of(at, state):
            span = pl.ds(pl.multiple_of(q * length + at, tile), tile)
            mixer = (
                r.mixer[span, :]
                + r.growth[span, :] * r.across[span, :]
                + skip * r.x[span, :].astype(single)
            )
            r.mixer[span, :] = mixer
            z = r.z[span, :].astype(single)
            gated = mixer * (z * jax.nn.sigmoid(z))
            squares = jnp.sum(gated * gated, axis=1, keepdims=True)
            dots = jnp.sum(r.gmix[span, :] * post * gated, axis=1, keepdims=True)
            r.sums[span, :] = jnp.where(lane == 0, squares, jnp.where(lane == 1, dots, 0.0))
            return state

        each(length // tile, tile, mixer_of)
        copy = send(
            r.sums.at[span], r.sums_far.at[span],
            swaps.at[2 + 2 * q], swaps.at[3 + 2 * q], other,
        )
        copy.start()
        trades.append(copy)

    full = 2 * inner

    def back_of(q):
        def one(at, state):
            span = pl.ds(pl.multiple_of(q * length + at, tile), tile)
            both = r.sums[span, :] + r.sums_far[span, :]
            scale = lax.rsqrt(both[:, 0:1] * (1.0 / full) + epsilon)
            dots = both[:, 1:2] * (1.0 / full)
            mixer, z = r.mixer[span, :], r.z[span, :].astype(single)
            sigmoid = jax.nn.sigmoid(z)
            act, slope = z * sigmoid, sigmoid * (1.0 + z * (1.0 - sigmoid))
            gated = mixer * act
            gmixed = r.gmix[span, :]
            r.mixed[span, :] = (gated * scale * post).astype(half)
            ggated = scale * (gmixed * post) - gated * (scale * scale * scale * dots)
            gmixer = ggated * act
            r.gz[span, :] = (ggated * mixer * slope).astype(half)
            r.gmh[span, :] = gmixer.astype(half)
            scaled = gmixer * r.growth[span, :]
            r.scaled[span, :] = scaled.astype(half)
            r.gmix[span, :] = gmixer
            r.across[span, :] = scaled * r.across[span, :]
            return (
                state[0] + fold(gmixed * gated * scale),
                state[1] + fold(gmixer * r.x[span, :].astype(single)),
            )

        return one

    state = (jnp.zeros((8, inner), single), jnp.zeros((8, inner), single))
    push = []
    for q in range(seqs):
        trades[q].wait_recv()
        state = each(length // tile, tile, back_of(q), state)
        span = pl.ds(q * length, length)
        r.local[q * inner : (q + 1) * inner, :] = mul_tn(r.scaled[span, :], r.cvec[span, :])

    def back(part):
        @pl.when((part >= 0) & (part < PARTS))
        def _():
            carry_step(part, n - 1, 0, r.gend, r.gout, 2, before)

    def back_one(part, state):
        back(part)
        return state

    @pl.when(s == n - 1)
    def _():
        lax.fori_loop(0, PARTS, back_one, 0)

    r.small[...] = jnp.zeros(r.small.shape, single)
    post_at = 5 * (conv // LANES)
    gain_at = post_at + inner // LANES
    head_at = gain_at + width // LANES

    def put(at, row):
        for c in range(row.shape[1] // LANES):
            r.small[at + c : at + c + 1, :] = row[:, c * LANES : (c + 1) * LANES]

    put(post_at, jnp.sum(state[0], axis=0, keepdims=True))
    r.small[head_at + 2 : head_at + 3, :] = jnp.sum(wide_mul(state[1], table_heads, 3), axis=0, keepdims=True)

    ra = Reduce(
        n, r.da, (r.rxa_a, r.rya_a, r.ryb_a, r.rxb_a, r.ta_a, r.tb_a, r.zb_a, r.zin_a),
        r.sem_reducea, r.sem_rza, place,
    )
    rb = Reduce(
        n, r.db, (r.rxa_b, r.rya_b, r.ryb_b, r.rxb_b, r.ta_b, r.tb_b, r.zb_b, r.zin_b),
        r.sem_reduceb, r.sem_rzb, place,
    )

    span_y = width // 2

    def grad_b(index, state):
        lanes = pl.ds(pl.multiple_of(index * span_y, span_y), span_y)
        own = r.db.shape[3]
        r.db[index, :, :, :, pl.ds(0, inner)] = (
            mul_tn(r.normed[:, lanes], r.gz[...]).astype(half).reshape(2, n, own, inner)
        )
        r.db[index, :, :, :, pl.ds(inner, inner)] = (
            mul_tn(r.cot[:, lanes], r.mixed[...]).astype(half).reshape(2, n, own, inner)
        )
        return state

    lax.fori_loop(0, 2, grad_b, 0)

    r.gsc[...] = jnp.zeros(r.gsc.shape, single)
    r.gdel[...] = jnp.zeros(r.gdel.shape, single)
    r.gdt[...] = jnp.zeros(r.gdt.shape, single)

    later = iota((length, length), 0) <= iota((length, length), 1)

    def intra_of(index, state):
        q, p = index // pairs, lax.rem(index, pairs)
        span = pl.ds(pl.multiple_of(q * length, length), length)
        lanes = pl.ds(pl.multiple_of(p * LANES, LANES), LANES)
        value, upper = r.x[span, lanes], r.gmh[span, lanes]
        scores = r.scores_t[span, :]
        out = None
        for a in range(2):
            h = 2 * p + a
            choose = ((iota((3 * LANES, LANES), 0) & (LANES - 1)) == h).astype(half)
            column = mul(r.run3[span, :], choose)
            step = mul(r.delta3[span, :], choose)
            step = jnp.concatenate([step] * (length // LANES), axis=1)
            row = r.runt[pl.ds(q * 16 + h, 1), :]
            gap = row - jnp.concatenate([column] * (length // LANES), axis=1)
            decays = jnp.exp(jnp.where(later, gap, -1e30))
            masked = jnp.where(side == a, upper, jnp.zeros_like(upper))
            mixing = (scores * decays * step).astype(half)
            term = mul(mixing, masked)
            out = term if out is None else out + term
            spread = mul_nt(value, masked) * decays
            kernel = spread * scores
            fall = jnp.sum(kernel, axis=1, keepdims=True)
            r.gdel[span, :] += jnp.where(lane == h, fall, 0.0)
            r.gsc[span, :] += spread * step
            r.gdt[pl.ds(q * 16 + h, 1), :] = jnp.sum(kernel * step, axis=0, keepdims=True)
        r.gin[span, lanes] = out
        @pl.when(s != n - 1)
        def _():
            back(2 * (index - delay))
            back(2 * (index - delay) + 1)

        for at, j in enumerate(rb.order):

            @pl.when(index == jnp.where(mid, 2 * at + 2, at))
            def _():
                rb.launch(j)

        return state

    delay = 2 * (n - 2 - s)
    mid = (s != 0) & (s != n - 1)
    lax.fori_loop(0, PARTS, intra_of, 0)

    def gate_part(index, state):
        lanes = pl.ds(pl.multiple_of(index * span_y, span_y), span_y)
        gate = wb[pl.ds(2 * index, 2)].reshape(span_y, inner)
        r.mixer[:, lanes] = mul_nt(r.gz[...], gate)
        return state

    def branch_of(index, state):
        lanes = pl.ds(pl.multiple_of(index * span_y, span_y), span_y)
        weight = wo[pl.ds(2 * index, 2)].reshape(span_y, inner)
        r.branch[:, lanes] = mul_nt(r.mixed[...], weight).astype(half)
        return state

    lax.fori_loop(0, 2, branch_of, 0)
    far = [send(r.branch, r.branch_far, swaps.at[6], swaps.at[7], other)]
    far[0].start()

    lax.fori_loop(0, 2, gate_part, 0)
    rb.middle(1)
    rb.middle(2)

    gdt = r.gdt[...].T
    bias_row, log_row = jnp.zeros((1, LANES), single), jnp.zeros((1, LANES), single)
    seg = [wide_mul(r.across[pl.ds(q * length, length), :], table_heads, 2) for q in range(seqs)]
    for q in range(seqs):
        span = pl.ds(q * length, length)
        states = pl.ds(q * inner, inner)
        r.across[span, :] = mul_nt(r.bvec[span, :], r.gend[states, :])
        r.gread[span, :] = mul(r.scaled[span, :], r.enter[states, :])
        gsc = r.gsc[span, :].astype(half)
        gread = r.gread[span, :] + mul_tn(gsc, r.bvec[span, :])
        gwrite = mul(gsc, r.cvec[span, :]) + mul(r.xw[span, :], r.gend[states, :])
        r.kept[span, :] = jnp.where(core == 0, gwrite, gread)
        r.given[span, :] = jnp.where(core == 0, gread, gwrite)
    trade2 = send(r.given, r.given_far, swaps.at[8], swaps.at[9], other)
    trade2.start()
    rb.middle(3)
    rb.middle(0)

    def inner_of(at, state):
        span = pl.ds(at, tile)
        back = r.across[span, :]
        total = (
            r.gin[span, :] + skip * r.gmix[span, :] + back * r.ending[span, :]
        )
        r.gin[span, :] = total
        r.across[span, :] = back * r.x[span, :].astype(single)
        return state

    each(rows // tile, tile, inner_of)

    for q in range(seqs):
        span = pl.ds(q * length, length)
        states = pl.ds(q * inner, inner)
        weight = wide_mul(r.across[span, :], table_heads, 2)
        product = r.gend[states, :].astype(single) * r.enter[states, :].astype(single)
        ones = jnp.ones((8, deep), half)
        across = sum(mul_nt(ones, piece) for piece in split(product, 2))
        end_row = wide_mul(across, table_heads, 3)[0:1] * cdecays[q]
        delta, run, wend = r.delta[span, :], r.run[span, :], r.wend[span, :]
        grun = jnp.where(
            lane < heads, pltpu.roll(gdt, LANES - 16 * q, 1) if q else gdt, 0.0
        )
        gdelta = r.gdel[span, :]
        grun = grun - delta * gdelta + seg[q]
        last = run[length - 1 : length, :]
        gdelta = gdelta + weight * jnp.exp(last - run)
        spread = weight * wend
        end_row = end_row + jnp.sum(spread, axis=0, keepdims=True)
        grun = grun - spread + jnp.where(iota((length, 1), 0) == length - 1, end_row, 0.0)
        glog = table_mul(high, grun, 3)
        gdelta = gdelta + glog * rate
        log_row = log_row + jnp.sum(glog * delta, axis=0, keepdims=True) * rate
        gdraw = jnp.where(real, gdelta * jax.nn.sigmoid(r.draw[span, :] + bias), 0.0)
        bias_row = bias_row + jnp.sum(gdraw, axis=0, keepdims=True)
        r.ga[span, conv:] = gdraw.astype(half)
    r.small[head_at : head_at + 1, :] = bias_row
    r.small[head_at + 1 : head_at + 2, :] = log_row

    trade2.wait_recv()
    for q in range(seqs):

        def pre_of(at, state):
            span = pl.ds(pl.multiple_of(q * length + at, tile), tile)
            r.gpre[q, pl.ds(at, tile), :inner] = r.gin[span, :] * r.slope[span, :inner]
            r.gpre[q, pl.ds(at, tile), inner:] = (
                r.kept[span, :] + r.given_far[span, :]
            ) * r.slope[span, inner:]
            return state

        each(length // tile, tile, pre_of)

    tails2 = send(
        r.gpre.at[:, pl.ds(0, 8)], r.gpre.at[:, pl.ds(length, 8)],
        r.sem_tail.at[2], r.sem_tail.at[3], before,
    )

    @pl.when(s == n - 1)
    def _():
        r.gpre[:, length:] = jnp.zeros((seqs, 8, conv), single)

    @pl.when(s != 0)
    def _():
        tails2.start()

    @pl.when(s != n - 1)
    def _():
        tails2.wait_recv()


    taps = [
        jnp.concatenate([filt_ref[k : k + 1, :], kern_ref[k : k + 1, :]], axis=1)
        for k in range(4)
    ]
    for q in range(seqs):

        def raw_grad(at, state):
            padded = r.gpre[q, pl.ds(at, tile + 8), :]
            total = taps[3] * padded[:tile]
            for k in range(3):
                total = total + taps[k] * pltpu.roll(padded, tile + 8 - (3 - k), 0)[:tile]
            span = pl.ds(pl.multiple_of(q * length + at, tile), tile)
            r.ga[span, :conv] = total.astype(half)
            return state

        each(length // tile, tile, raw_grad)

    def grad_a(index, state):
        lanes = pl.ds(pl.multiple_of(index * span_y, span_y), span_y)
        own, wide = r.da.shape[3:]
        r.da[index] = (
            mul_tn(r.normed[:, lanes], r.ga[...]).astype(half).reshape(2, n, own, wide)
        )
        return state

    lax.fori_loop(0, 2, grad_a, 0)
    ra.begin()

    def part_of(index, state):
        lanes = pl.ds(pl.multiple_of(index * span_y, span_y), span_y)
        block = pl.ds(2 * index, 2)
        value = wv[block].reshape(span_y, inner)
        select = ws[block].reshape(span_y, pick + LANES)
        r.part[:, lanes] = (
            r.mixer[:, lanes]
            + mul_nt(r.ga[:, :inner], value)
            + mul_nt(r.ga[:, inner:], select)
        ).astype(half)
        return state

    lax.fori_loop(0, 2, part_of, 0)
    far.append(send(r.part, r.part_far, swaps.at[10], swaps.at[11], other))
    far[1].start()

    def gain_of(at, state):
        span = pl.ds(at, tile)
        term = (
            r.part[span, :].astype(single)
            * r.hid[span, :].astype(single)
            * r.scale[span, 0:1]
        )
        return state + fold(term)

    gain_sum = each(rows // tile, tile, gain_of, jnp.zeros((8, width), single))
    put(gain_at, jnp.sum(gain_sum, axis=0, keepdims=True))

    taps_sum = tuple(jnp.zeros((8, conv), single) for _ in range(5))
    for q in range(seqs):

        def taps_of(at, state):
            pre = r.gpre[q, pl.ds(at, tile), :]
            padded = r.raw[q, pl.ds(at, tile + 8), :]
            terms = [pre * pltpu.roll(padded, 3 - k, 0)[8:] for k in range(3)]
            terms += [pre * padded[8:], pre]
            return tuple(total + fold(term) for total, term in zip(state, terms))

        taps_sum = each(length // tile, tile, taps_of, taps_sum)
    for k in range(5):
        put(k * (conv // LANES), jnp.sum(taps_sum[k], axis=0, keepdims=True))

    smalls = []
    for k in range(1, n):
        copy = send(
            r.small, r.zsmall.at[s],
            r.sem_zsmall.at[0, k - 1], r.sem_zsmall.at[1, k - 1], {"seq": zt[k]},
        )
        copy.start()
        smalls.append(copy)
    r.zsmall[s] = r.small[...]
    for j in rb.order:
        rb.join(j, sumb_o)
    far[0].wait_recv()
    far[1].wait_recv()

    def result_of(at, state):
        span = pl.ds(at, tile)
        wide = r.hid[span, :].astype(single)
        scale = r.scale[span, 0:1]
        r.gmix[span, :] = (
            wide + r.branch[span, :].astype(single) + r.branch_far[span, :].astype(single)
        )
        hat = (r.part[span, :].astype(single) + r.part_far[span, :].astype(single)) * gain
        dots = jnp.sum(hat * wide, axis=1, keepdims=True) * (1.0 / width)
        r.gin[span, :] = (
            r.cot[span, :].astype(single)
            + scale * hat
            - wide * (scale * scale * scale * dots)
        )
        return state

    each(rows // tile, tile, result_of)
    keep = [
        pltpu.make_async_copy(r.gmix, result_o, r.sem_own.at[0]),
        pltpu.make_async_copy(r.gin, hidden_o, r.sem_own.at[1]),
    ]
    for copy in keep:
        copy.start()
    for place_, j in enumerate(ra.order):
        ra.middle(j)
        if place_:
            ra.join(ra.order[place_ - 1], suma_o)
    ra.join(0, suma_o)
    for copy in smalls:
        copy.wait_recv()
    total_small = r.zsmall[0]
    for k in range(1, n):
        total_small = total_small + r.zsmall[k]
    r.dsmall[d] = total_small
    widely = []
    for k in range(3):
        copy = send(
            r.dsmall.at[d], r.dsmall.at[d],
            r.sem_dsmall.at[0, k], r.sem_dsmall.at[1, k], others[k],
        )
        copy.start()
        widely.append(copy)
    for copy in widely:
        copy.wait_recv()
    total_small = r.dsmall[0] + r.dsmall[1] + r.dsmall[2] + r.dsmall[3]
    r.dsmall[4] = total_small
    last_trade = send(r.dsmall.at[4], r.tsmall, r.sem_last.at[0], r.sem_last.at[1], other)
    last_trade.start()
    rb.finish(sumb_o)
    ra.finish(suma_o)
    last_trade.wait()

    def take(value, at, count):
        return jnp.concatenate([value[at + c : at + c + 1] for c in range(count)], axis=1)

    small_o[...] = jnp.zeros(small_o.shape, single)
    for k in range(5):
        at = k * (conv // LANES)
        small_o[k : k + 1, :] = take(total_small, at, conv // LANES)
    small_o[5:6, :inner] = take(total_small, post_at, inner // LANES)
    small_o[8:11, :LANES] = total_small[head_at : head_at + 3]
    both = total_small + r.tsmall[...]
    gains = jnp.broadcast_to(take(both, gain_at, width // LANES), (8, width))
    turn = lax.rem(width - (d * n + s) * own, width)
    small_o[7:8, :width] = pltpu.roll(gains, turn, 1)[0:1]

    for group in (gs, gv, gb, go):
        group.close()
    ra.close()
    rb.close()
    carry_close(n - 1, r.enter, r.leave, 0, after)
    carry_close(0, r.gend, r.gout, 2, before)

    @pl.when(s != n - 1)
    def _():
        tails.wait_send()

    @pl.when(s != 0)
    def _():
        tails2.wait_send()

    for copy in [trade, trade2] + trades:
        copy.wait_send()
    for copy in keep:
        copy.wait()
    for copy in far:
        copy.wait_send()
    for copy in smalls + widely:
        copy.wait_send()


def finish_kernel(heads, *refs):
    single = jnp.float32
    suma, sumb, small = refs[:3]
    tokens, weights, moments = refs[3:5], refs[5:15], refs[15:25]
    outputs, scratch = refs[25:57], refs[57:]
    weight_v, moment_v, grad_v, next_v, state_v = (
        scratch[:5], scratch[5:10], scratch[10:15], scratch[15:20], scratch[20:25]
    )
    sems = scratch[25:28]
    result_o, grad_o, next_o, state_o = (
        outputs[:2], outputs[2:12], outputs[12:22], outputs[22:32],
    )
    inner, pick = weight_v[0].shape[1], weight_v[2].shape[1]
    own = weight_v[0].shape[0]
    gone = []

    def leave(src, dst, sem):
        copy = pltpu.make_async_copy(src, dst, sem)
        copy.start()
        gone.append(copy)

    arrive = [
        [
            pltpu.make_async_copy(weights[i], weight_v[i], sems[0].at[0, i]),
            pltpu.make_async_copy(moments[i], moment_v[i], sems[0].at[1, i]),
        ]
        for i in range(5)
    ]
    for group in arrive:
        for copy in group:
            copy.start()
    token_v = scratch[28:]
    size = tokens[0].shape[0] // 2
    through = []
    for i in range(2):
        for k in range(2):
            span = pl.ds(k * size, size)
            copy = pltpu.make_async_copy(
                tokens[i].at[span], token_v[i].at[span], sems[1].at[0, 2 * i + k]
            )
            copy.start()
            through.append((copy, token_v[i].at[span], result_o[i].at[span]))

    def pass_on(at):
        copy, src, dst = through[at]
        copy.wait()
        leave(src, dst, sems[1].at[1, at])

    tall = jnp.concatenate([suma[:, inner + pick :], jnp.zeros((LANES - own, LANES), single)], axis=0).T
    grads = (sumb[:, :inner], suma[:, :inner], suma[:, inner : inner + pick], tall[:heads, :own], sumb[:, inner:])
    for i, grad in enumerate(grads):
        grad_v[i][...] = grad
        leave(grad_v[i], grad_o[i], sems[2].at[0, i])
    smalls = (
        small[7:8, :own],
        small[5:6, :inner],
        small[:5, :inner],
        small[:5, inner:],
        small[8:11, :heads],
    )
    for i, grad in enumerate(smalls):
        k = 5 + i
        flat = i < 2
        first_at = slice(0, 1) if flat else (slice(None), 0)
        second_at = slice(1, 2) if flat else (slice(None), 1)
        param = weights[k][...].reshape(grad.shape)
        fresh, first, second = step_of(param, moments[k][first_at], moments[k][second_at], grad)
        grad_o[k][...] = grad.reshape(grad_o[k].shape)
        next_o[k][...] = fresh.reshape(next_o[k].shape)
        state_o[k][first_at] = first
        state_o[k][second_at] = second
    pass_on(0)
    pass_on(1)
    for i, grad in enumerate(grads):
        for copy in arrive[i]:
            copy.wait()
        apart = i == 3
        first_at = (slice(None), 0) if apart else 0
        second_at = (slice(None), 1) if apart else 1
        fresh, first, second = step_of(
            weight_v[i][...], moment_v[i][first_at], moment_v[i][second_at], grad
        )
        next_v[i][...] = fresh
        state_v[i][first_at] = first
        state_v[i][second_at] = second
        leave(next_v[i], next_o[i], sems[2].at[1, i])
        leave(state_v[i], state_o[i], sems[2].at[2, i])
    pass_on(2)
    pass_on(3)
    for copy in gone:
        copy.wait()


def step_of(param, first, second, grad):
    first = first_decay * first + (1.0 - first_decay) * grad
    second = second_decay * second + (1.0 - second_decay) * grad * grad
    first_hat = first / (1.0 - first_decay**STEP)
    second_hat = second / (1.0 - second_decay**STEP)
    fresh = param - learn_rate * (
        first_hat / (jnp.sqrt(second_hat) + adam_epsilon) + weight_decay * param
    )
    return fresh, first, second


def fast(
    hidden, cotangent, gating, values, selector, timestep, output, prenorm, postnorm,
    filters, kernels, scalars, gating_adam, values_adam, selector_adam, timestep_adam,
    output_adam, prenorm_adam, postnorm_adam, filters_adam, kernels_adam, scalars_adam,
):
    half, single = jnp.bfloat16, jnp.float32
    n = lax.axis_size("seq")
    seqs, length, width = hidden.shape
    rows = seqs * length
    own, inner = gating.shape
    pick, heads = selector.shape[1], timestep.shape[1]
    conv = inner + pick
    scratch = plan(n, seqs, length, width, inner, pick, own, STATE)
    hid, cot = hidden.reshape(rows, width), cotangent.reshape(rows, width)
    shape = jax.ShapeDtypeStruct
    token = shape((rows, width), single)
    suma, sumb, small, *tokens = pl.pallas_call(
        functools.partial(main_kernel, n, seqs, length, heads),
        out_shape=(
            shape((own, conv + LANES), single),
            shape((own, 2 * inner), single),
            shape((16, conv), single),
            token,
            token,
        ),
        in_specs=[ANY] * 6 + [VMEM] * 6,
        out_specs=(VMEM,) * 3 + (ANY,) * 2,
        scratch_shapes=list(scratch),
        compiler_params=pltpu.CompilerParams(
            collective_id=0, has_side_effects=True, vmem_limit_bytes=VMEM_BYTES
        ),
    )(
        hid, cot, gating, values, selector, output.T, timestep.T, prenorm,
        postnorm, filters, kernels, scalars,
    )

    weights = (
        gating, values, selector, timestep.T, output.T, prenorm, postnorm,
        filters, kernels, scalars,
    )
    swapped = [jnp.transpose(m, (1, 0, 2)) for m in (filters_adam, kernels_adam, scalars_adam)]
    moments = (
        gating_adam, values_adam, selector_adam, jnp.transpose(timestep_adam, (2, 0, 1)),
        jnp.transpose(output_adam, (0, 2, 1)), prenorm_adam, postnorm_adam, *swapped,
    )
    out_shape = [shape((rows, width), single)] * 2
    out_shape += [shape(w.shape, single) for w in weights] * 2
    out_shape += [shape(m.shape, single) for m in moments]
    dma_shape = pltpu.SemaphoreType.DMA
    kinds = [ANY] * 5 + [VMEM] * 5
    done = pl.pallas_call(
        functools.partial(finish_kernel, heads),
        out_shape=out_shape,
        in_specs=[VMEM] * 3 + [ANY] * 2 + kinds * 2,
        out_specs=[ANY] * 2 + kinds * 3,
        scratch_shapes=[pltpu.VMEM(w.shape, single) for w in weights[:5]]
        + [pltpu.VMEM(m.shape, single) for m in moments[:5]]
        + [pltpu.VMEM(w.shape, single) for w in weights[:5]] * 2
        + [pltpu.VMEM(m.shape, single) for m in moments[:5]]
        + [dma_shape((2, 5)), dma_shape((2, 4)), dma_shape((3, 5))]
        + [pltpu.VMEM((rows, width), single)] * 2,
        compiler_params=pltpu.CompilerParams(vmem_limit_bytes=VMEM_BYTES),
    )(suma, sumb, small, *tokens, *weights, *moments)
    result, hidden_grad = (value.reshape(hidden.shape) for value in done[:2])

    def whole(group):
        big, tiny = group[:3], group[7:]
        return (*big, group[3].T, group[4].T, group[5], group[6], *tiny)

    states = done[22:]
    return (
        (result, hidden_grad)
        + whole(done[2:12])
        + whole(done[12:22])
        + (
            *states[:3],
            jnp.transpose(states[3], (1, 2, 0)),
            jnp.transpose(states[4], (0, 2, 1)),
            *states[5:7],
            *(jnp.transpose(m, (1, 0, 2)) for m in states[7:]),
        )
    )


def shards(*arrays):
    if (lax.axis_size("dp"), lax.axis_size("seq")) == (4, 4):
        return fast(*arrays)
    return general(*arrays)


def solution(mesh):
    placed = (
        P("dp", "seq", None),
        P("dp", "seq", None),
        P(("dp", "seq"), "tensor"),
        P(("dp", "seq"), "tensor"),
        P(("dp", "seq"), "tensor"),
        P(("dp", "seq"), "tensor"),
        P("tensor", ("dp", "seq")),
        P(("dp", "seq")),
        P("tensor"),
        P(None, "tensor"),
        P(None, "tensor"),
        P(None, "tensor"),
        P(None, ("dp", "seq"), "tensor"),
        P(None, ("dp", "seq"), "tensor"),
        P(None, ("dp", "seq"), "tensor"),
        P(None, ("dp", "seq"), "tensor"),
        P(None, "tensor", ("dp", "seq")),
        P(None, ("dp", "seq")),
        P(None, "tensor"),
        P(None, None, "tensor"),
        P(None, None, "tensor"),
        P(None, None, "tensor"),
    )
    return jax.shard_map(
        shards,
        mesh=mesh,
        in_specs=placed,
        out_specs=(
            P("dp", "seq", None),
            P("dp", "seq", None),
            P(("dp", "seq"), "tensor"),
            P(("dp", "seq"), "tensor"),
            P(("dp", "seq"), "tensor"),
            P(("dp", "seq"), "tensor"),
            P("tensor", ("dp", "seq")),
            P(("dp", "seq")),
            P("tensor"),
            P(None, "tensor"),
            P(None, "tensor"),
            P(None, "tensor"),
            P(("dp", "seq"), "tensor"),
            P(("dp", "seq"), "tensor"),
            P(("dp", "seq"), "tensor"),
            P(("dp", "seq"), "tensor"),
            P("tensor", ("dp", "seq")),
            P(("dp", "seq")),
            P("tensor"),
            P(None, "tensor"),
            P(None, "tensor"),
            P(None, "tensor"),
            P(None, ("dp", "seq"), "tensor"),
            P(None, ("dp", "seq"), "tensor"),
            P(None, ("dp", "seq"), "tensor"),
            P(None, ("dp", "seq"), "tensor"),
            P(None, "tensor", ("dp", "seq")),
            P(None, ("dp", "seq")),
            P(None, "tensor"),
            P(None, None, "tensor"),
            P(None, None, "tensor"),
            P(None, None, "tensor"),
        ),
        check_vma=False,
    )
```
